32 devices in a mesh: space: 4 (over x, core), freq: 8 (over z, y).
Axes of the slice: x: 2, y: 2, z: 4, core: 2. Of those that a mesh axis runs over, the one named last changes fastest.
Arguments:
- spectrum: float32 [32, 36, 128, 256], P('freq', None, 'space'), may hold values from 0.05 to 2
- land_sea: int32 [128, 256], P('space'), may hold values 0 or 1
- courant: float32 [32], P('freq'), may hold values from 0.2 to 0.65
- refract: float32 [32], P('freq'), may hold values from 0.2 to 0.9
- depth_dx: float32 [128, 256], P('space'), may hold values from -0.5 to 0.5
- depth_dy: float32 [128, 256], P('space'), may hold values from -0.5 to 0.5
- w_in: bfloat16 [1152, 2048], P(None, 'freq'), may hold values from -0.1875 to 0.1875
- w_out: bfloat16 [2048, 1152], P('freq'), may hold values from -0.125 to 0.125
Outputs:
- spectrum_out: float32 [32, 36, 128, 256], P('freq', None, 'space')
The draws below stay inside these ranges and needn't reach their ends.
All inputs are finite; a program needn't handle non-finite values. No bound on the sum of `land_sea` on one device may be relied on, other than what follows from the above.
Results may differ from the reference program's by a relative error of at most 0.003.
Values may be sent and summed in bfloat16 or wider, within the bound.
No kernel may reach another device: no remote copies, remote signals or barrier semaphores. Data moves between devices by JAX's collectives and lax.ppermute only.
A program may use at most 128 MiB of HBM per device.

```python
import math
import jax
import jax.numpy as jnp
from jax import lax

F = 32
DIRS = 36
HIDDEN_SIZE = 2048
PX = 32
PY = 256
STEPS = 2
CHAN = 1152
NX = 128


def touch_ends(array, rng, low, top_value):
    extent = array.shape
    index_at = [jax.random.randint(jax.random.fold_in(rng, axis), (), 0, extent[axis]) for axis in range(len(extent))]
    array = array.at[tuple(index_at)].set(low)
    longest = extent.index(max(extent))
    index_at[longest] = (index_at[longest] + 1) % extent[longest]
    return array.at[tuple(index_at)].set(top_value)


def steps_of(own_key, dims, pieces, least, high):
    factor_of, own = 1.0, jax.random.fold_in(own_key, 6)
    for axis_at, parts in pieces:
        heights = jnp.exp(jax.random.uniform(jax.random.fold_in(own, axis_at), (parts,), jnp.float32, least / len(pieces), high / len(pieces)))
        factor_of = factor_of * jnp.repeat(heights, dims[axis_at] // parts).reshape([-1 if axis == axis_at else 1 for axis in range(len(dims))])
    return factor_of


def bell_draw(stream_key, shape, width, reach, shards=(), kind=jnp.bfloat16):
    array = jax.random.normal(stream_key, shape, jnp.float32) * width
    if len(shards) > 0:
        array = steps_of(stream_key, shape, shards, -0.22, 0.18) * array
    return jnp.clip(array, min=-reach, max=reach).astype(kind)


def setup_inputs(seed: int = 0) -> dict:
    splits = jax.random.split(jax.random.key(seed), 9)
    spectrum = jnp.clip(jnp.exp(math.log(2.0) - 3.6888794 * jax.random.uniform(splits[0], (F, DIRS, NX, PY), jnp.float32) ** steps_of(splits[0], (F, DIRS, NX, PY), ((0, 8), (2, 4)), -0.2, 0.2)), 0.05, 2.0)
    land_sea = touch_ends((jax.random.randint(splits[1], (NX, PY), 0, 8) < 7).astype(jnp.int32), jax.random.fold_in(splits[1], 1), 0, 1)
    courant = jnp.clip(0.2 + 0.45 * jax.random.uniform(splits[2], (F,), jnp.float32) ** steps_of(splits[2], (F,), ((0, 8),), -0.2, 0.2), 0.2, 0.65)
    refract = jnp.clip(0.2 + 0.7 * jax.random.uniform(splits[3], (F,), jnp.float32) ** steps_of(splits[3], (F,), ((0, 8),), -0.2, 0.2), 0.2, 0.9)
    depth_dx = jnp.clip(jax.random.uniform(splits[4], (NX, PY), jnp.float32, -0.5, 0.5) * steps_of(splits[4], (NX, PY), ((0, 4),), -0.4, 0.0), -0.5, 0.5)
    depth_dy = jnp.clip(jax.random.uniform(splits[5], (NX, PY), jnp.float32, -0.5, 0.5) * steps_of(splits[5], (NX, PY), ((0, 4),), -0.4, 0.0), -0.5, 0.5)
    w_in = bell_draw(splits[6], (CHAN, HIDDEN_SIZE), CHAN ** -0.5, 0.1875, ((1, 8),))
    w_out = bell_draw(splits[7], (HIDDEN_SIZE, CHAN), HIDDEN_SIZE ** -0.5, 0.125, ((0, 8),))
    return dict(spectrum=spectrum, land_sea=land_sea, courant=courant, refract=refract, depth_dx=depth_dx, depth_dy=depth_dy, w_in=w_in, w_out=w_out)


step_scale = 0.5
epsilon = 1e-6


def direction_tables():
    angles = (jnp.arange(DIRS, dtype=jnp.float32) + 0.5) * (2.0 * math.pi / DIRS)
    return jnp.cos(angles), jnp.sin(angles)


def transport(padded, courant, refract, depth_dx, depth_dy, seamask):
    cosine, sine_dir = direction_tables()
    speed_x = courant[:, None] * cosine[None, :]
    speed_y = courant[:, None] * sine_dir[None, :]
    pos_x = jnp.maximum(speed_x, 0.0)[:, :, None, None]
    neg_x = jnp.maximum(-speed_x, 0.0)[:, :, None, None]
    pos_y = jnp.maximum(speed_y, 0.0)[:, :, None, None]
    neg_y = jnp.maximum(-speed_y, 0.0)[:, :, None, None]
    center = padded[:, :, 1:-1, 1:-1]
    keeping = 1.0 - jnp.abs(speed_x)[:, :, None, None] - jnp.abs(speed_y)[:, :, None, None]
    shifted = center * keeping + pos_x * padded[:, :, :-2, 1:-1] + neg_x * padded[:, :, 2:, 1:-1]
    shifted = shifted + pos_y * padded[:, :, 1:-1, :-2] + neg_y * padded[:, :, 1:-1, 2:]
    turn_rate = refract[:, None, None, None] * (sine_dir[None, :, None, None] * depth_dx[None, None]
                                                - cosine[None, :, None, None] * depth_dy[None, None])
    turn_pos = jnp.maximum(turn_rate, 0.0)
    turn_neg = jnp.maximum(-turn_rate, 0.0)
    turned = shifted * (1.0 - jnp.abs(turn_rate)) + jnp.roll(turn_pos * shifted, 1, axis=1)
    turned = turned + jnp.roll(turn_neg * shifted, -1, axis=1)
    return turned * seamask[None, None]


def interact(block, w_in, w_out):
    contract = (((0,), (0,)), ((), ()))
    energy_mean = jnp.mean(block, axis=0) + epsilon
    scaled = (block / energy_mean[None]).astype(jnp.bfloat16)
    preact = lax.dot_general(w_in, scaled, contract, preferred_element_type=jnp.float32)
    hidden = jax.nn.gelu(preact).astype(jnp.bfloat16)
    source = lax.dot_general(w_out, hidden, contract, preferred_element_type=jnp.float32).astype(jnp.bfloat16)
    return block * jnp.exp(step_scale * jnp.tanh(source.astype(jnp.float32)))


def reference(spectrum, land_sea, courant, refract, depth_dx, depth_dy, w_in, w_out):
    seamask = land_sea.astype(jnp.float32)
    field = spectrum
    blocks_count = NX // PX

    def one_frequency(inputs):
        layer, speed, bending = inputs
        padded = jnp.pad(layer[None], ((0, 0), (0, 0), (1, 1), (1, 1)))
        return transport(padded, speed[None], bending[None], depth_dx, depth_dy, seamask)[0]

    def one_block(block):
        return interact(block, w_in, w_out)

    for repeat in range(STEPS):
        field = lax.map(one_frequency, (field, courant, refract))
        blocks = field.reshape(CHAN, blocks_count, PX * PY).transpose(1, 0, 2)
        updated = lax.map(one_block, blocks)
        field = updated.transpose(1, 0, 2).reshape(F, DIRS, NX, PY)
    return field
```

```python
import math

import jax
import jax.numpy as jnp
from jax import lax
from jax.experimental import pallas as pl
from jax.experimental.pallas import tpu as pltpu
from jax.sharding import PartitionSpec as P

DIRS = 36
STEPS = 2
STEP_SCALE = 0.5
EPSILON = 1e-06
ROOT_MAX = 2.9
ENCODE = 32767.0 / ROOT_MAX
DECODE = ROOT_MAX / 32767.0
NCOEF = 7
BLOCK = 2 * DIRS
f32, bf16, i16 = jnp.float32, jnp.bfloat16, jnp.int16


def coefficients(courant, refract):
    angles = (jnp.arange(DIRS, dtype=f32) + 0.5) * (2.0 * math.pi / DIRS)
    cosine, sine = jnp.cos(angles), jnp.sin(angles)
    sx = courant[:, None] * cosine[None, :]
    sy = courant[:, None] * sine[None, :]
    keep = 1.0 - jnp.abs(sx) - jnp.abs(sy)
    parts = [
        keep,
        jnp.maximum(sx, 0.0),
        jnp.maximum(-sx, 0.0),
        jnp.maximum(sy, 0.0),
        jnp.maximum(-sy, 0.0),
        refract[:, None] * sine[None, :],
        refract[:, None] * cosine[None, :],
        jnp.zeros_like(sx),
    ]
    return jnp.stack(parts, axis=-1).reshape(-1, NCOEF + 1)


def encode(value):
    return (jnp.sqrt(value) * ENCODE + 0.5).astype(jnp.int32).astype(i16)


def decode(code):
    root = code.astype(jnp.int32).astype(f32) * DECODE
    return root * root


def spread(coef_ref, wide_ref, channels):
    @pl.loop(0, channels // BLOCK)
    def _(b):
        rows = pl.ds(pl.multiple_of(b * BLOCK, 8), BLOCK)
        part = coef_ref[rows, :]
        for k in range(NCOEF):
            wide_ref[k, rows, :] = jnp.broadcast_to(part[:, k : k + 1], (BLOCK, 128))


def transport(center, above, below, coefs, dx, dy, sea):
    rows, cols = center.shape
    lane = lax.broadcasted_iota(jnp.int32, (rows, cols), 1)
    west = jnp.where(lane == 0, 0.0, pltpu.roll(center, 1, 1))
    east = jnp.where(lane == cols - 1, 0.0, pltpu.roll(center, cols - 1, 1))
    keep, pos_x, neg_x, pos_y, neg_y, turn_x, turn_y = coefs
    shifted = center * keep + pos_x * above + neg_x * below + pos_y * west + neg_y * east
    turning = (turn_x * dx - turn_y * dy) * shifted
    forward = jnp.maximum(turning, 0.0)
    backward = forward - turning
    first = lax.broadcasted_iota(jnp.int32, (8, cols), 0)
    moved = pltpu.roll(forward, 1, 0)
    moved = jnp.concatenate(
        [
            jnp.where(first == 0, forward[DIRS - 1 : DIRS], moved[0:8]),
            moved[8:32],
            jnp.where(first == DIRS % 8, forward[2 * DIRS - 1 : 2 * DIRS], moved[32:40]),
            moved[40:72],
        ],
        axis=0,
    )
    other = pltpu.roll(backward, rows - 1, 0)
    other = jnp.concatenate(
        [
            other[0:32],
            jnp.where(first == (DIRS - 1) % 8, backward[0:1], other[32:40]),
            other[40:64],
            jnp.where(first == 7, backward[DIRS : DIRS + 1], other[64:72]),
        ],
        axis=0,
    )
    return (shifted - forward - backward + moved + other) * sea


def wide(ref, k, rows, cols):
    part = ref[k, rows, :]
    return jnp.concatenate([part] * (cols // 128), axis=1)


def first_kernel(groups, prows, spec_ref, low_ref, high_ref, coef_ref, dx_ref, dy_ref, sea_ref, out_ref, buf, coefw):
    channels, cols = low_ref.shape
    rows = groups * prows
    spread(coef_ref, coefw, channels)
    buf[0] = low_ref[...]
    buf[rows + 1] = high_ref[...]

    @pl.loop(0, rows)
    def _(r):
        for h in range(cols // 128):
            lanes = pl.ds(h * 128, 128)
            buf[r + 1, :, lanes] = spec_ref[h, pl.ds(r, channels, stride=rows), :]

    @pl.loop(0, groups)
    def _(g):
        @pl.loop(0, prows)
        def _(j):
            r = g * prows + j
            dx, dy, sea = (ref[pl.ds(r, 1), :] for ref in (dx_ref, dy_ref, sea_ref))
            for b in range(channels // BLOCK):
                part = pl.ds(b * BLOCK, BLOCK)
                coefs = [wide(coefw, k, part, cols) for k in range(NCOEF)]
                moved = transport(buf[r + 1, part, :], buf[r, part, :], buf[r + 2, part, :], coefs, dx, dy, sea)
                out_ref[g, j, part, :] = encode(moved)


def network(x_ref, hid_ref, win_ref, wout_ref, inverse, emit):
    hidden, channels = win_ref.shape
    mblock = min(512, hidden)
    for m in range(0, hidden, mblock):
        pre = jnp.dot(win_ref[m : m + mblock, :], x_ref[...], preferred_element_type=f32) * inverse
        act = 0.5 * pre * (1.0 + jnp.tanh(0.7978845608028654 * (pre + 0.044715 * pre * pre * pre)))
        hid_ref[m : m + mblock, :] = act.astype(bf16)
    cblock = 4 * BLOCK
    for c in range(0, channels, cblock):
        source = jnp.dot(wout_ref[c : c + cblock, :], hid_ref[...], preferred_element_type=f32)
        emit(c, cblock, jnp.exp(STEP_SCALE * jnp.tanh(source)))


def load_weights(groups, space, win_parts, wout_parts, win_ref, wout_ref, sem):
    copies = []
    spaces = len(win_parts)
    hidden = win_ref.shape[0]
    hpart = hidden // (groups * spaces)
    for n, part in enumerate(win_parts):
        for p in range(groups):
            row = pl.multiple_of(p * hpart * spaces + (space ^ n) * hpart, 8)
            slot = n * groups + p
            copies.append(
                pltpu.make_async_copy(part.at[pl.ds(p * hpart, hpart), :], win_ref.at[pl.ds(row, hpart), :], sem.at[slot])
            )
    many = spaces * groups
    for n, part in enumerate(wout_parts):
        size = part.shape[0]
        row = pl.multiple_of((space ^ n) * size, 8)
        copies.append(pltpu.make_async_copy(part, wout_ref.at[pl.ds(row, size), :], sem.at[many + n]))
    return copies


def step_one_kernel(groups, prows, many, space_ref, code_ref, *refs):
    win_parts, wout_parts = refs[:many], refs[many : 2 * many]
    field_ref, edge_ref, x_ref, hid_ref, win_ref, wout_ref, sem = refs[2 * many :]
    local = code_ref.shape[2]
    channels, cols = x_ref.shape
    copies = load_weights(groups, space_ref[0], win_parts, wout_parts, win_ref, wout_ref, sem)
    for copy in copies:
        copy.start()
    for copy in copies:
        copy.wait()

    @pl.loop(0, prows)
    def _(r):
        total = jnp.zeros((8, cols), f32)
        for q in range(groups):
            for b in range(local // BLOCK):
                part = pl.ds(b * BLOCK, BLOCK)
                at = pl.ds(q * local + b * BLOCK, BLOCK)
                value = decode(code_ref[q, r, part, :])
                field_ref[r, at, :] = value
                total = total + jnp.sum(value.reshape(BLOCK // 8, 8, cols), axis=0)
        total = jnp.sum(total, axis=0, keepdims=True)
        inverse = 1.0 / (total / channels + EPSILON)
        x_ref[...] = field_ref[r].astype(bf16)

        def emit(c, size, factor):
            part = pl.ds(c, size)
            field_ref[r, part, :] = field_ref[r, part, :] * factor

        network(x_ref, hid_ref, win_ref, wout_ref, inverse, emit)

        @pl.when(r == 0)
        def _():
            edge_ref[0] = encode(field_ref[r])

        @pl.when(r == prows - 1)
        def _():
            edge_ref[1] = encode(field_ref[r])


def step_two_kernel(groups, prows, many, space_ref, field_ref, low_ref, high_ref, coef_ref, dx_ref, dy_ref, sea_ref, *refs):
    win_parts, wout_parts = refs[:many], refs[many : 2 * many]
    out_ref, rows_ref, moved_ref, code_ref, coefw, x_ref, hid_ref, win_ref, wout_ref, sem = refs[2 * many :]
    local = out_ref.shape[2]
    channels, cols = x_ref.shape
    copies = load_weights(groups, space_ref[0], win_parts, wout_parts, win_ref, wout_ref, sem)
    for copy in copies:
        copy.start()
    spread(coef_ref, coefw, channels)
    rows_ref[0] = decode(low_ref[...])
    rows_ref[1] = decode(high_ref[...])
    for copy in copies:
        copy.wait()

    def one(r, above_ref, ra, below_ref, rb):
        dx, dy, sea = (ref[pl.ds(r, 1), :] for ref in (dx_ref, dy_ref, sea_ref))

        def blocks(b, total):
            part = pl.ds(pl.multiple_of(b * BLOCK, 8), BLOCK)
            coefs = [wide(coefw, k, part, cols) for k in range(NCOEF)]
            moved = transport(
                field_ref[r, part, :], above_ref[ra, part, :], below_ref[rb, part, :], coefs, dx, dy, sea
            )
            moved_ref[part, :] = moved
            return total + jnp.sum(moved.reshape(BLOCK // 8, 8, cols), axis=0)

        total = lax.fori_loop(0, channels // BLOCK, blocks, jnp.zeros((8, cols), f32))
        total = jnp.sum(total, axis=0, keepdims=True)
        inverse = 1.0 / (total / channels + EPSILON)
        x_ref[...] = moved_ref[...].astype(bf16)

        def emit(c, size, factor):
            part = pl.ds(c, size)
            moved_ref[part, :] = moved_ref[part, :] * factor

        network(x_ref, hid_ref, win_ref, wout_ref, inverse, emit)
        for q in range(groups):
            out_ref[q, r] = encode(moved_ref[pl.ds(q * local, local), :])

    if prows == 1:
        one(0, rows_ref, 0, rows_ref, 1)
        return
    one(0, rows_ref, 0, field_ref, 1)

    @pl.loop(1, prows - 1)
    def _(r):
        one(r, field_ref, r - 1, field_ref, r + 1)

    one(prows - 1, field_ref, prows - 2, rows_ref, 1)


def last_kernel(groups, prows, code_ref, out_ref):
    local, cols = code_ref.shape[2:]
    rows = groups * prows

    @pl.loop(0, groups)
    def _(g):
        @pl.loop(0, prows)
        def _(j):
            for b in range(local // BLOCK):
                value = decode(code_ref[g, j, pl.ds(b * BLOCK, BLOCK), :])
                start = (b * BLOCK) * rows + g * prows + j
                for h in range(cols // 128):
                    out_ref[h, pl.ds(start, BLOCK, stride=rows), :] = value[:, h * 128 : (h + 1) * 128]


def exchange(array, axis, bit):
    count = lax.axis_size(axis)
    return lax.ppermute(array, axis, [(i, i ^ bit) for i in range(count)])


def gather_freq(piece, dim, count):
    bit = count // 2
    bits = []
    while bit >= 1:
        bits.append(bit)
        bit //= 2
    have = piece
    for bit in bits:
        have = jnp.concatenate([have, exchange(have, "freq", bit)], axis=dim)
    return have, bits


def gather_space(have, count):
    parts = [have]
    bit = count // 2
    order = [0]
    while bit >= 1:
        parts = parts + [exchange(part, "space", bit) for part in parts]
        order = order + [o ^ bit for o in order]
        bit //= 2
    ranked = sorted(zip(order, range(len(parts))))
    return [parts[n] for _, n in ranked]


def split3(value):
    high = lax.reduce_precision(value, 8, 7)
    rest = value - high
    middle = lax.reduce_precision(rest, 8, 7)
    return [part.astype(bf16) for part in (high, middle, rest - middle)]


def body(spectrum, land_sea, courant, refract, depth_dx, depth_dy, w_in, w_out):
    groups, spaces = lax.axis_size("freq"), lax.axis_size("space")
    space, freq = lax.axis_index("space"), lax.axis_index("freq")
    freqs, dirs, rows, cols = spectrum.shape
    local = freqs * dirs
    channels = local * groups
    prows = rows // groups
    hidden_local = w_in.shape[1]
    hidden = hidden_local * groups
    sea = land_sea.astype(f32)

    last = spectrum[:, :, rows - 1, :].reshape(local, cols)
    first = spectrum[:, :, 0, :].reshape(local, cols)
    up = [(i, i + 1) for i in range(spaces - 1)]
    low = lax.ppermute(last, "space", up)
    high = lax.ppermute(first, "space", [(b, a) for a, b in up])

    hpart, cpart = hidden_local // spaces, channels // spaces
    win_piece = lax.dynamic_slice_in_dim(w_in, space * hpart, hpart, 1).T
    numbers = jnp.stack(split3(courant) + split3(refract))
    numbers = jnp.pad(numbers, ((0, 2), (0, channels - freqs)))
    win_piece = jnp.concatenate([numbers, win_piece], axis=0)
    wout_piece = lax.dynamic_slice_in_dim(w_out, space * cpart, cpart, 1).T
    win_have, bits = gather_freq(win_piece[None], 0, groups)
    wout_have, _ = gather_freq(wout_piece, 1, groups)
    order = [0]
    for bit in bits:
        order = order + [o ^ bit for o in order]
    numbers = win_have[:, 0:6, 0:freqs].astype(f32)
    numbers = numbers[:, 0:6:3] + numbers[:, 1:6:3] + numbers[:, 2:6:3]
    inverse_order = [order.index(n) for n in range(groups)]
    absolute = jnp.take(numbers, jnp.array(inverse_order, jnp.int32)[jnp.arange(groups) ^ freq], axis=0)
    coef_all = coefficients(absolute[:, 0].reshape(-1), absolute[:, 1].reshape(-1))
    win_have = win_have[:, 8:, :].reshape(groups * hpart, channels)
    win_parts = gather_space(win_have, spaces)
    wout_parts = gather_space(wout_have, spaces)
    many = len(win_parts)
    space_arr = space.reshape(1).astype(jnp.int32)

    any_spec = pl.BlockSpec(memory_space=pl.ANY)
    vmem = pl.BlockSpec(memory_space=pltpu.VMEM)
    smem = pl.BlockSpec(memory_space=pltpu.SMEM)
    code_shape = jax.ShapeDtypeStruct((groups, prows, local, cols), i16)
    net_scratch = [
        pltpu.VMEM((channels, cols), bf16),
        pltpu.VMEM((hidden, cols), bf16),
        pltpu.VMEM((hidden, channels), bf16),
        pltpu.VMEM((channels, hidden), bf16),
        pltpu.SemaphoreType.DMA((many * (groups + 1),)),
    ]
    params = pltpu.CompilerParams(vmem_limit_bytes=60 * 1024 * 1024)

    halves = cols // 128
    flat = spectrum.reshape(local * rows, halves, 128).transpose(1, 0, 2)
    sent = pl.pallas_call(
        lambda *refs: first_kernel(groups, prows, *refs),
        in_specs=[vmem] * 7,
        out_specs=vmem,
        out_shape=code_shape,
        scratch_shapes=[pltpu.VMEM((rows + 2, local, cols), f32), pltpu.VMEM((NCOEF, local, 128), f32)],
        compiler_params=params,
        name="first",
    )(flat, low, high, coefficients(courant, refract), depth_dx, depth_dy, sea)
    arrived = lax.all_to_all(sent, "freq", 0, 0, tiled=True)

    field, edges = pl.pallas_call(
        lambda *refs: step_one_kernel(groups, prows, many, *refs),
        in_specs=[smem, vmem] + [any_spec] * (2 * many),
        out_specs=(vmem, vmem),
        out_shape=(
            jax.ShapeDtypeStruct((prows, channels, cols), f32),
            jax.ShapeDtypeStruct((2, channels, cols), i16),
        ),
        scratch_shapes=net_scratch,
        compiler_params=params,
        name="step_one",
    )(space_arr, arrived, *win_parts, *wout_parts)

    chain = [(i, i + 1) for i in range(spaces * groups - 1)]
    low = lax.ppermute(edges[1], ("space", "freq"), chain)
    high = lax.ppermute(edges[0], ("space", "freq"), [(b, a) for a, b in chain])
    mine = [lax.dynamic_slice_in_dim(a, freq * prows, prows, 0) for a in (depth_dx, depth_dy, sea)]
    sent = pl.pallas_call(
        lambda *refs: step_two_kernel(groups, prows, many, *refs),
        in_specs=[smem] + [vmem] * 7 + [any_spec] * (2 * many),
        out_specs=vmem,
        out_shape=code_shape,
        scratch_shapes=[
            pltpu.VMEM((2, channels, cols), f32),
            pltpu.VMEM((channels, cols), f32),
            pltpu.VMEM((8, 128), i16),
            pltpu.VMEM((NCOEF, channels, 128), f32),
        ]
        + net_scratch,
        compiler_params=params,
        name="step_two",
    )(space_arr, field, low, high, coef_all, *mine, *win_parts, *wout_parts)
    arrived = lax.all_to_all(sent, "freq", 0, 0, tiled=True)

    out = pl.pallas_call(
        lambda *refs: last_kernel(groups, prows, *refs),
        in_specs=[vmem],
        out_specs=vmem,
        out_shape=jax.ShapeDtypeStruct((halves, local * rows, 128), f32),
        compiler_params=params,
        name="last",
    )(arrived)
    return out.transpose(1, 0, 2).reshape(freqs, dirs, rows, cols)


def solution(mesh):
    placed = (
        P("freq", None, "space", None),
        P("space", None),
        P("freq"),
        P("freq"),
        P("space", None),
        P("space", None),
        P(None, "freq"),
        P("freq", None),
    )
    return jax.shard_map(
        body, mesh=mesh, in_specs=placed, out_specs=P("freq", None, "space", None), check_vma=False
    )
```

```python
import math

import jax
import jax.numpy as jnp
from jax import lax
from jax.experimental import pallas as pl
from jax.experimental.pallas import tpu as pltpu
from jax.sharding import PartitionSpec as P

DIRS = 36
STEP_SCALE = 0.5
EPSILON = 1e-06
ROOT_MAX = 2.9
ENCODE = 32767.0 / ROOT_MAX
DECODE = ROOT_MAX / 32767.0
NCOEF = 7
BLOCK = 2 * DIRS
f32, bf16, i16, i32 = jnp.float32, jnp.bfloat16, jnp.int16, jnp.int32


def encode(value):
    return (jnp.sqrt(value) * ENCODE + 0.5).astype(i32).astype(i16)


def decode(code):
    root = code.astype(i32).astype(f32) * DECODE
    return root * root


def device_of(position, space, groups):
    flipped = position + (space & 1) * (groups - 1 - 2 * position)
    return flipped ^ ((flipped >> 1) & 1) if groups % 4 == 0 else flipped


def position_of(device, space, groups):
    flipped = device ^ ((device >> 1) & 1) if groups % 4 == 0 else device
    return flipped + (space & 1) * (groups - 1 - 2 * flipped)


def spread(numbers_ref, row, angle_ref, wide_ref, at):
    cosine, sine = angle_ref[0], angle_ref[1]
    second = lax.broadcasted_iota(i32, (BLOCK, 128), 0) >= DIRS
    courant = jnp.where(second, numbers_ref[0, row + 1], numbers_ref[0, row])
    refract = jnp.where(second, numbers_ref[1, row + 1], numbers_ref[1, row])
    sx, sy = courant * cosine, courant * sine
    values = [
        1.0 - jnp.abs(sx) - jnp.abs(sy),
        jnp.maximum(sx, 0.0),
        jnp.maximum(-sx, 0.0),
        jnp.maximum(sy, 0.0),
        jnp.maximum(-sy, 0.0),
        refract * sine,
        refract * cosine,
    ]
    for k, value in enumerate(values):
        wide_ref[k, pl.ds(at, BLOCK), :] = value


def transport(center, above, below, coefs, dx, dy, sea):
    rows, cols = center.shape
    lane = lax.broadcasted_iota(i32, (rows, cols), 1)
    west = jnp.where(lane == 0, 0.0, pltpu.roll(center, 1, 1))
    east = jnp.where(lane == cols - 1, 0.0, pltpu.roll(center, cols - 1, 1))
    keep, pos_x, neg_x, pos_y, neg_y, turn_x, turn_y = coefs
    shifted = center * keep + pos_x * above + neg_x * below + pos_y * west + neg_y * east
    turning = (turn_x * dx - turn_y * dy) * shifted
    forward = jnp.maximum(turning, 0.0)
    backward = forward - turning
    first = lax.broadcasted_iota(i32, (8, cols), 0)
    moved = pltpu.roll(forward, 1, 0)
    moved = jnp.concatenate(
        [
            jnp.where(first == 0, forward[DIRS - 1 : DIRS], moved[0:8]),
            moved[8:32],
            jnp.where(first == DIRS % 8, forward[2 * DIRS - 1 : 2 * DIRS], moved[32:40]),
            moved[40:72],
        ],
        axis=0,
    )
    other = pltpu.roll(backward, rows - 1, 0)
    other = jnp.concatenate(
        [
            other[0:32],
            jnp.where(first == (DIRS - 1) % 8, backward[0:1], other[32:40]),
            other[40:64],
            jnp.where(first == 7, backward[DIRS : DIRS + 1], other[64:72]),
        ],
        axis=0,
    )
    return (shifted - forward - backward + moved + other) * sea


def wide(ref, k, rows, cols):
    part = ref[k, rows, :]
    return jnp.concatenate([part] * (cols // 128), axis=1)


def first_kernel(split, groups, prows, where_ref, numbers_ref, spec_ref, low_ref, high_ref, dx_ref, dy_ref, sea_ref, *refs):
    outs, (shifted_ref, turning_ref) = refs[: len(split)], refs[len(split) :]
    channels, cols = low_ref.shape
    rows = groups * prows
    space = where_ref[0]
    line = lax.broadcasted_iota(i32, (rows, cols), 0)
    lane = lax.broadcasted_iota(i32, (rows, cols), 1)
    angles = [(d + 0.5) * (2.0 * math.pi / DIRS) for d in range(DIRS)]

    @pl.loop(0, channels // DIRS)
    def _(f):
        courant, refract = numbers_ref[0, f], numbers_ref[1, f]
        dx, dy = dx_ref[...] * refract, dy_ref[...] * refract
        for d in range(DIRS):
            c = f * DIRS + d
            cosine, sine = math.cos(angles[d]), math.sin(angles[d])
            center = spec_ref[pl.ds(pl.multiple_of(c * rows, 8), rows), :]
            if cosine > 0:
                beside = jnp.where(line == 0, low_ref[pl.ds(c, 1), :], pltpu.roll(center, 1, 0))
            else:
                beside = jnp.where(line == rows - 1, high_ref[pl.ds(c, 1), :], pltpu.roll(center, rows - 1, 0))
            if sine > 0:
                behind = jnp.where(lane == 0, 0.0, pltpu.roll(center, 1, 1))
            else:
                behind = jnp.where(lane == cols - 1, 0.0, pltpu.roll(center, cols - 1, 1))
            sx, sy = courant * abs(cosine), courant * abs(sine)
            shifted = center * (1.0 - sx - sy) + beside * sx + behind * sy
            shifted_ref[c] = shifted
            turning_ref[c] = (sine * dx - cosine * dy) * shifted

    some = 16 if channels % 16 == 0 else 8

    @pl.loop(0, rows // 8)
    def _(t):
        tall = pl.ds(pl.multiple_of(t * 8, 8), 8)
        for h in range(cols // 128):
            lanes = pl.ds(h * 128, 128)
            sea = sea_ref[tall, lanes].astype(f32)
            for at in range(0, channels, some):
                tile = []
                for c in range(at, at + some):
                    f, d = divmod(c, DIRS)
                    before = turning_ref[f * DIRS + (d - 1) % DIRS, tall, lanes]
                    after = turning_ref[f * DIRS + (d + 1) % DIRS, tall, lanes]
                    value = shifted_ref[c, tall, lanes] - jnp.abs(turning_ref[c, tall, lanes])
                    tile.append((value + jnp.maximum(before, 0.0) - jnp.minimum(after, 0.0)) * sea)
                tile = jnp.swapaxes(jnp.stack(tile), 0, 1)
                for k in range(8):
                    j = k % prows
                    q = device_of(t * (8 // prows) + k // prows, space, groups)
                    for out, members in zip(outs, split):
                        if j in members:
                            out[q, members.index(j), pl.ds(at, some), lanes] = encode(tile[k])


def network(x_ref, hid_ref, win_ref, wout_ref, inverse, emit):
    hidden, channels = win_ref.shape
    mblock = min(512, hidden)
    for m in range(0, hidden, mblock):
        pre = jnp.dot(win_ref[m : m + mblock, :], x_ref[...], preferred_element_type=f32) * inverse
        act = 0.5 * pre * (1.0 + jnp.tanh(0.7978845608028654 * (pre + 0.044715 * pre * pre * pre)))
        hid_ref[m : m + mblock, :] = act.astype(bf16)
    cblock = 4 * BLOCK
    for c in range(0, channels, cblock):
        source = jnp.dot(wout_ref[c : c + cblock, :], hid_ref[...], preferred_element_type=f32)
        emit(c, cblock, jnp.exp(STEP_SCALE * jnp.tanh(source)))


def load_weights(plan, space, parts, win_ref, wout_ref, sem):
    copies = []
    for part, (kind, places, size, width) in zip(parts, plan):
        for n, (f, s) in enumerate(places):
            if kind == 0:
                row = pl.multiple_of(f * width + (space ^ s) * size, 8)
                target = win_ref.at[pl.ds(row, size), :]
            else:
                row = pl.multiple_of((space ^ s) * size, 8)
                target = wout_ref.at[pl.ds(row, size), pl.ds(f * width, width)]
            copies.append(pltpu.make_async_copy(part.at[n, pl.ds(0, size), :], target, sem.at[len(copies)]))
    for copy in copies:
        copy.start()

    def wait():
        for copy in copies:
            copy.wait()

    return wait


def mean_inverse(total, channels):
    total = jnp.sum(total, axis=0, keepdims=True)
    return 1.0 / (total * (1.0 / channels) + EPSILON)


def step_one_kernel(own, groups, plan, edges, where_ref, code_ref, *refs):
    parts, refs = refs[: len(plan)], refs[len(plan) :]
    field_ref, refs = refs[0], refs[1:]
    edge_refs, (x_ref, hid_ref, win_ref, wout_ref, sem) = refs[: 2 * edges], refs[2 * edges :]
    local = code_ref.shape[2]
    channels, cols = x_ref.shape
    wait = load_weights(plan, where_ref[0], parts, win_ref, wout_ref, sem)
    for n in range(len(own)):
        def block(q, total):
            for b in range(local // BLOCK):
                part = pl.ds(b * BLOCK, BLOCK)
                at = pl.ds(pl.multiple_of(q * local + b * BLOCK, 8), BLOCK)
                value = decode(code_ref[q, n, part, :])
                field_ref[n, at, :] = value
                total = total + jnp.sum(value.reshape(BLOCK // 8, 8, cols), axis=0)
            return total

        total = lax.fori_loop(0, groups, block, jnp.zeros((8, cols), f32))
        inverse = mean_inverse(total, channels)
        x_ref[...] = field_ref[n].astype(bf16)
        if n == 0:
            wait()

        def emit(c, size, factor):
            part = pl.ds(c, size)
            field_ref[n, part, :] = field_ref[n, part, :] * factor

        network(x_ref, hid_ref, win_ref, wout_ref, inverse, emit)
        if edges and n == 0:
            edge_refs[0][...] = encode(field_ref[n])
        if edges and n == len(own) - 1:
            edge_refs[1][...] = encode(field_ref[n])


def step_two_kernel(own, split, groups, prows, plan, with_halo, where_ref, numbers_ref, angle_ref, dx_ref, dy_ref, sea_ref, *refs):
    fields, refs = refs[: len(split)], refs[len(split) :]
    halos, refs = refs[: 2 * with_halo], refs[2 * with_halo :]
    parts, refs = refs[: len(plan)], refs[len(plan) :]
    out_ref, halo_ref, moved_ref, coefw, x_ref, hid_ref, win_ref, wout_ref, sem = refs
    local = out_ref.shape[2]
    channels, cols = x_ref.shape
    space, device = where_ref[0], where_ref[1]
    wait = load_weights(plan, space, parts, win_ref, wout_ref, sem)
    for n, halo in enumerate(halos):
        halo_ref[n] = decode(halo[...])

    @pl.loop(0, groups)
    def _(q):
        row = (q ^ device) * (local // DIRS)
        for b in range(local // BLOCK):
            at = pl.multiple_of(q * local + b * BLOCK, 8)
            spread(numbers_ref, row + 2 * b, angle_ref, coefw, at)

    def held(j):
        if j < 0:
            return halo_ref, 0
        if j >= prows:
            return halo_ref, 1
        for field, members in zip(fields, split):
            if j in members:
                return field, members.index(j)

    first_row = position_of(device, space, groups) * prows
    for n, j in enumerate(own):
        r = first_row + j
        dx, dy = dx_ref[pl.ds(r, 1), :], dy_ref[pl.ds(r, 1), :]
        sea = sea_ref[pl.ds(r, 1), :].astype(f32)
        (here, hn), (above, an), (below, bn) = held(j), held(j - 1), held(j + 1)

        def block(b, total):
            part = pl.ds(pl.multiple_of(b * BLOCK, 8), BLOCK)
            coefs = [wide(coefw, k, part, cols) for k in range(NCOEF)]
            moved = transport(here[hn, part, :], above[an, part, :], below[bn, part, :], coefs, dx, dy, sea)
            moved_ref[part, :] = moved
            return total + jnp.sum(moved.reshape(BLOCK // 8, 8, cols), axis=0)

        total = lax.fori_loop(0, channels // BLOCK, block, jnp.zeros((8, cols), f32))
        inverse = mean_inverse(total, channels)
        x_ref[...] = moved_ref[...].astype(bf16)
        if n == 0:
            wait()

        def emit(c, size, factor):
            part = pl.ds(c, size)
            moved_ref[part, :] = moved_ref[part, :] * factor

        network(x_ref, hid_ref, win_ref, wout_ref, inverse, emit)

        @pl.loop(0, groups)
        def _(q):
            out_ref[q, n] = encode(moved_ref[pl.ds(pl.multiple_of(q * local, 8), local), :])


def last_kernel(split, groups, prows, where_ref, *refs):
    codes, out_ref = refs[:-1], refs[-1]
    local, cols = codes[0].shape[2:]
    rows = groups * prows
    space = where_ref[0]
    together = max(1, 8 // prows)
    some = 16 if local % 16 == 0 else 8

    @pl.loop(0, groups // together)
    def _(t):
        owners = [device_of(t * together + k, space, groups) for k in range(together)]

        @pl.loop(0, local // some)
        def _(c):
            at = pl.multiple_of(c * some, some)
            for h in range(cols // 128):
                lanes = pl.ds(h * 128, 128)
                tile = []
                for q in owners:
                    for j in range(prows):
                        for code, members in zip(codes, split):
                            if j in members:
                                tile.append(decode(code[q, members.index(j), pl.ds(at, some), lanes]))
                tile = jnp.swapaxes(jnp.stack(tile), 0, 1)
                for k in range(some):
                    start = pl.multiple_of((at + k) * rows + t * (together * prows), 8)
                    out_ref[pl.ds(start, together * prows), lanes] = tile[k]


def exchange(array, axis, bit):
    count = lax.axis_size(axis)
    return lax.ppermute(array, axis, [(i, i ^ bit) for i in range(count)])


def gather(piece, stages):
    have, places = piece[None], [(0, 0)]
    arrays = [(have, places)]
    for n, (axis, bit) in enumerate(stages):
        got = []
        for have, places in arrays:
            flip = [(f ^ bit, s) if axis == "freq" else (f, s ^ bit) for f, s in places]
            got.append((exchange(have, axis, bit), flip))
        if n < len(stages) - 2:
            (have, places), (more, flip) = arrays[0], got[0]
            arrays = [(jnp.concatenate([have, more], axis=0), places + flip)]
        else:
            arrays = arrays + got
    return arrays


def bits_of(count):
    return [1 << n for n in reversed(range(count.bit_length() - 1))]


def split3(value):
    high = lax.reduce_precision(value, 8, 7)
    rest = value - high
    middle = lax.reduce_precision(rest, 8, 7)
    return [part.astype(bf16) for part in (high, middle, rest - middle)]


def body(spectrum, land_sea, courant, refract, depth_dx, depth_dy, w_in, w_out):
    groups, spaces = lax.axis_size("freq"), lax.axis_size("space")
    space, freq = lax.axis_index("space"), lax.axis_index("freq")
    freqs, dirs, rows, cols = spectrum.shape
    local = freqs * dirs
    channels = local * groups
    prows = rows // groups
    hidden_local = w_in.shape[1]
    hidden = hidden_local * groups

    last = spectrum[:, :, rows - 1, :].reshape(local, cols)
    first = spectrum[:, :, 0, :].reshape(local, cols)
    up = [(i, i + 1) for i in range(spaces - 1)]
    low = lax.ppermute(last, "space", up)
    high = lax.ppermute(first, "space", [(b, a) for a, b in up])

    hpart, cpart = hidden_local // spaces, channels // spaces
    win_piece = lax.dynamic_slice_in_dim(w_in, space * hpart, hpart, 1).T
    numbers = jnp.stack(split3(courant) + split3(refract))
    numbers = jnp.pad(numbers, ((0, 2), (0, channels - freqs)))
    win_piece = jnp.concatenate([win_piece, numbers], axis=0)
    wout_piece = lax.dynamic_slice_in_dim(w_out, space * cpart, cpart, 1).T
    along_freq = [("freq", bit) for bit in bits_of(groups)]
    along_space = [("space", bit) for bit in bits_of(spaces)]
    win_arrays = gather(win_piece, along_freq + along_space)
    wout_arrays = gather(wout_piece, along_freq[:-1] + along_space[:1] + along_freq[-1:] + along_space[1:])
    plan, parts = [], []
    for kind, arrays, size in ((0, win_arrays, hpart), (1, wout_arrays, cpart)):
        for have, places in arrays:
            plan.append((kind, places, size, hidden_local))
            parts.append(have)
    have, places = win_arrays[0]
    found = {f: n for n, (f, s) in reversed(list(enumerate(places)))}
    raw = have[:, hpart : hpart + 6, 0:freqs].astype(f32)
    raw = raw.reshape(len(places), 2, 3, freqs).sum(axis=2)
    numbers = jnp.concatenate([raw[found[f]] for f in range(groups)], axis=1)
    copies = sum(len(places) for _, places, _, _ in plan)

    angles = (jnp.arange(DIRS, dtype=f32) + 0.5) * (2.0 * math.pi / DIRS)
    angles = jnp.stack([jnp.cos(angles), jnp.sin(angles)])
    angles = jnp.broadcast_to(jnp.tile(angles, (1, 2))[:, :, None], (2, BLOCK, 128))
    place = jnp.stack([space, freq]).astype(i32)

    any_spec = pl.BlockSpec(memory_space=pl.ANY)
    vmem = pl.BlockSpec(memory_space=pltpu.VMEM)
    smem = pl.BlockSpec(memory_space=pltpu.SMEM)
    params = pltpu.CompilerParams(vmem_limit_bytes=60 * 1024 * 1024)
    net_scratch = [
        pltpu.VMEM((channels, cols), bf16),
        pltpu.VMEM((hidden, cols), bf16),
        pltpu.VMEM((hidden, channels), bf16),
        pltpu.VMEM((channels, hidden), bf16),
        pltpu.SemaphoreType.DMA((copies,)),
    ]

    outer = sorted({0, prows - 1})
    inner = [j for j in range(prows) if j not in outer]
    split = [outer] + ([inner] if inner else [])

    def code_shape(own):
        return jax.ShapeDtypeStruct((groups, len(own), local, cols), i16)

    flat = spectrum.reshape(local * rows, cols)
    sent = pl.pallas_call(
        lambda *refs: first_kernel(split, groups, prows, *refs),
        in_specs=[smem, smem] + [vmem] * 6,
        out_specs=[vmem] * len(split),
        out_shape=[code_shape(own) for own in split],
        scratch_shapes=[pltpu.VMEM((local, rows, cols), f32)] * 2,
        compiler_params=params,
        name="first",
    )(place, jnp.stack([courant, refract]), flat, low, high, depth_dx, depth_dy, land_sea)
    arrived = [lax.all_to_all(part, "freq", 0, 0, tiled=True) for part in sent]

    fields = []
    for own, codes in zip(split, arrived):
        edges = own is outer
        edge_shape = [jax.ShapeDtypeStruct((channels, cols), i16)] * (2 * edges)
        made = pl.pallas_call(
            lambda *refs, own=own, edges=edges: step_one_kernel(own, groups, plan, edges, *refs),
            in_specs=[smem, vmem] + [any_spec] * len(plan),
            out_specs=[vmem] * (1 + len(edge_shape)),
            out_shape=[jax.ShapeDtypeStruct((len(own), channels, cols), f32)] + edge_shape,
            scratch_shapes=net_scratch,
            compiler_params=params,
            name="step_one",
        )(place, codes, *parts)
        fields.append(made[0])
        if edges:
            edge = made[1:]

    chain = []
    for n in range(spaces * groups):
        s, p = divmod(n, groups)
        chain.append(s * groups + device_of(p, s, groups))
    chain = list(zip(chain[:-1], chain[1:]))
    low = lax.ppermute(edge[1], ("space", "freq"), chain)
    high = lax.ppermute(edge[0], ("space", "freq"), [(b, a) for a, b in chain])

    arrived = [None] * len(split)
    for own in reversed(split):
        halo = own is outer
        sent = pl.pallas_call(
            lambda *refs, own=own, halo=halo: step_two_kernel(own, split, groups, prows, plan, halo, *refs),
            in_specs=[smem, smem] + [vmem] * (4 + len(split) + 2 * halo) + [any_spec] * len(plan),
            out_specs=vmem,
            out_shape=code_shape(own),
            scratch_shapes=[
                pltpu.VMEM((2, channels, cols) if halo else (1, 8, 128), f32),
                pltpu.VMEM((channels, cols), f32),
                pltpu.VMEM((NCOEF, channels, 128), f32),
            ]
            + net_scratch,
            compiler_params=params,
            name="step_two",
        )(place, numbers, angles, depth_dx, depth_dy, land_sea, *fields, *((low, high) if halo else ()), *parts)
        arrived[split.index(own)] = lax.all_to_all(sent, "freq", 0, 0, tiled=True)

    out = pl.pallas_call(
        lambda *refs: last_kernel(split, groups, prows, *refs),
        in_specs=[smem] + [vmem] * len(split),
        out_specs=vmem,
        out_shape=jax.ShapeDtypeStruct((local * rows, cols), f32),
        compiler_params=params,
        name="last",
    )(place, *arrived)
    return out.reshape(freqs, dirs, rows, cols)


def solution(mesh):
    placed = (
        P("freq", None, "space", None),
        P("space", None),
        P("freq"),
        P("freq"),
        P("space", None),
        P("space", None),
        P(None, "freq"),
        P("freq", None),
    )
    return jax.shard_map(
        body, mesh=mesh, in_specs=placed, out_specs=P("freq", None, "space", None), check_vma=False
    )
```

```python
import math

import jax
import jax.numpy as jnp
from jax import lax
from jax.experimental import pallas as pl
from jax.experimental.pallas import tpu as pltpu
from jax.sharding import PartitionSpec as P

DIRS = 36
STEP_SCALE = 0.5
EPSILON = 1e-06
ROOT_MAX = 2.9
ENCODE = 32767.0 / ROOT_MAX
DECODE = ROOT_MAX / 32767.0
NCOEF = 7
BLOCK = 2 * DIRS
f32, bf16, i16, i32 = jnp.float32, jnp.bfloat16, jnp.int16, jnp.int32


def encode(value):
    return (jnp.sqrt(value) * ENCODE + 0.5).astype(i32).astype(i16)


def decode(code):
    root = code.astype(i32).astype(f32) * DECODE
    return root * root


def device_of(position, space, groups):
    flipped = position + (space & 1) * (groups - 1 - 2 * position)
    return flipped ^ ((flipped >> 1) & 1) if groups % 4 == 0 else flipped


def position_of(device, space, groups):
    flipped = device ^ ((device >> 1) & 1) if groups % 4 == 0 else device
    return flipped + (space & 1) * (groups - 1 - 2 * flipped)


def spread(numbers_ref, row, angle_ref, wide_ref, at):
    cosine, sine = angle_ref[0], angle_ref[1]
    second = lax.broadcasted_iota(i32, (BLOCK, 128), 0) >= DIRS
    courant = jnp.where(second, numbers_ref[0, row + 1], numbers_ref[0, row])
    refract = jnp.where(second, numbers_ref[1, row + 1], numbers_ref[1, row])
    sx, sy = courant * cosine, courant * sine
    values = [
        1.0 - jnp.abs(sx) - jnp.abs(sy),
        jnp.maximum(sx, 0.0),
        jnp.maximum(-sx, 0.0),
        jnp.maximum(sy, 0.0),
        jnp.maximum(-sy, 0.0),
        refract * sine,
        refract * cosine,
    ]
    for k, value in enumerate(values):
        wide_ref[k, pl.ds(at, BLOCK), :] = value


def transport(center, above, below, coefs, dx, dy, sea):
    rows, cols = center.shape
    lane = lax.broadcasted_iota(i32, (rows, cols), 1)
    west = jnp.where(lane == 0, 0.0, pltpu.roll(center, 1, 1))
    east = jnp.where(lane == cols - 1, 0.0, pltpu.roll(center, cols - 1, 1))
    keep, pos_x, neg_x, pos_y, neg_y, turn_x, turn_y = coefs
    shifted = center * keep + pos_x * above + neg_x * below + pos_y * west + neg_y * east
    turning = (turn_x * dx - turn_y * dy) * shifted
    forward = jnp.maximum(turning, 0.0)
    backward = forward - turning
    first = lax.broadcasted_iota(i32, (8, cols), 0)
    moved = pltpu.roll(forward, 1, 0)
    moved = jnp.concatenate(
        [
            jnp.where(first == 0, forward[DIRS - 1 : DIRS], moved[0:8]),
            moved[8:32],
            jnp.where(first == DIRS % 8, forward[2 * DIRS - 1 : 2 * DIRS], moved[32:40]),
            moved[40:72],
        ],
        axis=0,
    )
    other = pltpu.roll(backward, rows - 1, 0)
    other = jnp.concatenate(
        [
            other[0:32],
            jnp.where(first == (DIRS - 1) % 8, backward[0:1], other[32:40]),
            other[40:64],
            jnp.where(first == 7, backward[DIRS : DIRS + 1], other[64:72]),
        ],
        axis=0,
    )
    return (shifted - forward - backward + moved + other) * sea


def wide(ref, k, rows, cols):
    part = ref[k, rows, :]
    return jnp.concatenate([part] * (cols // 128), axis=1)


def first_kernel(split, groups, prows, where_ref, numbers_ref, spec_ref, low_ref, high_ref, dx_ref, dy_ref, sea_ref, *refs):
    outs, (shifted_ref, turning_ref) = refs[: len(split) * groups], refs[len(split) * groups :]
    channels, cols = low_ref.shape
    rows = groups * prows
    space, device = where_ref[0], where_ref[1]
    line = lax.broadcasted_iota(i32, (rows, cols), 0)
    lane = lax.broadcasted_iota(i32, (rows, cols), 1)
    angles = [(d + 0.5) * (2.0 * math.pi / DIRS) for d in range(DIRS)]

    @pl.loop(0, channels // DIRS)
    def _(f):
        courant, refract = numbers_ref[0, f], numbers_ref[1, f]
        dx, dy = dx_ref[...] * refract, dy_ref[...] * refract
        for d in range(DIRS):
            c = f * DIRS + d
            cosine, sine = math.cos(angles[d]), math.sin(angles[d])
            center = spec_ref[pl.ds(pl.multiple_of(c * rows, 8), rows), :]
            if cosine > 0:
                beside = jnp.where(line == 0, low_ref[pl.ds(c, 1), :], pltpu.roll(center, 1, 0))
            else:
                beside = jnp.where(line == rows - 1, high_ref[pl.ds(c, 1), :], pltpu.roll(center, rows - 1, 0))
            if sine > 0:
                behind = jnp.where(lane == 0, 0.0, pltpu.roll(center, 1, 1))
            else:
                behind = jnp.where(lane == cols - 1, 0.0, pltpu.roll(center, cols - 1, 1))
            sx, sy = courant * abs(cosine), courant * abs(sine)
            shifted = center * (1.0 - sx - sy) + beside * sx + behind * sy
            shifted_ref[c] = shifted
            turning_ref[c] = (sine * dx - cosine * dy) * shifted

    some = 16 if channels % 16 == 0 else 8

    share = 8 // prows

    for tile_at in range(0, groups, share):
        t = position_of(tile_at ^ device, space, groups) // share
        tall = pl.ds(pl.multiple_of(t * 8, 8), 8)
        slots = [(device_of(t * share + i, space, groups) ^ device) - tile_at for i in range(share)]

        @pl.loop(0, channels // some)
        def _(n):
            at = pl.multiple_of(n * some, some)
            for h in range(cols // 128):
                lanes = pl.ds(h * 128, 128)
                sea = sea_ref[tall, lanes].astype(f32)
                tile = []
                for i in range(some):
                    c = at + i
                    d = c % DIRS
                    before = turning_ref[jnp.where(d == 0, c + DIRS - 1, c - 1), tall, lanes]
                    after = turning_ref[jnp.where(d == DIRS - 1, c - DIRS + 1, c + 1), tall, lanes]
                    value = shifted_ref[c, tall, lanes] - jnp.abs(turning_ref[c, tall, lanes])
                    tile.append((value + jnp.maximum(before, 0.0) - jnp.minimum(after, 0.0)) * sea)
                tile = encode(jnp.swapaxes(jnp.stack(tile), 0, 1))
                for slot in range(share):
                    for j in range(prows):
                        value = tile[j]
                        for i in range(1, share):
                            value = jnp.where(slots[i] == slot, tile[i * prows + j], value)
                        for m, members in enumerate(split):
                            if j in members:
                                out = outs[m * groups + tile_at + slot]
                                out[members.index(j), pl.ds(at, some), lanes] = value


def network(x_ref, hid_ref, win_ref, wout_ref, inverse, emit, wait):
    hidden, channels = win_ref.shape
    if wait:
        wait(0)
    mblock = min(512, hidden)
    for m in range(0, hidden, mblock):
        pre = jnp.dot(win_ref[m : m + mblock, :], x_ref[...], preferred_element_type=f32) * inverse
        act = 0.5 * pre * (1.0 + jnp.tanh(0.7978845608028654 * (pre + 0.044715 * pre * pre * pre)))
        hid_ref[m : m + mblock, :] = act.astype(bf16)
    if wait:
        wait(1)
    cblock = 4 * BLOCK
    for c in range(0, channels, cblock):
        source = jnp.dot(wout_ref[c : c + cblock, :], hid_ref[...], preferred_element_type=f32)
        emit(c, cblock, jnp.exp(STEP_SCALE * jnp.tanh(source)))


def load_weights(plan, space, parts, win_ref, wout_ref, sem):
    copies = []
    for part, (kind, places, size, width) in zip(parts, plan):
        for n, (f, s) in enumerate(places):
            if kind == 0:
                row = pl.multiple_of(f * width + (space ^ s) * size, 8)
                target = win_ref.at[pl.ds(row, size), :]
            else:
                row = pl.multiple_of((space ^ s) * size, 8)
                target = wout_ref.at[pl.ds(row, size), pl.ds(f * width, width)]
            copies.append(pltpu.make_async_copy(part.at[n, pl.ds(0, size), :], target, sem.at[len(copies)]))
    for copy in copies:
        copy.start()

    first = sum(len(places) for kind, places, _, _ in plan if kind == 0)

    def wait(kind):
        for copy in copies[:first] if kind == 0 else copies[first:]:
            copy.wait()

    return wait


def mean_inverse(total, channels):
    total = jnp.sum(total, axis=0, keepdims=True)
    return 1.0 / (total * (1.0 / channels) + EPSILON)


def step_one_kernel(own, groups, plan, edges, where_ref, *refs):
    codes, refs = refs[:groups], refs[groups:]
    parts, refs = refs[: len(plan)], refs[len(plan) :]
    field_ref, refs = refs[0], refs[1:]
    edge_refs, (x_ref, hid_ref, win_ref, wout_ref, sem) = refs[: 2 * edges], refs[2 * edges :]
    local = codes[0].shape[1]
    channels, cols = x_ref.shape
    wait = load_weights(plan, where_ref[0], parts, win_ref, wout_ref, sem)
    for n in range(len(own)):
        total = jnp.zeros((8, cols), f32)
        for k in range(groups):
            row = (k ^ where_ref[1]) * local
            for b in range(local // BLOCK):
                value = decode(codes[k][n, pl.ds(b * BLOCK, BLOCK), :])
                field_ref[n, pl.ds(pl.multiple_of(row + b * BLOCK, 8), BLOCK), :] = value
                total = total + jnp.sum(value.reshape(BLOCK // 8, 8, cols), axis=0)
        inverse = mean_inverse(total, channels)
        x_ref[...] = field_ref[n].astype(bf16)

        def emit(c, size, factor):
            part = pl.ds(c, size)
            field_ref[n, part, :] = field_ref[n, part, :] * factor

        network(x_ref, hid_ref, win_ref, wout_ref, inverse, emit, wait if n == 0 else None)
        if edges and n == 0:
            edge_refs[0][...] = encode(field_ref[n])
        if edges and n == len(own) - 1:
            edge_refs[1][...] = encode(field_ref[n])


def step_two_kernel(own, split, groups, prows, plan, with_halo, where_ref, numbers_ref, angle_ref, dx_ref, dy_ref, sea_ref, *refs):
    fields, refs = refs[: len(split)], refs[len(split) :]
    halos, refs = refs[: 2 * with_halo], refs[2 * with_halo :]
    parts, refs = refs[: len(plan)], refs[len(plan) :]
    outs, refs = refs[:groups], refs[groups:]
    halo_ref, moved_ref, coefw, x_ref, hid_ref, win_ref, wout_ref, sem = refs
    local = outs[0].shape[1]
    channels, cols = x_ref.shape
    space, device = where_ref[0], where_ref[1]
    wait = load_weights(plan, space, parts, win_ref, wout_ref, sem)
    for n, halo in enumerate(halos):
        halo_ref[n] = decode(halo[...])

    @pl.loop(0, groups)
    def _(q):
        row = (q ^ device) * (local // DIRS)
        for b in range(local // BLOCK):
            at = pl.multiple_of(q * local + b * BLOCK, 8)
            spread(numbers_ref, row + 2 * b, angle_ref, coefw, at)

    def held(j):
        if j < 0:
            return halo_ref, 0
        if j >= prows:
            return halo_ref, 1
        for field, members in zip(fields, split):
            if j in members:
                return field, members.index(j)

    first_row = position_of(device, space, groups) * prows
    for n, j in enumerate(own):
        r = first_row + j
        dx, dy = dx_ref[pl.ds(r, 1), :], dy_ref[pl.ds(r, 1), :]
        sea = sea_ref[pl.ds(r, 1), :].astype(f32)
        (here, hn), (above, an), (below, bn) = held(j), held(j - 1), held(j + 1)

        def block(b, total):
            part = pl.ds(pl.multiple_of(b * BLOCK, 8), BLOCK)
            coefs = [wide(coefw, k, part, cols) for k in range(NCOEF)]
            moved = transport(here[hn, part, :], above[an, part, :], below[bn, part, :], coefs, dx, dy, sea)
            moved_ref[part, :] = moved
            return total + jnp.sum(moved.reshape(BLOCK // 8, 8, cols), axis=0)

        total = lax.fori_loop(0, channels // BLOCK, block, jnp.zeros((8, cols), f32))
        inverse = mean_inverse(total, channels)
        x_ref[...] = moved_ref[...].astype(bf16)

        def emit(c, size, factor):
            part = pl.ds(c, size)
            moved_ref[part, :] = moved_ref[part, :] * factor

        network(x_ref, hid_ref, win_ref, wout_ref, inverse, emit, wait if n == 0 else None)

        for k in range(groups):
            outs[k][n] = encode(moved_ref[pl.ds(pl.multiple_of((k ^ device) * local, 8), local), :])


def last_kernel(split, groups, prows, where_ref, *refs):
    codes, out_ref = refs[:-1], refs[-1]
    local, cols = codes[0].shape[1:]
    rows = groups * prows
    space, device = where_ref[0], where_ref[1]
    share = 8 // prows
    some = 16 if local % 16 == 0 else 8

    for tile_at in range(0, groups, share):
        t = position_of(tile_at ^ device, space, groups) // share
        slots = [(device_of(t * share + i, space, groups) ^ device) - tile_at for i in range(share)]

        @pl.loop(0, local // some)
        def _(n):
            at = pl.multiple_of(n * some, some)
            for h in range(cols // 128):
                lanes = pl.ds(h * 128, 128)
                tile = []
                for i in range(share):
                    for j in range(prows):
                        for m, members in enumerate(split):
                            if j in members:
                                source = codes[m * groups + tile_at : m * groups + tile_at + share]
                                found = [code[members.index(j), pl.ds(at, some), lanes] for code in source]
                        value = found[0]
                        for slot in range(1, share):
                            value = jnp.where(slots[i] == slot, found[slot], value)
                        tile.append(decode(value))
                tile = jnp.swapaxes(jnp.stack(tile), 0, 1)
                for k in range(some):
                    start = pl.multiple_of((at + k) * rows + t * 8, 8)
                    out_ref[pl.ds(start, 8), lanes] = tile[k]


def exchange(array, axis, bit):
    count = lax.axis_size(axis)
    return lax.ppermute(array, axis, [(i, i ^ bit) for i in range(count)])


def gather(piece, stages):
    have, places = piece[None], [(0, 0)]
    arrays = [(have, places)]
    for n, (axis, bit) in enumerate(stages):
        got = []
        for have, places in arrays:
            flip = [(f ^ bit, s) if axis == "freq" else (f, s ^ bit) for f, s in places]
            got.append((exchange(have, axis, bit), flip))
        if n < len(stages) - 2:
            (have, places), (more, flip) = arrays[0], got[0]
            arrays = [(jnp.concatenate([have, more], axis=0), places + flip)]
        else:
            arrays = arrays + got
    return arrays


def bits_of(count):
    return [1 << n for n in reversed(range(count.bit_length() - 1))]


def split3(value):
    high = lax.reduce_precision(value, 8, 7)
    rest = value - high
    middle = lax.reduce_precision(rest, 8, 7)
    return [part.astype(bf16) for part in (high, middle, rest - middle)]


def body(spectrum, land_sea, courant, refract, depth_dx, depth_dy, w_in, w_out):
    groups, spaces = lax.axis_size("freq"), lax.axis_size("space")
    space, freq = lax.axis_index("space"), lax.axis_index("freq")
    freqs, dirs, rows, cols = spectrum.shape
    local = freqs * dirs
    channels = local * groups
    prows = rows // groups
    hidden_local = w_in.shape[1]
    hidden = hidden_local * groups

    last = spectrum[:, :, rows - 1, :].reshape(local, cols)
    first = spectrum[:, :, 0, :].reshape(local, cols)
    up = [(i, i + 1) for i in range(spaces - 1)]
    low = lax.ppermute(last, "space", up)
    high = lax.ppermute(first, "space", [(b, a) for a, b in up])

    hpart, cpart = hidden_local // spaces, channels // spaces
    win_piece = lax.dynamic_slice_in_dim(w_in, space * hpart, hpart, 1).T
    numbers = jnp.stack(split3(courant) + split3(refract))
    numbers = jnp.pad(numbers, ((0, 2), (0, channels - freqs)))
    win_piece = jnp.concatenate([win_piece, numbers], axis=0)
    wout_piece = lax.dynamic_slice_in_dim(w_out, space * cpart, cpart, 1).T
    along_freq = [("freq", bit) for bit in bits_of(groups)]
    along_space = [("space", bit) for bit in bits_of(spaces)]
    win_arrays = gather(win_piece, along_freq + along_space)
    wout_arrays = gather(wout_piece, along_freq[:-1] + along_space[:1] + along_freq[-1:] + along_space[1:])
    plan, parts = [], []
    for kind, arrays, size in ((0, win_arrays, hpart), (1, wout_arrays, cpart)):
        for have, places in arrays:
            plan.append((kind, places, size, hidden_local))
            parts.append(have)
    have, places = win_arrays[0]
    found = {f: n for n, (f, s) in reversed(list(enumerate(places)))}
    raw = have[:, hpart : hpart + 6, 0:freqs].astype(f32)
    raw = raw.reshape(len(places), 2, 3, freqs).sum(axis=2)
    numbers = jnp.concatenate([raw[found[f]] for f in range(groups)], axis=1)
    copies = sum(len(places) for _, places, _, _ in plan)

    angles = (jnp.arange(DIRS, dtype=f32) + 0.5) * (2.0 * math.pi / DIRS)
    angles = jnp.stack([jnp.cos(angles), jnp.sin(angles)])
    angles = jnp.broadcast_to(jnp.tile(angles, (1, 2))[:, :, None], (2, BLOCK, 128))
    place = jnp.stack([space, freq]).astype(i32)

    any_spec = pl.BlockSpec(memory_space=pl.ANY)
    vmem = pl.BlockSpec(memory_space=pltpu.VMEM)
    smem = pl.BlockSpec(memory_space=pltpu.SMEM)
    params = pltpu.CompilerParams(vmem_limit_bytes=60 * 1024 * 1024)
    net_scratch = [
        pltpu.VMEM((channels, cols), bf16),
        pltpu.VMEM((hidden, cols), bf16),
        pltpu.VMEM((hidden, channels), bf16),
        pltpu.VMEM((channels, hidden), bf16),
        pltpu.SemaphoreType.DMA((copies,)),
    ]

    outer = sorted({0, prows - 1})
    inner = [j for j in range(prows) if j not in outer]
    split = [outer] + ([inner] if inner else [])

    def code_shapes(own):
        return [jax.ShapeDtypeStruct((len(own), local, cols), i16)] * groups

    order = sorted(range(1, groups), key=lambda k: -k)

    def transpose(parts):
        arrived = list(parts)
        for k in order:
            arrived[k] = exchange(parts[k], "freq", k)
        return arrived

    flat = spectrum.reshape(local * rows, cols)
    sent = pl.pallas_call(
        lambda *refs: first_kernel(split, groups, prows, *refs),
        in_specs=[smem, smem] + [vmem] * 6,
        out_specs=[vmem] * (len(split) * groups),
        out_shape=[shape for own in split for shape in code_shapes(own)],
        scratch_shapes=[pltpu.VMEM((local, rows, cols), f32)] * 2,
        compiler_params=params,
        name="first",
    )(place, jnp.stack([courant, refract]), flat, low, high, depth_dx, depth_dy, land_sea)
    arrived = [transpose(sent[n * groups : (n + 1) * groups]) for n in range(len(split))]

    fields = []
    for own, codes in zip(split, arrived):
        edges = own is outer
        edge_shape = [jax.ShapeDtypeStruct((channels, cols), i16)] * (2 * edges)
        made = pl.pallas_call(
            lambda *refs, own=own, edges=edges: step_one_kernel(own, groups, plan, edges, *refs),
            in_specs=[smem] + [vmem] * groups + [any_spec] * len(plan),
            out_specs=[vmem] * (1 + len(edge_shape)),
            out_shape=[jax.ShapeDtypeStruct((len(own), channels, cols), f32)] + edge_shape,
            scratch_shapes=net_scratch,
            compiler_params=params,
            name="step_one",
        )(place, *codes, *parts)
        fields.append(made[0])
        if edges:
            edge = made[1:]

    chain = []
    for n in range(spaces * groups):
        s, p = divmod(n, groups)
        chain.append(s * groups + device_of(p, s, groups))
    chain = list(zip(chain[:-1], chain[1:]))
    low = lax.ppermute(edge[1], ("space", "freq"), chain)
    high = lax.ppermute(edge[0], ("space", "freq"), [(b, a) for a, b in chain])

    arrived = [None] * len(split)
    for own in reversed(split):
        halo = own is outer
        sent = pl.pallas_call(
            lambda *refs, own=own, halo=halo: step_two_kernel(own, split, groups, prows, plan, halo, *refs),
            in_specs=[smem, smem] + [vmem] * (4 + len(split) + 2 * halo) + [any_spec] * len(plan),
            out_specs=[vmem] * groups,
            out_shape=code_shapes(own),
            scratch_shapes=[
                pltpu.VMEM((2, channels, cols) if halo else (1, 8, 128), f32),
                pltpu.VMEM((channels, cols), f32),
                pltpu.VMEM((NCOEF, channels, 128), f32),
            ]
            + net_scratch,
            compiler_params=params,
            name="step_two",
        )(place, numbers, angles, depth_dx, depth_dy, land_sea, *fields, *((low, high) if halo else ()), *parts)
        arrived[split.index(own)] = transpose(sent)

    out = pl.pallas_call(
        lambda *refs: last_kernel(split, groups, prows, *refs),
        in_specs=[smem] + [vmem] * (len(split) * groups),
        out_specs=vmem,
        out_shape=jax.ShapeDtypeStruct((local * rows, cols), f32),
        compiler_params=params,
        name="last",
    )(place, *arrived[0], *(arrived[1] if len(split) > 1 else ()))
    return out.reshape(freqs, dirs, rows, cols)


def solution(mesh):
    placed = (
        P("freq", None, "space", None),
        P("space", None),
        P("freq"),
        P("freq"),
        P("space", None),
        P("space", None),
        P(None, "freq"),
        P("freq", None),
    )
    return jax.shard_map(
        body, mesh=mesh, in_specs=placed, out_specs=P("freq", None, "space", None), check_vma=False
    )
```

```python
import math

import jax
import jax.numpy as jnp
from jax import lax
from jax.experimental import pallas as pl
from jax.experimental.pallas import tpu as pltpu
from jax.sharding import PartitionSpec as P


DIRS = 36
STEP_SCALE = 0.5
EPSILON = 1e-06
ROOT_MAX = 2.9
ENCODE = 32767.0 / ROOT_MAX
DECODE = ROOT_MAX / 32767.0
NCOEF = 7
BLOCK = 2 * DIRS
f32, bf16, i16, i32 = jnp.float32, jnp.bfloat16, jnp.int16, jnp.int32


def encode(value):
    return (jnp.sqrt(value) * ENCODE + 0.5).astype(i32).astype(i16)


def decode(code):
    root = code.astype(i32).astype(f32) * DECODE
    return root * root


def device_of(position, space, groups):
    flipped = position + (space & 1) * (groups - 1 - 2 * position)
    return flipped ^ ((flipped >> 1) & 1) if groups % 4 == 0 else flipped


def position_of(device, space, groups):
    flipped = device ^ ((device >> 1) & 1) if groups % 4 == 0 else device
    return flipped + (space & 1) * (groups - 1 - 2 * flipped)


def spread(numbers_ref, row, angle_ref, wide_ref, at):
    cosine, sine = angle_ref[0], angle_ref[1]
    second = lax.broadcasted_iota(i32, (BLOCK, 128), 0) >= DIRS
    courant = jnp.where(second, numbers_ref[0, row + 1], numbers_ref[0, row])
    refract = jnp.where(second, numbers_ref[1, row + 1], numbers_ref[1, row])
    sx, sy = courant * cosine, courant * sine
    values = [
        1.0 - jnp.abs(sx) - jnp.abs(sy),
        jnp.maximum(sx, 0.0),
        jnp.maximum(-sx, 0.0),
        jnp.maximum(sy, 0.0),
        jnp.maximum(-sy, 0.0),
        refract * sine,
        refract * cosine,
    ]
    for k, value in enumerate(values):
        wide_ref[k, pl.ds(at, BLOCK), :] = value


def transport(center, above, below, coefs, dx, dy, sea):
    rows, cols = center.shape
    lane = lax.broadcasted_iota(i32, (rows, cols), 1)
    west = jnp.where(lane == 0, 0.0, pltpu.roll(center, 1, 1))
    east = jnp.where(lane == cols - 1, 0.0, pltpu.roll(center, cols - 1, 1))
    keep, pos_x, neg_x, pos_y, neg_y, turn_x, turn_y = coefs
    shifted = center * keep + pos_x * above + neg_x * below + pos_y * west + neg_y * east
    turning = (turn_x * dx - turn_y * dy) * shifted
    forward = jnp.maximum(turning, 0.0)
    backward = forward - turning
    first = lax.broadcasted_iota(i32, (8, cols), 0)
    moved = pltpu.roll(forward, 1, 0)
    moved = jnp.concatenate(
        [
            jnp.where(first == 0, forward[DIRS - 1 : DIRS], moved[0:8]),
            moved[8:32],
            jnp.where(first == DIRS % 8, forward[2 * DIRS - 1 : 2 * DIRS], moved[32:40]),
            moved[40:72],
        ],
        axis=0,
    )
    other = pltpu.roll(backward, rows - 1, 0)
    other = jnp.concatenate(
        [
            other[0:32],
            jnp.where(first == (DIRS - 1) % 8, backward[0:1], other[32:40]),
            other[40:64],
            jnp.where(first == 7, backward[DIRS : DIRS + 1], other[64:72]),
        ],
        axis=0,
    )
    return (shifted - forward - backward + moved + other) * sea


def wide(ref, k, rows, cols):
    part = ref[k, rows, :]
    return jnp.concatenate([part] * (cols // 128), axis=1)


def first_kernel(split, groups, prows, where_ref, numbers_ref, spec_ref, low_ref, high_ref, dx_ref, dy_ref, sea_ref, *refs):
    outs, (shifted_ref, turning_ref) = refs[: len(split) * groups], refs[len(split) * groups :]
    channels, cols = low_ref.shape
    rows = groups * prows
    space, device = where_ref[0], where_ref[1]
    line = lax.broadcasted_iota(i32, (rows, cols), 0)
    lane = lax.broadcasted_iota(i32, (rows, cols), 1)
    angles = [(d + 0.5) * (2.0 * math.pi / DIRS) for d in range(DIRS)]

    @pl.loop(0, channels // DIRS)
    def _(f):
        courant, refract = numbers_ref[0, f], numbers_ref[1, f]
        dx, dy = dx_ref[...] * refract, dy_ref[...] * refract
        for d in range(DIRS):
            c = f * DIRS + d
            cosine, sine = math.cos(angles[d]), math.sin(angles[d])
            center = spec_ref[pl.ds(pl.multiple_of(c * rows, 8), rows), :]
            if cosine > 0:
                beside = jnp.where(line == 0, low_ref[pl.ds(c, 1), :], pltpu.roll(center, 1, 0))
            else:
                beside = jnp.where(line == rows - 1, high_ref[pl.ds(c, 1), :], pltpu.roll(center, rows - 1, 0))
            if sine > 0:
                behind = jnp.where(lane == 0, 0.0, pltpu.roll(center, 1, 1))
            else:
                behind = jnp.where(lane == cols - 1, 0.0, pltpu.roll(center, cols - 1, 1))
            sx, sy = courant * abs(cosine), courant * abs(sine)
            shifted = center * (1.0 - sx - sy) + beside * sx + behind * sy
            shifted_ref[c] = shifted
            turning_ref[c] = (sine * dx - cosine * dy) * shifted

    some = 16 if channels % 16 == 0 else 8

    share = 8 // prows

    for tile_at in range(0, groups, share):
        t = position_of(tile_at ^ device, space, groups) // share
        tall = pl.ds(pl.multiple_of(t * 8, 8), 8)
        slots = [(device_of(t * share + i, space, groups) ^ device) - tile_at for i in range(share)]

        @pl.loop(0, channels // some)
        def _(n):
            at = pl.multiple_of(n * some, some)
            for h in range(cols // 128):
                lanes = pl.ds(h * 128, 128)
                sea = sea_ref[tall, lanes].astype(f32)
                tile = []
                for i in range(some):
                    c = at + i
                    d = c % DIRS
                    before = turning_ref[jnp.where(d == 0, c + DIRS - 1, c - 1), tall, lanes]
                    after = turning_ref[jnp.where(d == DIRS - 1, c - DIRS + 1, c + 1), tall, lanes]
                    value = shifted_ref[c, tall, lanes] - jnp.abs(turning_ref[c, tall, lanes])
                    tile.append((value + jnp.maximum(before, 0.0) - jnp.minimum(after, 0.0)) * sea)
                tile = encode(jnp.swapaxes(jnp.stack(tile), 0, 1))
                for slot in range(share):
                    for j in range(prows):
                        value = tile[j]
                        for i in range(1, share):
                            value = jnp.where(slots[i] == slot, tile[i * prows + j], value)
                        for m, members in enumerate(split):
                            if j in members:
                                out = outs[m * groups + tile_at + slot]
                                out[members.index(j), pl.ds(at, some), lanes] = value


def network(x_ref, hid_ref, win_ref, wout_ref, inverse, emit, wait):
    hidden, channels = win_ref.shape
    if wait:
        wait(0)
    mblock = min(512, hidden)
    for m in range(0, hidden, mblock):
        pre = jnp.dot(win_ref[m : m + mblock, :], x_ref[...], preferred_element_type=f32) * inverse
        act = 0.5 * pre * (1.0 + jnp.tanh(0.7978845608028654 * (pre + 0.044715 * pre * pre * pre)))
        hid_ref[m : m + mblock, :] = act.astype(bf16)
    if wait:
        wait(1)
    cblock = 4 * BLOCK
    for c in range(0, channels, cblock):
        source = jnp.dot(wout_ref[c : c + cblock, :], hid_ref[...], preferred_element_type=f32)
        emit(c, cblock, jnp.exp(STEP_SCALE * jnp.tanh(source)))


def load_weights(plan, space, parts, win_ref, wout_ref, sem):
    copies = []
    for part, (kind, places, size, width) in zip(parts, plan):
        for n, (f, s) in enumerate(places):
            if kind == 0:
                row = pl.multiple_of(f * width + (space ^ s) * size, 8)
                target = win_ref.at[pl.ds(row, size), :]
            else:
                row = pl.multiple_of((space ^ s) * size, 8)
                target = wout_ref.at[pl.ds(row, size), pl.ds(f * width, width)]
            copies.append(pltpu.make_async_copy(part.at[n, pl.ds(0, size), :], target, sem.at[len(copies)]))
    for copy in copies:
        copy.start()

    first = sum(len(places) for kind, places, _, _ in plan if kind == 0)

    def wait(kind):
        for copy in copies[:first] if kind == 0 else copies[first:]:
            copy.wait()

    return wait


def mean_inverse(total, channels):
    total = jnp.sum(total, axis=0, keepdims=True)
    return 1.0 / (total * (1.0 / channels) + EPSILON)


def step_one_kernel(own, groups, plan, edges, where_ref, *refs):
    codes, refs = refs[:groups], refs[groups:]
    parts, refs = refs[: len(plan)], refs[len(plan) :]
    field_ref, refs = refs[0], refs[1:]
    edge_refs, (x_ref, hid_ref, win_ref, wout_ref, sem) = refs[: 2 * edges], refs[2 * edges :]
    local = codes[0].shape[1]
    channels, cols = x_ref.shape
    wait = load_weights(plan, where_ref[0], parts, win_ref, wout_ref, sem)
    for n in range(len(own)):
        total = jnp.zeros((8, cols), f32)
        for k in range(groups):
            row = (k ^ where_ref[1]) * local
            for b in range(local // BLOCK):
                value = decode(codes[k][n, pl.ds(b * BLOCK, BLOCK), :])
                field_ref[n, pl.ds(pl.multiple_of(row + b * BLOCK, 8), BLOCK), :] = value
                total = total + jnp.sum(value.reshape(BLOCK // 8, 8, cols), axis=0)
        inverse = mean_inverse(total, channels)
        x_ref[...] = field_ref[n].astype(bf16)

        def emit(c, size, factor):
            part = pl.ds(c, size)
            field_ref[n, part, :] = field_ref[n, part, :] * factor

        network(x_ref, hid_ref, win_ref, wout_ref, inverse, emit, wait if n == 0 else None)
        if edges and n == 0:
            edge_refs[0][...] = encode(field_ref[n])
        if edges and n == len(own) - 1:
            edge_refs[1][...] = encode(field_ref[n])


def step_two_kernel(own, split, groups, prows, plan, with_halo, where_ref, numbers_ref, angle_ref, dx_ref, dy_ref, sea_ref, *refs):
    fields, refs = refs[: len(split)], refs[len(split) :]
    halos, refs = refs[: 2 * with_halo], refs[2 * with_halo :]
    parts, refs = refs[: len(plan)], refs[len(plan) :]
    outs, refs = refs[:groups], refs[groups:]
    halo_ref, moved_ref, coefw, x_ref, hid_ref, win_ref, wout_ref, sem = refs
    local = outs[0].shape[1]
    channels, cols = x_ref.shape
    space, device = where_ref[0], where_ref[1]
    wait = load_weights(plan, space, parts, win_ref, wout_ref, sem)
    for n, halo in enumerate(halos):
        halo_ref[n] = decode(halo[...])

    @pl.loop(0, groups)
    def _(q):
        row = (q ^ device) * (local // DIRS)
        for b in range(local // BLOCK):
            at = pl.multiple_of(q * local + b * BLOCK, 8)
            spread(numbers_ref, row + 2 * b, angle_ref, coefw, at)

    def held(j):
        if j < 0:
            return halo_ref, 0
        if j >= prows:
            return halo_ref, 1
        for field, members in zip(fields, split):
            if j in members:
                return field, members.index(j)

    first_row = position_of(device, space, groups) * prows
    for n, j in enumerate(own):
        r = first_row + j
        dx, dy = dx_ref[pl.ds(r, 1), :], dy_ref[pl.ds(r, 1), :]
        sea = sea_ref[pl.ds(r, 1), :].astype(f32)
        (here, hn), (above, an), (below, bn) = held(j), held(j - 1), held(j + 1)

        def block(b, total):
            part = pl.ds(pl.multiple_of(b * BLOCK, 8), BLOCK)
            coefs = [wide(coefw, k, part, cols) for k in range(NCOEF)]
            moved = transport(here[hn, part, :], above[an, part, :], below[bn, part, :], coefs, dx, dy, sea)
            moved_ref[part, :] = moved
            return total + jnp.sum(moved.reshape(BLOCK // 8, 8, cols), axis=0)

        total = lax.fori_loop(0, channels // BLOCK, block, jnp.zeros((8, cols), f32))
        inverse = mean_inverse(total, channels)
        x_ref[...] = moved_ref[...].astype(bf16)

        def emit(c, size, factor):
            part = pl.ds(c, size)
            moved_ref[part, :] = moved_ref[part, :] * factor

        network(x_ref, hid_ref, win_ref, wout_ref, inverse, emit, wait if n == 0 else None)

        for k in range(groups):
            outs[k][n] = encode(moved_ref[pl.ds(pl.multiple_of((k ^ device) * local, 8), local), :])


def last_kernel(split, groups, prows, where_ref, *refs):
    codes, out_ref = refs[:-1], refs[-1]
    local, cols = codes[0].shape[1:]
    rows = groups * prows
    space, device = where_ref[0], where_ref[1]
    share = 8 // prows
    some = 16 if local % 16 == 0 else 8

    for tile_at in range(0, groups, share):
        t = position_of(tile_at ^ device, space, groups) // share
        slots = [(device_of(t * share + i, space, groups) ^ device) - tile_at for i in range(share)]

        @pl.loop(0, local // some)
        def _(n):
            at = pl.multiple_of(n * some, some)
            for h in range(cols // 128):
                lanes = pl.ds(h * 128, 128)
                tile = []
                for i in range(share):
                    for j in range(prows):
                        for m, members in enumerate(split):
                            if j in members:
                                source = codes[m * groups + tile_at : m * groups + tile_at + share]
                                found = [code[members.index(j), pl.ds(at, some), lanes] for code in source]
                        value = found[0]
                        for slot in range(1, share):
                            value = jnp.where(slots[i] == slot, found[slot], value)
                        tile.append(decode(value))
                tile = jnp.swapaxes(jnp.stack(tile), 0, 1)
                for k in range(some):
                    start = pl.multiple_of((at + k) * rows + t * 8, 8)
                    out_ref[pl.ds(start, 8), lanes] = tile[k]


def exchange(array, axis, bit):
    count = lax.axis_size(axis)
    return lax.ppermute(array, axis, [(i, i ^ bit) for i in range(count)])


def gather(piece, stages):
    have, places = piece[None], [(0, 0)]
    arrays = [(have, places)]
    for n, (axis, bit) in enumerate(stages):
        got = []
        for have, places in arrays:
            flip = [(f ^ bit, s) if axis == "freq" else (f, s ^ bit) for f, s in places]
            got.append((exchange(have, axis, bit), flip))
        if n < len(stages) - 2:
            (have, places), (more, flip) = arrays[0], got[0]
            arrays = [(jnp.concatenate([have, more], axis=0), places + flip)]
        else:
            arrays = arrays + got
    return arrays


def bits_of(count):
    return [1 << n for n in reversed(range(count.bit_length() - 1))]


def split3(value):
    high = lax.reduce_precision(value, 8, 7)
    rest = value - high
    middle = lax.reduce_precision(rest, 8, 7)
    return [part.astype(bf16) for part in (high, middle, rest - middle)]


def body(spectrum, land_sea, courant, refract, depth_dx, depth_dy, w_in, w_out):
    groups, spaces = lax.axis_size("freq"), lax.axis_size("space")
    space, freq = lax.axis_index("space"), lax.axis_index("freq")
    freqs, dirs, rows, cols = spectrum.shape
    local = freqs * dirs
    channels = local * groups
    prows = rows // groups
    hidden_local = w_in.shape[1]
    hidden = hidden_local * groups

    last = spectrum[:, :, rows - 1, :].reshape(local, cols)
    first = spectrum[:, :, 0, :].reshape(local, cols)
    up = [(i, i + 1) for i in range(spaces - 1)]
    low = lax.ppermute(last, "space", up)
    high = lax.ppermute(first, "space", [(b, a) for a, b in up])

    hpart, cpart = hidden_local // spaces, channels // spaces
    win_piece = lax.dynamic_slice_in_dim(w_in, space * hpart, hpart, 1).T
    numbers = jnp.stack(split3(courant) + split3(refract))
    numbers = jnp.pad(numbers, ((0, 2), (0, channels - freqs)))
    win_piece = jnp.concatenate([win_piece, numbers], axis=0)
    wout_piece = lax.dynamic_slice_in_dim(w_out, space * cpart, cpart, 1).T
    along_freq = [("freq", bit) for bit in bits_of(groups)]
    along_space = [("space", bit) for bit in bits_of(spaces)]
    win_arrays = gather(win_piece, along_freq + along_space)
    wout_arrays = gather(wout_piece, along_freq[:-1] + along_space[:1] + along_freq[-1:] + along_space[1:])
    plan, parts = [], []
    for kind, arrays, size in ((0, win_arrays, hpart), (1, wout_arrays, cpart)):
        for have, places in arrays:
            plan.append((kind, places, size, hidden_local))
            parts.append(have)
    have, places = win_arrays[0]
    found = {f: n for n, (f, s) in reversed(list(enumerate(places)))}
    raw = have[:, hpart : hpart + 6, 0:freqs].astype(f32)
    raw = raw.reshape(len(places), 2, 3, freqs).sum(axis=2)
    numbers = jnp.concatenate([raw[found[f]] for f in range(groups)], axis=1)
    copies = sum(len(places) for _, places, _, _ in plan)

    angles = (jnp.arange(DIRS, dtype=f32) + 0.5) * (2.0 * math.pi / DIRS)
    angles = jnp.stack([jnp.cos(angles), jnp.sin(angles)])
    angles = jnp.broadcast_to(jnp.tile(angles, (1, 2))[:, :, None], (2, BLOCK, 128))
    place = jnp.stack([space, freq]).astype(i32)

    any_spec = pl.BlockSpec(memory_space=pl.ANY)
    vmem = pl.BlockSpec(memory_space=pltpu.VMEM)
    smem = pl.BlockSpec(memory_space=pltpu.SMEM)
    params = pltpu.CompilerParams(vmem_limit_bytes=60 * 1024 * 1024)
    net_scratch = [
        pltpu.VMEM((channels, cols), bf16),
        pltpu.VMEM((hidden, cols), bf16),
        pltpu.VMEM((hidden, channels), bf16),
        pltpu.VMEM((channels, hidden), bf16),
        pltpu.SemaphoreType.DMA((copies,)),
    ]

    outer = sorted({0, prows - 1})
    inner = [j for j in range(prows) if j not in outer]
    split = [outer] + ([inner] if inner else [])

    def code_shapes(own):
        return [jax.ShapeDtypeStruct((len(own), local, cols), i16)] * groups

    order = sorted(range(1, groups), key=lambda k: -k)

    def transpose(parts):
        arrived = list(parts)
        for k in order:
            arrived[k] = exchange(parts[k], "freq", k)
        return arrived

    flat = spectrum.reshape(local * rows, cols)
    sent = pl.pallas_call(
        lambda *refs: first_kernel(split, groups, prows, *refs),
        in_specs=[smem, smem] + [vmem] * 6,
        out_specs=[vmem] * (len(split) * groups),
        out_shape=[shape for own in split for shape in code_shapes(own)],
        scratch_shapes=[pltpu.VMEM((local, rows, cols), f32)] * 2,
        compiler_params=params,
        name="kfirst",
    )(place, jnp.stack([courant, refract]), flat, low, high, depth_dx, depth_dy, land_sea)
    arrived = [transpose(sent[n * groups : (n + 1) * groups]) for n in range(len(split))]

    fields = []
    for own, codes in zip(split, arrived):
        edges = own is outer
        edge_shape = [jax.ShapeDtypeStruct((channels, cols), i16)] * (2 * edges)
        made = pl.pallas_call(
            lambda *refs, own=own, edges=edges: step_one_kernel(own, groups, plan, edges, *refs),
            in_specs=[smem] + [vmem] * groups + [any_spec] * len(plan),
            out_specs=[vmem] * (1 + len(edge_shape)),
            out_shape=[jax.ShapeDtypeStruct((len(own), channels, cols), f32)] + edge_shape,
            scratch_shapes=net_scratch,
            compiler_params=params,
        )(place, *codes, *parts)
        fields.append(made[0])
        if edges:
            edge = made[1:]

    chain = []
    for n in range(spaces * groups):
        s, p = divmod(n, groups)
        chain.append(s * groups + device_of(p, s, groups))
    chain = list(zip(chain[:-1], chain[1:]))
    low = lax.ppermute(edge[1], ("space", "freq"), chain)
    high = lax.ppermute(edge[0], ("space", "freq"), [(b, a) for a, b in chain])

    arrived = [None] * len(split)
    for own in reversed(split):
        halo = own is outer
        sent = pl.pallas_call(
            lambda *refs, own=own, halo=halo: step_two_kernel(own, split, groups, prows, plan, halo, *refs),
            in_specs=[smem, smem] + [vmem] * (4 + len(split) + 2 * halo) + [any_spec] * len(plan),
            out_specs=[vmem] * groups,
            out_shape=code_shapes(own),
            scratch_shapes=[
                pltpu.VMEM((2, channels, cols) if halo else (1, 8, 128), f32),
                pltpu.VMEM((channels, cols), f32),
                pltpu.VMEM((NCOEF, channels, 128), f32),
            ]
            + net_scratch,
            compiler_params=params,
        )(place, numbers, angles, depth_dx, depth_dy, land_sea, *fields, *((low, high) if halo else ()), *parts)
        arrived[split.index(own)] = transpose(sent)

    out = pl.pallas_call(
        lambda *refs: last_kernel(split, groups, prows, *refs),
        in_specs=[smem] + [vmem] * (len(split) * groups),
        out_specs=vmem,
        out_shape=jax.ShapeDtypeStruct((local * rows, cols), f32),
        compiler_params=params,
        name="klast",
    )(place, *arrived[0], *(arrived[1] if len(split) > 1 else ()))
    return out.reshape(freqs, dirs, rows, cols)


def solution(mesh):
    placed = (
        P("freq", None, "space", None),
        P("space", None),
        P("freq"),
        P("freq"),
        P("space", None),
        P("space", None),
        P(None, "freq"),
        P("freq", None),
    )

    return jax.shard_map(body, mesh=mesh, in_specs=placed, out_specs=P("freq", None, "space", None), check_vma=False)
```

```python
import math

import jax
import jax.numpy as jnp
from jax import lax
from jax.experimental import pallas as pl
from jax.experimental.pallas import tpu as pltpu
from jax.sharding import PartitionSpec as P


DIRS = 36
STEP_SCALE = 0.5
EPSILON = 1e-06
ROOT_MAX = 2.9
ENCODE = 32767.0 / ROOT_MAX
DECODE = ROOT_MAX / 32767.0
NCOEF = 5
BLOCK = 2 * DIRS
f32, bf16, i16, i32 = jnp.float32, jnp.bfloat16, jnp.int16, jnp.int32


def encode(value):
    return (jnp.sqrt(value) * ENCODE + 0.5).astype(i32).astype(i16)


def decode(code):
    root = code.astype(i32).astype(f32) * DECODE
    return root * root


def device_of(position, space, groups):
    flipped = position + (space & 1) * (groups - 1 - 2 * position)
    return flipped ^ ((flipped >> 1) & 1) if groups % 4 == 0 else flipped


def position_of(device, space, groups):
    flipped = device ^ ((device >> 1) & 1) if groups % 4 == 0 else device
    return flipped + (space & 1) * (groups - 1 - 2 * flipped)


def spread(numbers_ref, row, angle_ref, wide_ref, at):
    cosine, sine = angle_ref[0], angle_ref[1]
    second = lax.broadcasted_iota(i32, (BLOCK, 128), 0) >= DIRS
    courant = jnp.where(second, numbers_ref[0, row + 1], numbers_ref[0, row])
    refract = jnp.where(second, numbers_ref[1, row + 1], numbers_ref[1, row])
    sx, sy = courant * cosine, courant * sine
    sx, sy = jnp.abs(sx), jnp.abs(sy)
    values = [1.0 - sx - sy, sx, sy, refract * sine, refract * cosine]
    for k, value in enumerate(values):
        wide_ref[k, pl.ds(at, BLOCK), :] = value


def one_sided(positive, row, yes, no):
    if all(positive):
        return yes()
    if not any(positive):
        return no()
    change = next(n for n in range(8) if positive[n] != positive[0])
    first, second = (yes(), no()) if positive[0] else (no(), yes())
    return jnp.where(row < change, first, second)


def transport(at, here, above, below, coefw, dx, dy, sea, write):
    cols = dx.shape[1]
    row = lax.broadcasted_iota(i32, (8, cols), 0)
    lane = lax.broadcasted_iota(i32, (8, cols), 1)
    count = BLOCK // 8
    cosine = [math.cos((d + 0.5) * (2.0 * math.pi / DIRS)) > 0 for d in range(DIRS)] * 2
    sine = [math.sin((d + 0.5) * (2.0 * math.pi / DIRS)) > 0 for d in range(DIRS)] * 2
    part = [pl.ds(pl.multiple_of(at + g * 8, 8), 8) for g in range(count)]
    shifted, forward, backward = [], [], []
    for g in range(count):
        center = here(part[g])
        rows = slice(g * 8, g * 8 + 8)
        beside = one_sided(cosine[rows], row, lambda: above(part[g]), lambda: below(part[g]))
        behind = one_sided(
            sine[rows],
            row,
            lambda: jnp.where(lane == 0, 0.0, pltpu.roll(center, 1, 1)),
            lambda: jnp.where(lane == cols - 1, 0.0, pltpu.roll(center, cols - 1, 1)),
        )
        keep, sx, sy, turn_x, turn_y = (
            jnp.concatenate([coefw[k, part[g], :]] * (cols // 128), axis=1) for k in range(NCOEF)
        )
        value = center * keep + beside * sx + behind * sy
        turning = (turn_x * dx - turn_y * dy) * value
        forward.append(jnp.maximum(turning, 0.0))
        backward.append(forward[g] - turning)
        shifted.append(value - jnp.abs(turning))
    down = [pltpu.roll(value, 1, 0) for value in forward]
    up = [pltpu.roll(value, 7, 0) for value in backward]
    half = DIRS // 8
    for g in range(count):
        before = pltpu.roll(forward[half], 5, 0) if g == 0 else down[g - 1]
        after = pltpu.roll(backward[half], 3, 0) if g == count - 1 else up[g + 1]
        moved = jnp.where(row == 0, before, down[g])
        other = jnp.where(row == 7, after, up[g])
        if g == half:
            moved = jnp.where(row == DIRS % 8, pltpu.roll(forward[count - 1], 5, 0), moved)
            other = jnp.where(row == DIRS % 8 - 1, pltpu.roll(backward[0], 3, 0), other)
        write(part[g], (shifted[g] + moved + other) * sea)


def first_kernel(split, groups, prows, where_ref, numbers_ref, source_ref, low_ref, high_ref, dx_ref, dy_ref, sea_ref, *refs):
    outs, (spec_ref, shifted_ref, turning_ref, sem) = refs[: len(split) * groups], refs[len(split) * groups :]
    channels, cols = low_ref.shape
    rows = groups * prows
    space, device = where_ref[0], where_ref[1]
    line = lax.broadcasted_iota(i32, (rows, cols), 0)
    lane = lax.broadcasted_iota(i32, (rows, cols), 1)
    angles = [(d + 0.5) * (2.0 * math.pi / DIRS) for d in range(DIRS)]

    def copy(f):
        part = pl.ds(pl.multiple_of(f * (DIRS * rows), 8), DIRS * rows)
        return pltpu.make_async_copy(source_ref.at[part, :], spec_ref.at[part, :], sem.at[f])

    for f in range(channels // DIRS):
        copy(f).start()

    @pl.loop(0, channels // DIRS)
    def _(f):
        copy(f).wait()
        courant, refract = numbers_ref[0, f], numbers_ref[1, f]
        dx, dy = dx_ref[...] * refract, dy_ref[...] * refract
        for d in range(DIRS):
            c = f * DIRS + d
            cosine, sine = math.cos(angles[d]), math.sin(angles[d])
            center = spec_ref[pl.ds(pl.multiple_of(c * rows, 8), rows), :]
            if cosine > 0:
                beside = jnp.where(line == 0, low_ref[pl.ds(c, 1), :], pltpu.roll(center, 1, 0))
            else:
                beside = jnp.where(line == rows - 1, high_ref[pl.ds(c, 1), :], pltpu.roll(center, rows - 1, 0))
            if sine > 0:
                behind = jnp.where(lane == 0, 0.0, pltpu.roll(center, 1, 1))
            else:
                behind = jnp.where(lane == cols - 1, 0.0, pltpu.roll(center, cols - 1, 1))
            sx, sy = courant * abs(cosine), courant * abs(sine)
            shifted = center * (1.0 - sx - sy) + beside * sx + behind * sy
            shifted_ref[c] = shifted
            turning_ref[c] = (sine * dx - cosine * dy) * shifted

    some = 16 if channels % 16 == 0 else 8

    share = 8 // prows

    for tile_at in range(0, groups, share):
        t = position_of(tile_at ^ device, space, groups) // share
        tall = pl.ds(pl.multiple_of(t * 8, 8), 8)
        slots = [(device_of(t * share + i, space, groups) ^ device) - tile_at for i in range(share)]

        @pl.loop(0, channels // some)
        def _(n):
            at = pl.multiple_of(n * some, some)
            for h in range(cols // 128):
                lanes = pl.ds(h * 128, 128)
                sea = sea_ref[tall, lanes].astype(f32)
                tile = []
                for i in range(some):
                    c = at + i
                    d = c % DIRS
                    before = turning_ref[jnp.where(d == 0, c + DIRS - 1, c - 1), tall, lanes]
                    after = turning_ref[jnp.where(d == DIRS - 1, c - DIRS + 1, c + 1), tall, lanes]
                    value = shifted_ref[c, tall, lanes] - jnp.abs(turning_ref[c, tall, lanes])
                    tile.append((value + jnp.maximum(before, 0.0) - jnp.minimum(after, 0.0)) * sea)
                tile = encode(jnp.swapaxes(jnp.stack(tile), 0, 1))
                for slot in range(share):
                    for j in range(prows):
                        value = tile[j]
                        for i in range(1, share):
                            value = jnp.where(slots[i] == slot, tile[i * prows + j], value)
                        for m, members in enumerate(split):
                            if j in members:
                                out = outs[m * groups + tile_at + slot]
                                out[members.index(j), pl.ds(at, some), lanes] = value


class Net:
    def __init__(self, plan, groups, spaces, space, parts, scratch):
        self.x, self.hid, self.win, self.wout, self.sem = scratch
        self.groups, self.spaces = groups, spaces
        self.hidden, self.channels = self.win.shape
        self.hpart = self.hidden // (groups * spaces)
        self.cpart = self.channels // spaces
        self.pending = True
        pieces = [(kind, f, s, part.at[n]) for part, (kind, places) in zip(parts, plan) for n, (f, s) in enumerate(places)]
        for kind, f, s, piece in sorted(pieces, key=lambda item: item[:3]):
            self.copy(kind, f, space ^ s, piece).start()
        self.piece = [part.at[0] for part in (parts[0], parts[-1])]

    def copy(self, kind, f, s, piece):
        if kind == 0:
            size, unit = self.hpart, f * self.spaces + s
            target = self.win.at[pl.ds(pl.multiple_of(unit * size, 8), size), :]
        else:
            size, unit = self.cpart, s * self.groups + f
            width = self.hidden // self.groups
            target = self.wout.at[pl.ds(pl.multiple_of(s * size, 8), size), pl.ds(f * width, width)]
        return pltpu.make_async_copy(piece.at[pl.ds(0, size), :], target, self.sem.at[kind, unit])

    def run(self, inverse, emit):
        mblock, cblock = min(512, self.hidden), 4 * BLOCK
        for m in range(0, self.hidden, mblock):
            if self.pending and m == 0:
                for unit in range(self.groups * self.spaces):
                    self.copy(0, unit // self.spaces, unit % self.spaces, self.piece[0]).wait()
            pre = jnp.dot(self.win[m : m + mblock, :], self.x[...], preferred_element_type=f32) * inverse
            half = 0.5 * pre
            inside = pre * (0.7978845608028654 + (0.7978845608028654 * 0.044715) * (pre * pre))
            self.hid[m : m + mblock, :] = (half + half * jnp.tanh(inside)).astype(bf16)
        for c in range(0, self.channels, cblock):
            if self.pending and c == 0:
                for s in range(self.spaces):
                    for f in range(self.groups):
                        self.copy(1, f, s, self.piece[1]).wait()
            source = jnp.dot(self.wout[c : c + cblock, :], self.hid[...], preferred_element_type=f32)
            emit(pl.ds(c, cblock), jnp.exp(STEP_SCALE * jnp.tanh(source)))
        self.pending = False


def mean_inverse(total, channels):
    total = jnp.sum(total, axis=0, keepdims=True)
    return 1.0 / (total * (1.0 / channels) + EPSILON)


def step_one(own, codes, field_ref, device, net):
    local, cols = codes[0].shape[1:]
    for n in range(len(own)):
        total = jnp.zeros((8, cols), f32)
        for k in range(len(codes)):
            row = (k ^ device) * local
            for b in range(local // BLOCK):
                value = decode(codes[k][n, pl.ds(b * BLOCK, BLOCK), :])
                field_ref[n, pl.ds(pl.multiple_of(row + b * BLOCK, 8), BLOCK), :] = value
                total = total + jnp.sum(value.reshape(BLOCK // 8, 8, cols), axis=0)
        net.x[...] = field_ref[n].astype(bf16)

        def emit(part, factor):
            field_ref[n, part, :] = field_ref[n, part, :] * factor

        net.run(mean_inverse(total, net.channels), emit)


def step_two(own, held, outs, grid, coefw, moved_ref, first_row, device, net):
    numbers_ref, angle_ref, dx_ref, dy_ref, sea_ref = grid
    local, cols = outs[0].shape[1:]
    groups, channels = len(outs), net.channels

    @pl.loop(0, groups)
    def _(q):
        row = (q ^ device) * (local // DIRS)
        for b in range(local // BLOCK):
            at = pl.multiple_of(q * local + b * BLOCK, 8)
            spread(numbers_ref, row + 2 * b, angle_ref, coefw, at)

    for n, j in enumerate(own):
        r = first_row + j
        dx, dy = dx_ref[pl.ds(r, 1), :], dy_ref[pl.ds(r, 1), :]
        sea = sea_ref[pl.ds(r, 1), :].astype(f32)
        (here, hn), (above, an), (below, bn) = held(j), held(j - 1), held(j + 1)

        def block(b, total):
            sums = [total]

            def write(part, value):
                moved_ref[part, :] = value
                sums.append(sums[-1] + value)

            at = pl.multiple_of(b * BLOCK, 8)
            transport(
                at,
                lambda part: here[hn, part, :],
                lambda part: above[an, part, :],
                lambda part: below[bn, part, :],
                coefw,
                jnp.broadcast_to(dx, (8, cols)),
                jnp.broadcast_to(dy, (8, cols)),
                jnp.broadcast_to(sea, (8, cols)),
                write,
            )
            return sums[-1]

        total = lax.fori_loop(0, channels // BLOCK, block, jnp.zeros((8, cols), f32))
        net.x[...] = moved_ref[...].astype(bf16)

        def emit(part, factor):
            moved_ref[part, :] = moved_ref[part, :] * factor

        net.run(mean_inverse(total, channels), emit)
        for k in range(groups):
            outs[k][n] = encode(moved_ref[pl.ds(pl.multiple_of((k ^ device) * local, 8), local), :])


def take(refs, count):
    return list(refs[:count]), refs[count:]


def outer_one_kernel(split, sizes, plan, where_ref, numbers_ref, angle_ref, *refs):
    groups, spaces, _ = sizes
    codes, refs = take(refs, groups)
    parts, refs = take(refs, len(plan))
    (field_ref, *edges), refs = take(refs, 3)
    net = Net(plan, groups, spaces, where_ref[0], parts, refs)
    step_one(split[0], codes, field_ref, where_ref[1], net)
    for edge, n in zip(edges, (0, len(split[0]) - 1)):
        edge[...] = encode(field_ref[n])


def inner_kernel(split, sizes, plan, where_ref, *refs):
    groups, spaces, prows = sizes
    grid, refs = take(refs, 5)
    (outer_ref,), refs = take(refs, 1)
    codes, refs = take(refs, groups)
    parts, refs = take(refs, len(plan))
    (field_ref,), refs = take(refs, 1)
    outs, refs = take(refs, groups)
    (moved_ref, coefw), scratch = take(refs, 2)
    space, device = where_ref[0], where_ref[1]
    net = Net(plan, groups, spaces, space, parts, scratch)
    step_one(split[1], codes, field_ref, device, net)

    def held(j):
        return (outer_ref, split[0].index(j)) if j in split[0] else (field_ref, split[1].index(j))

    first_row = position_of(device, space, groups) * prows
    step_two(split[1], held, outs, grid, coefw, moved_ref, first_row, device, net)


def outer_two_kernel(split, sizes, plan, where_ref, *refs):
    groups, spaces, prows = sizes
    grid, refs = take(refs, 5)
    fields, refs = take(refs, len(split))
    halos, refs = take(refs, 2)
    parts, refs = take(refs, len(plan))
    outs, refs = take(refs, groups)
    (halo_ref, moved_ref, coefw), scratch = take(refs, 3)
    space, device = where_ref[0], where_ref[1]
    net = Net(plan, groups, spaces, space, parts, scratch)
    for n, halo in enumerate(halos):
        halo_ref[n] = decode(halo[...])

    def held(j):
        if j < 0 or j >= prows:
            return halo_ref, int(j >= prows)
        for field, members in zip(fields, split):
            if j in members:
                return field, members.index(j)

    first_row = position_of(device, space, groups) * prows
    step_two(split[0], held, outs, grid, coefw, moved_ref, first_row, device, net)


def last_kernel(split, groups, prows, where_ref, *refs):
    codes, out_ref = refs[:-1], refs[-1]
    local, cols = codes[0].shape[1:]
    rows = groups * prows
    space, device = where_ref[0], where_ref[1]
    share = 8 // prows
    some = 16 if local % 16 == 0 else 8

    for tile_at in range(0, groups, share):
        t = position_of(tile_at ^ device, space, groups) // share
        slots = [(device_of(t * share + i, space, groups) ^ device) - tile_at for i in range(share)]

        @pl.loop(0, local // some)
        def _(n):
            at = pl.multiple_of(n * some, some)
            for h in range(cols // 128):
                lanes = pl.ds(h * 128, 128)
                tile = []
                for i in range(share):
                    for j in range(prows):
                        for m, members in enumerate(split):
                            if j in members:
                                source = codes[m * groups + tile_at : m * groups + tile_at + share]
                                found = [code[members.index(j), pl.ds(at, some), lanes] for code in source]
                        value = found[0]
                        for slot in range(1, share):
                            value = jnp.where(slots[i] == slot, found[slot], value)
                        tile.append(decode(value))
                tile = jnp.swapaxes(jnp.stack(tile), 0, 1)
                for k in range(some):
                    start = pl.multiple_of((at + k) * rows + t * 8, 8)
                    out_ref[pl.ds(start, 8), lanes] = tile[k]


def exchange(array, axis, bit):
    count = lax.axis_size(axis)
    return lax.ppermute(array, axis, [(i, i ^ bit) for i in range(count)])


def gather(piece, freq_bits, space_bits):
    have, places = piece[None], [(0, 0)]
    for bit in freq_bits[:-1]:
        have = jnp.concatenate([have, exchange(have, "freq", bit)], axis=0)
        places = places + [(f ^ bit, s) for f, s in places]
    arrays = [(have, places)]
    for bit in freq_bits[-1:]:
        arrays.append((exchange(have, "freq", bit), [(f ^ bit, s) for f, s in places]))
    for n, bit in enumerate(space_bits):
        got = []
        for have, places in arrays:
            flip = [(f, s ^ bit) for f, s in places]
            got.append((exchange(have, "space", bit), flip))
        if n == 0 or n == len(space_bits) - 1:
            arrays = arrays + got
        else:
            arrays = [
                (jnp.concatenate([a, b], axis=0), p + q) for (a, p), (b, q) in zip(arrays, got)
            ]
    return arrays


def bits_of(count):
    return [1 << n for n in reversed(range(count.bit_length() - 1))]


def split3(value):
    high = lax.reduce_precision(value, 8, 7)
    rest = value - high
    middle = lax.reduce_precision(rest, 8, 7)
    return [part.astype(bf16) for part in (high, middle, rest - middle)]


def body(spectrum, land_sea, courant, refract, depth_dx, depth_dy, w_in, w_out):
    groups, spaces = lax.axis_size("freq"), lax.axis_size("space")
    space, freq = lax.axis_index("space"), lax.axis_index("freq")
    freqs, dirs, rows, cols = spectrum.shape
    local = freqs * dirs
    channels = local * groups
    prows = rows // groups
    hidden_local = w_in.shape[1]
    hidden = hidden_local * groups

    last = spectrum[:, :, rows - 1, :].reshape(local, cols)
    first = spectrum[:, :, 0, :].reshape(local, cols)
    up = [(i, i + 1) for i in range(spaces - 1)]
    low = lax.ppermute(last, "space", up)
    high = lax.ppermute(first, "space", [(b, a) for a, b in up])

    hpart, cpart = hidden_local // spaces, channels // spaces
    win_piece = lax.dynamic_slice_in_dim(w_in, space * hpart, hpart, 1).T
    numbers = jnp.stack(split3(courant) + split3(refract))
    numbers = jnp.pad(numbers, ((0, 2), (0, channels - freqs)))
    win_piece = jnp.concatenate([win_piece, numbers], axis=0)
    wout_piece = lax.dynamic_slice_in_dim(w_out, space * cpart, cpart, 1).T
    win_arrays = gather(win_piece, bits_of(groups), bits_of(spaces))
    wout_arrays = gather(wout_piece, bits_of(groups), bits_of(spaces))
    plan, parts = [], []
    for kind, arrays in ((0, win_arrays), (1, wout_arrays)):
        for have, places in arrays:
            plan.append((kind, places))
            parts.append(have)
    found = {}
    for have, places in win_arrays[:2]:
        raw = have[:, hpart : hpart + 6, 0:freqs].astype(f32)
        raw = raw.reshape(len(places), 2, 3, freqs).sum(axis=2)
        found.update({f: raw[n] for n, (f, s) in enumerate(places)})
    numbers = jnp.concatenate([found[f] for f in range(groups)], axis=1)

    angles = (jnp.arange(DIRS, dtype=f32) + 0.5) * (2.0 * math.pi / DIRS)
    angles = jnp.stack([jnp.cos(angles), jnp.sin(angles)])
    angles = jnp.broadcast_to(jnp.tile(angles, (1, 2))[:, :, None], (2, BLOCK, 128))
    place = jnp.stack([space, freq]).astype(i32)

    any_spec = pl.BlockSpec(memory_space=pl.ANY)
    vmem = pl.BlockSpec(memory_space=pltpu.VMEM)
    smem = pl.BlockSpec(memory_space=pltpu.SMEM)
    params = pltpu.CompilerParams(vmem_limit_bytes=60 * 1024 * 1024)
    net_scratch = [
        pltpu.VMEM((channels, cols), bf16),
        pltpu.VMEM((hidden, cols), bf16),
        pltpu.VMEM((hidden, channels), bf16),
        pltpu.VMEM((channels, hidden), bf16),
        pltpu.SemaphoreType.DMA((2, groups * spaces)),
    ]

    outer = sorted({0, prows - 1})
    inner = [j for j in range(prows) if j not in outer]
    split = [outer] + ([inner] if inner else [])

    def code_shapes(own):
        return [jax.ShapeDtypeStruct((len(own), local, cols), i16)] * groups

    order = sorted(range(1, groups), key=lambda k: -k)

    def transpose(parts):
        arrived = list(parts)
        for k in order:
            arrived[k] = exchange(parts[k], "freq", k)
        return arrived

    flat = spectrum.reshape(local * rows, cols)
    sent = pl.pallas_call(
        lambda *refs: first_kernel(split, groups, prows, *refs),
        in_specs=[smem, smem, any_spec] + [vmem] * 5,
        out_specs=[vmem] * (len(split) * groups),
        out_shape=[shape for own in split for shape in code_shapes(own)],
        scratch_shapes=[pltpu.VMEM((local * rows, cols), f32)]
        + [pltpu.VMEM((local, rows, cols), f32)] * 2
        + [pltpu.SemaphoreType.DMA((freqs,))],
        compiler_params=params,
        name="kfirst",
    )(place, jnp.stack([courant, refract]), flat, low, high, depth_dx, depth_dy, land_sea)
    arrived = [transpose(sent[n * groups : (n + 1) * groups]) for n in range(len(split))]

    sizes = (groups, spaces, prows)
    step_scratch = [pltpu.VMEM((channels, cols), f32), pltpu.VMEM((NCOEF, channels, 128), f32)]

    def field_shape(own):
        return jax.ShapeDtypeStruct((len(own), channels, cols), f32)

    edge_shape = jax.ShapeDtypeStruct((channels, cols), i16)
    field, *edge = pl.pallas_call(
        lambda *refs: outer_one_kernel(split, sizes, plan, *refs),
        in_specs=[smem, smem, any_spec] + [vmem] * groups + [any_spec] * len(plan),
        out_specs=[vmem] * 3,
        out_shape=[field_shape(outer), edge_shape, edge_shape],
        scratch_shapes=net_scratch,
        compiler_params=params,
        name="kone0",
    )(place, numbers, angles, *arrived[0], *parts)
    fields = [field]

    chain = []
    for n in range(spaces * groups):
        s, p = divmod(n, groups)
        chain.append(s * groups + device_of(p, s, groups))
    chain = list(zip(chain[:-1], chain[1:]))
    low = lax.ppermute(edge[1], ("space", "freq"), chain)
    high = lax.ppermute(edge[0], ("space", "freq"), [(b, a) for a, b in chain])

    grid = (numbers, angles, depth_dx, depth_dy, land_sea)
    back = []
    if inner:
        field, *sent = pl.pallas_call(
            lambda *refs: inner_kernel(split, sizes, plan, *refs),
            in_specs=[smem, smem] + [vmem] * (5 + groups) + [any_spec] * len(plan),
            out_specs=[vmem] * (1 + groups),
            out_shape=[field_shape(inner)] + code_shapes(inner),
            scratch_shapes=step_scratch + net_scratch,
            compiler_params=params,
            name="kmid",
        )(place, *grid, fields[0], *arrived[1], *parts)
        fields.append(field)
        back = transpose(sent)
    sent = pl.pallas_call(
        lambda *refs: outer_two_kernel(split, sizes, plan, *refs),
        in_specs=[smem, smem] + [vmem] * (4 + len(split) + 2) + [any_spec] * len(plan),
        out_specs=[vmem] * groups,
        out_shape=code_shapes(outer),
        scratch_shapes=[pltpu.VMEM((2, channels, cols), f32)] + step_scratch + net_scratch,
        compiler_params=params,
        name="ktwo0",
    )(place, *grid, *fields, low, high, *parts)
    back = transpose(sent) + back

    out = pl.pallas_call(
        lambda *refs: last_kernel(split, groups, prows, *refs),
        in_specs=[smem] + [vmem] * (len(split) * groups),
        out_specs=vmem,
        out_shape=jax.ShapeDtypeStruct((local * rows, cols), f32),
        compiler_params=params,
        name="klast",
    )(place, *back)
    return out.reshape(freqs, dirs, rows, cols)


def solution(mesh):
    placed = (
        P("freq", None, "space", None),
        P("space", None),
        P("freq"),
        P("freq"),
        P("space", None),
        P("space", None),
        P(None, "freq"),
        P("freq", None),
    )

    return jax.shard_map(
        body, mesh=mesh, in_specs=placed, out_specs=P("freq", None, "space", None), check_vma=False
    )
```

```python
import math

import jax
import jax.numpy as jnp
from jax import lax
from jax.experimental import pallas as pl
from jax.experimental.pallas import tpu as pltpu
from jax.sharding import PartitionSpec as P


DIRS = 36
STEP_SCALE = 0.5
EPSILON = 1e-06
ROOT_MAX = 2.9
ENCODE = 32767.0 / ROOT_MAX
DECODE = ROOT_MAX / 32767.0
NCOEF = 5
BLOCK = 2 * DIRS
f32, bf16, i16, i32 = jnp.float32, jnp.bfloat16, jnp.int16, jnp.int32


def encode(value):
    return (jnp.sqrt(value) * ENCODE + 0.5).astype(i32).astype(i16)


def decode(code):
    root = code.astype(i32).astype(f32) * DECODE
    return root * root


def device_of(position, space, groups):
    flipped = position + (space & 1) * (groups - 1 - 2 * position)
    return flipped ^ ((flipped >> 1) & 1) if groups % 4 == 0 else flipped


def position_of(device, space, groups):
    flipped = device ^ ((device >> 1) & 1) if groups % 4 == 0 else device
    return flipped + (space & 1) * (groups - 1 - 2 * flipped)


def spread(numbers_ref, row, angle_ref, wide_ref, at):
    cosine, sine = angle_ref[0], angle_ref[1]
    second = lax.broadcasted_iota(i32, (BLOCK, 128), 0) >= DIRS
    courant = jnp.where(second, numbers_ref[0, row + 1], numbers_ref[0, row])
    refract = jnp.where(second, numbers_ref[1, row + 1], numbers_ref[1, row])
    sx, sy = courant * cosine, courant * sine
    sx, sy = jnp.abs(sx), jnp.abs(sy)
    values = [1.0 - sx - sy, sx, sy, refract * sine, refract * cosine]
    for k, value in enumerate(values):
        wide_ref[k, pl.ds(at, BLOCK), :] = value


def one_sided(positive, row, yes, no):
    if all(positive):
        return yes()
    if not any(positive):
        return no()
    change = next(n for n in range(8) if positive[n] != positive[0])
    first, second = (yes(), no()) if positive[0] else (no(), yes())
    return jnp.where(row < change, first, second)


def transport(at, here, above, below, coefw, dx, dy, sea, write):
    cols = dx.shape[1]
    row = lax.broadcasted_iota(i32, (8, cols), 0)
    lane = lax.broadcasted_iota(i32, (8, cols), 1)
    count = BLOCK // 8
    cosine = [math.cos((d + 0.5) * (2.0 * math.pi / DIRS)) > 0 for d in range(DIRS)] * 2
    sine = [math.sin((d + 0.5) * (2.0 * math.pi / DIRS)) > 0 for d in range(DIRS)] * 2
    part = [pl.ds(pl.multiple_of(at + g * 8, 8), 8) for g in range(count)]
    shifted, forward, backward = [], [], []
    for g in range(count):
        center = here(part[g])
        rows = slice(g * 8, g * 8 + 8)
        beside = one_sided(cosine[rows], row, lambda: above(part[g]), lambda: below(part[g]))
        behind = one_sided(
            sine[rows],
            row,
            lambda: jnp.where(lane == 0, 0.0, pltpu.roll(center, 1, 1)),
            lambda: jnp.where(lane == cols - 1, 0.0, pltpu.roll(center, cols - 1, 1)),
        )
        keep, sx, sy, turn_x, turn_y = (
            jnp.concatenate([coefw[k, part[g], :]] * (cols // 128), axis=1) for k in range(NCOEF)
        )
        value = center * keep + beside * sx + behind * sy
        turning = (turn_x * dx - turn_y * dy) * value
        forward.append(jnp.maximum(turning, 0.0))
        backward.append(forward[g] - turning)
        shifted.append(value - jnp.abs(turning))
    down = [pltpu.roll(value, 1, 0) for value in forward]
    up = [pltpu.roll(value, 7, 0) for value in backward]
    half = DIRS // 8
    for g in range(count):
        before = pltpu.roll(forward[half], 5, 0) if g == 0 else down[g - 1]
        after = pltpu.roll(backward[half], 3, 0) if g == count - 1 else up[g + 1]
        moved = jnp.where(row == 0, before, down[g])
        other = jnp.where(row == 7, after, up[g])
        if g == half:
            moved = jnp.where(row == DIRS % 8, pltpu.roll(forward[count - 1], 5, 0), moved)
            other = jnp.where(row == DIRS % 8 - 1, pltpu.roll(backward[0], 3, 0), other)
        write(part[g], (shifted[g] + moved + other) * sea)


def first_kernel(split, groups, prows, where_ref, numbers_ref, source_ref, low_ref, high_ref, dx_ref, dy_ref, sea_ref, *refs):
    outs, (spec_ref, turned_ref, sem) = refs[: len(split) * groups], refs[len(split) * groups :]
    channels, cols = low_ref.shape
    rows = groups * prows
    space, device = where_ref[0], where_ref[1]
    line = lax.broadcasted_iota(i32, (rows, cols), 0)
    lane = lax.broadcasted_iota(i32, (rows, cols), 1)
    angles = [(d + 0.5) * (2.0 * math.pi / DIRS) for d in range(DIRS)]

    def copy(f):
        part = pl.ds(pl.multiple_of(f * (DIRS * rows), 8), DIRS * rows)
        return pltpu.make_async_copy(source_ref.at[part, :], spec_ref.at[part, :], sem.at[f])

    for f in range(channels // DIRS):
        copy(f).start()

    @pl.loop(0, channels // DIRS)
    def _(f):
        copy(f).wait()
        courant, refract = numbers_ref[0, f], numbers_ref[1, f]
        dx, dy = dx_ref[...] * refract, dy_ref[...] * refract
        sea = sea_ref[...].astype(f32)

        def flow(d):
            c = f * DIRS + d
            cosine, sine = math.cos(angles[d]), math.sin(angles[d])
            center = spec_ref[pl.ds(pl.multiple_of(c * rows, 8), rows), :]
            if cosine > 0:
                beside = jnp.where(line == 0, low_ref[pl.ds(c, 1), :], pltpu.roll(center, 1, 0))
            else:
                beside = jnp.where(line == rows - 1, high_ref[pl.ds(c, 1), :], pltpu.roll(center, rows - 1, 0))
            if sine > 0:
                behind = jnp.where(lane == 0, 0.0, pltpu.roll(center, 1, 1))
            else:
                behind = jnp.where(lane == cols - 1, 0.0, pltpu.roll(center, cols - 1, 1))
            sx, sy = courant * abs(cosine), courant * abs(sine)
            shifted = center * (1.0 - sx - sy) + beside * sx + behind * sy
            return shifted, (sine * dx - cosine * dy) * shifted

        final = flow(DIRS - 1)
        here = flow(0)
        before, opening = final[1], here[1]
        for d in range(DIRS):
            if d + 1 < DIRS - 1:
                following = flow(d + 1)
            else:
                following = final if d + 1 == DIRS - 1 else (None, opening)
            value = here[0] - jnp.abs(here[1]) + jnp.maximum(before, 0.0) - jnp.minimum(following[1], 0.0)
            turned_ref[f * DIRS + d] = value * sea
            before, here = here[1], following

    some = 16 if channels % 16 == 0 else 8

    share = 8 // prows

    for tile_at in range(0, groups, share):
        t = position_of(tile_at ^ device, space, groups) // share
        tall = pl.ds(pl.multiple_of(t * 8, 8), 8)
        slots = [(device_of(t * share + i, space, groups) ^ device) - tile_at for i in range(share)]

        @pl.loop(0, channels // some)
        def _(n):
            at = pl.multiple_of(n * some, some)
            for h in range(cols // 128):
                lanes = pl.ds(h * 128, 128)
                tile = [turned_ref[at + i, tall, lanes] for i in range(some)]
                tile = encode(jnp.swapaxes(jnp.stack(tile), 0, 1))
                for slot in range(share):
                    for j in range(prows):
                        value = tile[j]
                        for i in range(1, share):
                            value = jnp.where(slots[i] == slot, tile[i * prows + j], value)
                        for m, members in enumerate(split):
                            if j in members:
                                out = outs[m * groups + tile_at + slot]
                                out[members.index(j), pl.ds(at, some), lanes] = value


class Net:
    def __init__(self, plan, groups, spaces, space, parts, scratch):
        self.x, self.hid, self.win, self.wout, self.sem = scratch
        self.groups, self.spaces = groups, spaces
        self.hidden, self.channels = self.win.shape
        self.hpart = self.hidden // (groups * spaces)
        self.cpart = self.channels // spaces
        self.pending = True
        pieces = [(kind, f, s, part.at[n]) for part, (kind, places) in zip(parts, plan) for n, (f, s) in enumerate(places)]
        for kind, f, s, piece in sorted(pieces, key=lambda item: item[:3]):
            self.copy(kind, f, space ^ s, piece).start()
        self.piece = [part.at[0] for part in (parts[0], parts[-1])]

    def copy(self, kind, f, s, piece):
        if kind == 0:
            size, unit = self.hpart, f * self.spaces + s
            target = self.win.at[pl.ds(pl.multiple_of(unit * size, 8), size), :]
        else:
            size, unit = self.cpart, s * self.groups + f
            width = self.hidden // self.groups
            target = self.wout.at[pl.ds(pl.multiple_of(s * size, 8), size), pl.ds(f * width, width)]
        return pltpu.make_async_copy(piece.at[pl.ds(0, size), :], target, self.sem.at[kind, unit])

    def run(self, inverse, emit):
        mblock, cblock = min(512, self.hidden), 4 * BLOCK
        for m in range(0, self.hidden, mblock):
            if self.pending and m == 0:
                for unit in range(self.groups * self.spaces):
                    self.copy(0, unit // self.spaces, unit % self.spaces, self.piece[0]).wait()
            pre = jnp.dot(self.win[m : m + mblock, :], self.x[...], preferred_element_type=f32) * inverse
            half = 0.5 * pre
            inside = pre * (0.7978845608028654 + (0.7978845608028654 * 0.044715) * (pre * pre))
            self.hid[m : m + mblock, :] = (half + half * jnp.tanh(inside)).astype(bf16)
        for c in range(0, self.channels, cblock):
            if self.pending and c == 0:
                for s in range(self.spaces):
                    for f in range(self.groups):
                        self.copy(1, f, s, self.piece[1]).wait()
            source = jnp.dot(self.wout[c : c + cblock, :], self.hid[...], preferred_element_type=f32)
            emit(pl.ds(c, cblock), jnp.exp(STEP_SCALE * jnp.tanh(source)))
        self.pending = False


def mean_inverse(total, channels):
    total = jnp.sum(total, axis=0, keepdims=True)
    return 1.0 / (total * (1.0 / channels) + EPSILON)


def step_one(own, codes, field_ref, device, net):
    local, cols = codes[0].shape[1:]
    for n in range(len(own)):
        total = jnp.zeros((8, cols), f32)
        for k in range(len(codes)):
            row = (k ^ device) * local
            for b in range(local // BLOCK):
                value = decode(codes[k][n, pl.ds(b * BLOCK, BLOCK), :])
                field_ref[n, pl.ds(pl.multiple_of(row + b * BLOCK, 8), BLOCK), :] = value
                total = total + jnp.sum(value.reshape(BLOCK // 8, 8, cols), axis=0)
        net.x[...] = field_ref[n].astype(bf16)

        def emit(part, factor):
            field_ref[n, part, :] = field_ref[n, part, :] * factor

        net.run(mean_inverse(total, net.channels), emit)


def step_two(own, held, outs, grid, coefw, moved_ref, first_row, device, net):
    numbers_ref, angle_ref, dx_ref, dy_ref, sea_ref = grid
    local, cols = outs[0].shape[1:]
    groups, channels = len(outs), net.channels

    @pl.loop(0, groups)
    def _(q):
        row = (q ^ device) * (local // DIRS)
        for b in range(local // BLOCK):
            at = pl.multiple_of(q * local + b * BLOCK, 8)
            spread(numbers_ref, row + 2 * b, angle_ref, coefw, at)

    for n, j in enumerate(own):
        r = first_row + j
        dx, dy = dx_ref[pl.ds(r, 1), :], dy_ref[pl.ds(r, 1), :]
        sea = sea_ref[pl.ds(r, 1), :].astype(f32)
        (here, hn), (above, an), (below, bn) = held(j), held(j - 1), held(j + 1)

        def block(b, total):
            sums = [total]

            def write(part, value):
                moved_ref[part, :] = value
                sums.append(sums[-1] + value)

            at = pl.multiple_of(b * BLOCK, 8)
            transport(
                at,
                lambda part: here[hn, part, :],
                lambda part: above[an, part, :],
                lambda part: below[bn, part, :],
                coefw,
                jnp.broadcast_to(dx, (8, cols)),
                jnp.broadcast_to(dy, (8, cols)),
                jnp.broadcast_to(sea, (8, cols)),
                write,
            )
            return sums[-1]

        total = lax.fori_loop(0, channels // BLOCK, block, jnp.zeros((8, cols), f32))
        net.x[...] = moved_ref[...].astype(bf16)

        def emit(part, factor):
            moved_ref[part, :] = moved_ref[part, :] * factor

        net.run(mean_inverse(total, channels), emit)
        for k in range(groups):
            outs[k][n] = encode(moved_ref[pl.ds(pl.multiple_of((k ^ device) * local, 8), local), :])


def take(refs, count):
    return list(refs[:count]), refs[count:]


def step_kernel(split, sizes, plan, where_ref, *refs):
    groups, spaces, prows = sizes
    grid, refs = take(refs, 5)
    codes, refs = take(refs, groups * len(split))
    parts, refs = take(refs, len(plan))
    fields, refs = take(refs, len(split))
    edges, refs = take(refs, 2)
    outs, refs = take(refs, groups * (len(split) - 1))
    (moved_ref, coefw), scratch = take(refs, 2)
    space, device = where_ref[0], where_ref[1]
    net = Net(plan, groups, spaces, space, parts, scratch)
    for m, members in enumerate(split):
        step_one(members, codes[m * groups : (m + 1) * groups], fields[m], device, net)
    for edge, n in zip(edges, (0, len(split[0]) - 1)):
        edge[...] = encode(fields[0][n])

    def held(j):
        return (fields[0], split[0].index(j)) if j in split[0] else (fields[1], split[1].index(j))

    if len(split) > 1:
        first_row = position_of(device, space, groups) * prows
        step_two(split[1], held, outs, grid, coefw, moved_ref, first_row, device, net)


def outer_two_kernel(split, sizes, plan, where_ref, *refs):
    groups, spaces, prows = sizes
    grid, refs = take(refs, 5)
    fields, refs = take(refs, len(split))
    halos, refs = take(refs, 2)
    parts, refs = take(refs, len(plan))
    outs, refs = take(refs, groups)
    (halo_ref, moved_ref, coefw), scratch = take(refs, 3)
    space, device = where_ref[0], where_ref[1]
    net = Net(plan, groups, spaces, space, parts, scratch)
    for n, halo in enumerate(halos):
        halo_ref[n] = decode(halo[...])

    def held(j):
        if j < 0 or j >= prows:
            return halo_ref, int(j >= prows)
        for field, members in zip(fields, split):
            if j in members:
                return field, members.index(j)

    first_row = position_of(device, space, groups) * prows
    step_two(split[0], held, outs, grid, coefw, moved_ref, first_row, device, net)


def last_kernel(split, groups, prows, where_ref, *refs):
    codes, out_ref = refs[:-1], refs[-1]
    local, cols = codes[0].shape[1:]
    rows = groups * prows
    space, device = where_ref[0], where_ref[1]
    share = 8 // prows
    some = 16 if local % 16 == 0 else 8

    for tile_at in range(0, groups, share):
        t = position_of(tile_at ^ device, space, groups) // share
        slots = [(device_of(t * share + i, space, groups) ^ device) - tile_at for i in range(share)]

        @pl.loop(0, local // some)
        def _(n):
            at = pl.multiple_of(n * some, some)
            for h in range(cols // 128):
                lanes = pl.ds(h * 128, 128)
                tile = []
                for i in range(share):
                    for j in range(prows):
                        for m, members in enumerate(split):
                            if j in members:
                                source = codes[m * groups + tile_at : m * groups + tile_at + share]
                                found = [code[members.index(j), pl.ds(at, some), lanes] for code in source]
                        value = found[0]
                        for slot in range(1, share):
                            value = jnp.where(slots[i] == slot, found[slot], value)
                        tile.append(decode(value))
                tile = jnp.swapaxes(jnp.stack(tile), 0, 1)
                for k in range(some):
                    start = pl.multiple_of((at + k) * rows + t * 8, 8)
                    out_ref[pl.ds(start, 8), lanes] = tile[k]


def exchange(array, axis, bit):
    count = lax.axis_size(axis)
    return lax.ppermute(array, axis, [(i, i ^ bit) for i in range(count)])


def gather(piece, freq_bits, space_bits):
    have, places = piece[None], [(0, 0)]
    for bit in freq_bits[:-1]:
        have = jnp.concatenate([have, exchange(have, "freq", bit)], axis=0)
        places = places + [(f ^ bit, s) for f, s in places]
    arrays = [(have, places)]
    for bit in freq_bits[-1:]:
        arrays.append((exchange(have, "freq", bit), [(f ^ bit, s) for f, s in places]))
    for n, bit in enumerate(space_bits):
        got = []
        for have, places in arrays:
            flip = [(f, s ^ bit) for f, s in places]
            got.append((exchange(have, "space", bit), flip))
        if n == 0 or n == len(space_bits) - 1:
            arrays = arrays + got
        else:
            arrays = [
                (jnp.concatenate([a, b], axis=0), p + q) for (a, p), (b, q) in zip(arrays, got)
            ]
    return arrays


def bits_of(count):
    return [1 << n for n in reversed(range(count.bit_length() - 1))]


def split3(value):
    high = lax.reduce_precision(value, 8, 7)
    rest = value - high
    middle = lax.reduce_precision(rest, 8, 7)
    return [part.astype(bf16) for part in (high, middle, rest - middle)]


def body(spectrum, land_sea, courant, refract, depth_dx, depth_dy, w_in, w_out):
    groups, spaces = lax.axis_size("freq"), lax.axis_size("space")
    space, freq = lax.axis_index("space"), lax.axis_index("freq")
    freqs, dirs, rows, cols = spectrum.shape
    local = freqs * dirs
    channels = local * groups
    prows = rows // groups
    hidden_local = w_in.shape[1]
    hidden = hidden_local * groups

    last = spectrum[:, :, rows - 1, :].reshape(local, cols)
    first = spectrum[:, :, 0, :].reshape(local, cols)
    up = [(i, i + 1) for i in range(spaces - 1)]
    low = lax.ppermute(last, "space", up)
    high = lax.ppermute(first, "space", [(b, a) for a, b in up])

    hpart, cpart = hidden_local // spaces, channels // spaces
    win_piece = lax.dynamic_slice_in_dim(w_in, space * hpart, hpart, 1).T
    numbers = jnp.stack(split3(courant) + split3(refract))
    numbers = jnp.pad(numbers, ((0, 2), (0, channels - freqs)))
    win_piece = jnp.concatenate([win_piece, numbers], axis=0)
    wout_piece = lax.dynamic_slice_in_dim(w_out, space * cpart, cpart, 1).T
    win_arrays = gather(win_piece, bits_of(groups), bits_of(spaces))
    wout_arrays = gather(wout_piece, bits_of(groups), bits_of(spaces))
    plan, parts = [], []
    for kind, arrays in ((0, win_arrays), (1, wout_arrays)):
        for have, places in arrays:
            plan.append((kind, places))
            parts.append(have)
    found = {}
    for have, places in win_arrays[:2]:
        raw = have[:, hpart : hpart + 6, 0:freqs].astype(f32)
        raw = raw.reshape(len(places), 2, 3, freqs).sum(axis=2)
        found.update({f: raw[n] for n, (f, s) in enumerate(places)})
    numbers = jnp.concatenate([found[f] for f in range(groups)], axis=1)

    angles = (jnp.arange(DIRS, dtype=f32) + 0.5) * (2.0 * math.pi / DIRS)
    angles = jnp.stack([jnp.cos(angles), jnp.sin(angles)])
    angles = jnp.broadcast_to(jnp.tile(angles, (1, 2))[:, :, None], (2, BLOCK, 128))
    place = jnp.stack([space, freq]).astype(i32)

    any_spec = pl.BlockSpec(memory_space=pl.ANY)
    vmem = pl.BlockSpec(memory_space=pltpu.VMEM)
    smem = pl.BlockSpec(memory_space=pltpu.SMEM)
    params = pltpu.CompilerParams(vmem_limit_bytes=60 * 1024 * 1024)
    net_scratch = [
        pltpu.VMEM((channels, cols), bf16),
        pltpu.VMEM((hidden, cols), bf16),
        pltpu.VMEM((hidden, channels), bf16),
        pltpu.VMEM((channels, hidden), bf16),
        pltpu.SemaphoreType.DMA((2, groups * spaces)),
    ]

    outer = sorted({0, prows - 1})
    inner = [j for j in range(prows) if j not in outer]
    split = [outer] + ([inner] if inner else [])

    def code_shapes(own):
        return [jax.ShapeDtypeStruct((len(own), local, cols), i16)] * groups

    order = sorted(range(1, groups), key=lambda k: -k)

    def transpose(parts):
        arrived = list(parts)
        for k in order:
            arrived[k] = exchange(parts[k], "freq", k)
        return arrived

    flat = spectrum.reshape(local * rows, cols)
    sent = pl.pallas_call(
        lambda *refs: first_kernel(split, groups, prows, *refs),
        in_specs=[smem, smem, any_spec] + [vmem] * 5,
        out_specs=[vmem] * (len(split) * groups),
        out_shape=[shape for own in split for shape in code_shapes(own)],
        scratch_shapes=[pltpu.VMEM((local * rows, cols), f32)]
        + [pltpu.VMEM((local, rows, cols), f32)]
        + [pltpu.SemaphoreType.DMA((freqs,))],
        compiler_params=params,
        name="kfirst",
    )(place, jnp.stack([courant, refract]), flat, low, high, depth_dx, depth_dy, land_sea)
    arrived = [transpose(sent[n * groups : (n + 1) * groups]) for n in range(len(split))]

    sizes = (groups, spaces, prows)
    step_scratch = [pltpu.VMEM((channels, cols), f32), pltpu.VMEM((NCOEF, channels, 128), f32)]

    def field_shape(own):
        return jax.ShapeDtypeStruct((len(own), channels, cols), f32)

    edge_shape = jax.ShapeDtypeStruct((channels, cols), i16)
    grid = (numbers, angles, depth_dx, depth_dy, land_sea)
    made = pl.pallas_call(
        lambda *refs: step_kernel(split, sizes, plan, *refs),
        in_specs=[smem, smem] + [vmem] * (4 + groups * len(split)) + [any_spec] * len(plan),
        out_specs=[vmem] * (len(split) + 2 + groups * len(split[1:])),
        out_shape=[field_shape(own) for own in split]
        + [edge_shape] * 2
        + [shape for own in split[1:] for shape in code_shapes(own)],
        scratch_shapes=step_scratch + net_scratch,
        compiler_params=params,
        name="kstep",
    )(place, *grid, *[code for codes in arrived for code in codes], *parts)
    fields, edge, sent = made[: len(split)], made[len(split) : len(split) + 2], made[len(split) + 2 :]

    chain = []
    for n in range(spaces * groups):
        s, p = divmod(n, groups)
        chain.append(s * groups + device_of(p, s, groups))
    chain = list(zip(chain[:-1], chain[1:]))
    low = lax.ppermute(edge[1], ("space", "freq"), chain)
    high = lax.ppermute(edge[0], ("space", "freq"), [(b, a) for a, b in chain])

    back = transpose(sent) if inner else []
    sent = pl.pallas_call(
        lambda *refs: outer_two_kernel(split, sizes, plan, *refs),
        in_specs=[smem, smem] + [vmem] * (4 + len(split) + 2) + [any_spec] * len(plan),
        out_specs=[vmem] * groups,
        out_shape=code_shapes(outer),
        scratch_shapes=[pltpu.VMEM((2, channels, cols), f32)] + step_scratch + net_scratch,
        compiler_params=params,
        name="ktwo0",
    )(place, *grid, *fields, low, high, *parts)
    back = transpose(sent) + back

    out = pl.pallas_call(
        lambda *refs: last_kernel(split, groups, prows, *refs),
        in_specs=[smem] + [vmem] * (len(split) * groups),
        out_specs=vmem,
        out_shape=jax.ShapeDtypeStruct((local * rows, cols), f32),
        compiler_params=params,
        name="klast",
    )(place, *back)
    return out.reshape(freqs, dirs, rows, cols)


def solution(mesh):
    placed = (
        P("freq", None, "space", None),
        P("space", None),
        P("freq"),
        P("freq"),
        P("space", None),
        P("space", None),
        P(None, "freq"),
        P("freq", None),
    )

    return jax.shard_map(
        body, mesh=mesh, in_specs=placed, out_specs=P("freq", None, "space", None), check_vma=False
    )
```

```python
import math

import jax
import jax.numpy as jnp
from jax import lax
from jax.experimental import pallas as pl
from jax.experimental.pallas import tpu as pltpu
from jax.sharding import PartitionSpec as P


DIRS = 36
STEP_SCALE = 0.5
EPSILON = 1e-06
ROOT_MAX = 2.9
ENCODE = 32767.0 / ROOT_MAX
DECODE = ROOT_MAX / 32767.0
NCOEF = 5
BLOCK = 2 * DIRS
f32, bf16, i16, i32 = jnp.float32, jnp.bfloat16, jnp.int16, jnp.int32


def encode(value):
    return (jnp.sqrt(value) * ENCODE + 0.5).astype(i32).astype(i16)


def decode(code):
    root = code.astype(i32).astype(f32) * DECODE
    return root * root


def device_of(position, space, groups):
    flipped = position + (space & 1) * (groups - 1 - 2 * position)
    return flipped ^ ((flipped >> 1) & 1) if groups % 4 == 0 else flipped


def position_of(device, space, groups):
    flipped = device ^ ((device >> 1) & 1) if groups % 4 == 0 else device
    return flipped + (space & 1) * (groups - 1 - 2 * flipped)


def spread(numbers_ref, row, angle_ref, wide_ref, at):
    cosine, sine = angle_ref[0], angle_ref[1]
    second = lax.broadcasted_iota(i32, (BLOCK, 128), 0) >= DIRS
    courant = jnp.where(second, numbers_ref[0, row + 1], numbers_ref[0, row])
    refract = jnp.where(second, numbers_ref[1, row + 1], numbers_ref[1, row])
    sx, sy = courant * cosine, courant * sine
    sx, sy = jnp.abs(sx), jnp.abs(sy)
    values = [1.0 - sx - sy, sx, sy, refract * sine, refract * cosine]
    for k, value in enumerate(values):
        wide_ref[k, pl.ds(at, BLOCK), :] = value


def one_sided(positive, row, yes, no):
    if all(positive):
        return yes()
    if not any(positive):
        return no()
    change = next(n for n in range(8) if positive[n] != positive[0])
    first, second = (yes(), no()) if positive[0] else (no(), yes())
    return jnp.where(row < change, first, second)


def transport(at, here, above, below, coefw, dx, dy, sea, write):
    cols = dx.shape[1]
    row = lax.broadcasted_iota(i32, (8, cols), 0)
    lane = lax.broadcasted_iota(i32, (8, cols), 1)
    count = BLOCK // 8
    cosine = [math.cos((d + 0.5) * (2.0 * math.pi / DIRS)) > 0 for d in range(DIRS)] * 2
    sine = [math.sin((d + 0.5) * (2.0 * math.pi / DIRS)) > 0 for d in range(DIRS)] * 2
    part = [pl.ds(pl.multiple_of(at + g * 8, 8), 8) for g in range(count)]
    shifted, forward, backward = [], [], []
    for g in range(count):
        center = here(part[g])
        rows = slice(g * 8, g * 8 + 8)
        beside = one_sided(cosine[rows], row, lambda: above(part[g]), lambda: below(part[g]))
        behind = one_sided(
            sine[rows],
            row,
            lambda: jnp.where(lane == 0, 0.0, pltpu.roll(center, 1, 1)),
            lambda: jnp.where(lane == cols - 1, 0.0, pltpu.roll(center, cols - 1, 1)),
        )
        keep, sx, sy, turn_x, turn_y = (
            jnp.concatenate([coefw[k, part[g], :]] * (cols // 128), axis=1) for k in range(NCOEF)
        )
        value = center * keep + beside * sx + behind * sy
        turning = (turn_x * dx - turn_y * dy) * value
        forward.append(jnp.maximum(turning, 0.0))
        backward.append(forward[g] - turning)
        shifted.append(value - jnp.abs(turning))
    down = [pltpu.roll(value, 1, 0) for value in forward]
    up = [pltpu.roll(value, 7, 0) for value in backward]
    half = DIRS // 8
    for g in range(count):
        before = pltpu.roll(forward[half], 5, 0) if g == 0 else down[g - 1]
        after = pltpu.roll(backward[half], 3, 0) if g == count - 1 else up[g + 1]
        moved = jnp.where(row == 0, before, down[g])
        other = jnp.where(row == 7, after, up[g])
        if g == half:
            moved = jnp.where(row == DIRS % 8, pltpu.roll(forward[count - 1], 5, 0), moved)
            other = jnp.where(row == DIRS % 8 - 1, pltpu.roll(backward[0], 3, 0), other)
        write(part[g], (shifted[g] + moved + other) * sea)


def first_kernel(split, groups, prows, where_ref, numbers_ref, source_ref, low_ref, high_ref, dx_ref, dy_ref, sea_ref, *refs):
    outs, (spec_ref, turned_ref, sem) = refs[: len(split) * groups], refs[len(split) * groups :]
    channels, cols = low_ref.shape
    rows = groups * prows
    space, device = where_ref[0], where_ref[1]
    line = lax.broadcasted_iota(i32, (rows, cols), 0)
    lane = lax.broadcasted_iota(i32, (rows, cols), 1)
    angles = [(d + 0.5) * (2.0 * math.pi / DIRS) for d in range(DIRS)]

    def copy(f):
        part = pl.ds(pl.multiple_of(f * (DIRS * rows), 8), DIRS * rows)
        return pltpu.make_async_copy(source_ref.at[part, :], spec_ref.at[part, :], sem.at[f])

    for f in range(channels // DIRS):
        copy(f).start()

    @pl.loop(0, channels // DIRS)
    def _(f):
        copy(f).wait()
        courant, refract = numbers_ref[0, f], numbers_ref[1, f]
        dx, dy = dx_ref[...] * refract, dy_ref[...] * refract
        sea = sea_ref[...].astype(f32)

        def flow(d):
            c = f * DIRS + d
            cosine, sine = math.cos(angles[d]), math.sin(angles[d])
            center = spec_ref[pl.ds(pl.multiple_of(c * rows, 8), rows), :]
            if cosine > 0:
                beside = jnp.where(line == 0, low_ref[pl.ds(c, 1), :], pltpu.roll(center, 1, 0))
            else:
                beside = jnp.where(line == rows - 1, high_ref[pl.ds(c, 1), :], pltpu.roll(center, rows - 1, 0))
            if sine > 0:
                behind = jnp.where(lane == 0, 0.0, pltpu.roll(center, 1, 1))
            else:
                behind = jnp.where(lane == cols - 1, 0.0, pltpu.roll(center, cols - 1, 1))
            sx, sy = courant * abs(cosine), courant * abs(sine)
            shifted = center * (1.0 - sx - sy) + beside * sx + behind * sy
            return shifted, (sine * dx - cosine * dy) * shifted

        final = flow(DIRS - 1)
        here = flow(0)
        before, opening = final[1], here[1]
        for d in range(DIRS):
            if d + 1 < DIRS - 1:
                following = flow(d + 1)
            else:
                following = final if d + 1 == DIRS - 1 else (None, opening)
            value = here[0] - jnp.abs(here[1]) + jnp.maximum(before, 0.0) - jnp.minimum(following[1], 0.0)
            turned_ref[f * DIRS + d] = value * sea
            before, here = here[1], following

    some = 16 if channels % 16 == 0 else 8

    share = 8 // prows

    for tile_at in range(0, groups, share):
        t = position_of(tile_at ^ device, space, groups) // share
        tall = pl.ds(pl.multiple_of(t * 8, 8), 8)
        slots = [(device_of(t * share + i, space, groups) ^ device) - tile_at for i in range(share)]

        @pl.loop(0, channels // some)
        def _(n):
            at = pl.multiple_of(n * some, some)
            for h in range(cols // 128):
                lanes = pl.ds(h * 128, 128)
                tile = [turned_ref[at + i, tall, lanes] for i in range(some)]
                tile = encode(jnp.swapaxes(jnp.stack(tile), 0, 1))
                for slot in range(share):
                    for j in range(prows):
                        value = tile[j]
                        for i in range(1, share):
                            value = jnp.where(slots[i] == slot, tile[i * prows + j], value)
                        for m, members in enumerate(split):
                            if j in members:
                                out = outs[m * groups + tile_at + slot]
                                out[members.index(j), pl.ds(at, some), lanes] = value


class Net:
    def __init__(self, plan, groups, spaces, space, parts, scratch):
        self.x, self.hid, self.win, self.wout, self.sem = scratch
        self.groups, self.spaces = groups, spaces
        self.hidden, self.channels = self.win.shape
        self.hpart = self.hidden // (groups * spaces)
        self.cpart = self.channels // spaces
        self.pending = True
        pieces = [(kind, f, s, part.at[n]) for part, (kind, places) in zip(parts, plan) for n, (f, s) in enumerate(places)]
        for kind, f, s, piece in sorted(pieces, key=lambda item: item[:3]):
            self.copy(kind, f, space ^ s, piece).start()
        self.piece = [part.at[0] for part in (parts[0], parts[-1])]

    def copy(self, kind, f, s, piece):
        if kind == 0:
            size, unit = self.hpart, f * self.spaces + s
            target = self.win.at[pl.ds(pl.multiple_of(unit * size, 8), size), :]
        else:
            size, unit = self.cpart, s * self.groups + f
            width = self.hidden // self.groups
            target = self.wout.at[pl.ds(pl.multiple_of(s * size, 8), size), pl.ds(f * width, width)]
        return pltpu.make_async_copy(piece.at[pl.ds(0, size), :], target, self.sem.at[kind, unit])

    def run(self, inverse, emit):
        mblock, cblock = min(512, self.hidden), 4 * BLOCK
        for m in range(0, self.hidden, mblock):
            if self.pending and m == 0:
                for unit in range(self.groups * self.spaces):
                    self.copy(0, unit // self.spaces, unit % self.spaces, self.piece[0]).wait()
            pre = jnp.dot(self.win[m : m + mblock, :], self.x[...], preferred_element_type=f32) * inverse
            half = 0.5 * pre
            inside = pre * (0.7978845608028654 + (0.7978845608028654 * 0.044715) * (pre * pre))
            self.hid[m : m + mblock, :] = (half + half * jnp.tanh(inside)).astype(bf16)
        for c in range(0, self.channels, cblock):
            if self.pending and c == 0:
                for s in range(self.spaces):
                    for f in range(self.groups):
                        self.copy(1, f, s, self.piece[1]).wait()
            source = jnp.dot(self.wout[c : c + cblock, :], self.hid[...], preferred_element_type=f32)
            emit(pl.ds(c, cblock), jnp.exp(STEP_SCALE * jnp.tanh(source)))
        self.pending = False


def mean_inverse(total, channels):
    total = jnp.sum(total, axis=0, keepdims=True)
    return 1.0 / (total * (1.0 / channels) + EPSILON)


def step_one(own, codes, field_ref, device, net):
    local, cols = codes[0].shape[1:]
    for n in range(len(own)):
        total = jnp.zeros((8, cols), f32)
        for k in range(len(codes)):
            row = (k ^ device) * local
            for b in range(local // BLOCK):
                value = decode(codes[k][n, pl.ds(b * BLOCK, BLOCK), :])
                field_ref[n, pl.ds(pl.multiple_of(row + b * BLOCK, 8), BLOCK), :] = value
                total = total + jnp.sum(value.reshape(BLOCK // 8, 8, cols), axis=0)
        net.x[...] = field_ref[n].astype(bf16)

        def emit(part, factor):
            field_ref[n, part, :] = field_ref[n, part, :] * factor

        net.run(mean_inverse(total, net.channels), emit)


def step_two(own, held, outs, grid, coefw, moved_ref, first_row, device, net):
    numbers_ref, angle_ref, dx_ref, dy_ref, sea_ref = grid
    local, cols = outs[0].shape[1:]
    groups, channels = len(outs), net.channels

    @pl.loop(0, groups)
    def _(q):
        row = (q ^ device) * (local // DIRS)
        for b in range(local // BLOCK):
            at = pl.multiple_of(q * local + b * BLOCK, 8)
            spread(numbers_ref, row + 2 * b, angle_ref, coefw, at)

    for n, j in enumerate(own):
        r = first_row + j
        dx, dy = dx_ref[pl.ds(r, 1), :], dy_ref[pl.ds(r, 1), :]
        sea = sea_ref[pl.ds(r, 1), :].astype(f32)
        (here, hn), (above, an), (below, bn) = held(j), held(j - 1), held(j + 1)

        def block(b, total):
            sums = [total]

            def write(part, value):
                moved_ref[part, :] = value
                sums.append(sums[-1] + value)

            at = pl.multiple_of(b * BLOCK, 8)
            transport(
                at,
                lambda part: here[hn, part, :],
                lambda part: above[an, part, :],
                lambda part: below[bn, part, :],
                coefw,
                jnp.broadcast_to(dx, (8, cols)),
                jnp.broadcast_to(dy, (8, cols)),
                jnp.broadcast_to(sea, (8, cols)),
                write,
            )
            return sums[-1]

        total = lax.fori_loop(0, channels // BLOCK, block, jnp.zeros((8, cols), f32))
        net.x[...] = moved_ref[...].astype(bf16)

        def emit(part, factor):
            moved_ref[part, :] = moved_ref[part, :] * factor

        net.run(mean_inverse(total, channels), emit)
        for k in range(groups):
            outs[k][n] = encode(moved_ref[pl.ds(pl.multiple_of((k ^ device) * local, 8), local), :])


def take(refs, count):
    return list(refs[:count]), refs[count:]


def outer_one_kernel(split, sizes, plan, where_ref, numbers_ref, angle_ref, *refs):
    groups, spaces, _ = sizes
    codes, refs = take(refs, groups)
    parts, refs = take(refs, len(plan))
    (field_ref, *edges), refs = take(refs, 3)
    net = Net(plan, groups, spaces, where_ref[0], parts, refs)
    step_one(split[0], codes, field_ref, where_ref[1], net)
    for edge, n in zip(edges, (0, len(split[0]) - 1)):
        edge[...] = encode(field_ref[n])


def inner_kernel(split, sizes, plan, where_ref, *refs):
    groups, spaces, prows = sizes
    grid, refs = take(refs, 5)
    (outer_ref,), refs = take(refs, 1)
    codes, refs = take(refs, groups)
    parts, refs = take(refs, len(plan))
    (field_ref,), refs = take(refs, 1)
    outs, refs = take(refs, groups)
    (moved_ref, coefw), scratch = take(refs, 2)
    space, device = where_ref[0], where_ref[1]
    net = Net(plan, groups, spaces, space, parts, scratch)
    step_one(split[1], codes, field_ref, device, net)

    def held(j):
        return (outer_ref, split[0].index(j)) if j in split[0] else (field_ref, split[1].index(j))

    first_row = position_of(device, space, groups) * prows
    step_two(split[1], held, outs, grid, coefw, moved_ref, first_row, device, net)


def outer_two_kernel(split, sizes, plan, where_ref, *refs):
    groups, spaces, prows = sizes
    grid, refs = take(refs, 5)
    fields, refs = take(refs, len(split))
    halos, refs = take(refs, 2)
    parts, refs = take(refs, len(plan))
    outs, refs = take(refs, groups)
    (halo_ref, moved_ref, coefw), scratch = take(refs, 3)
    space, device = where_ref[0], where_ref[1]
    net = Net(plan, groups, spaces, space, parts, scratch)
    for n, halo in enumerate(halos):
        halo_ref[n] = decode(halo[...])

    def held(j):
        if j < 0 or j >= prows:
            return halo_ref, int(j >= prows)
        for field, members in zip(fields, split):
            if j in members:
                return field, members.index(j)

    first_row = position_of(device, space, groups) * prows
    step_two(split[0], held, outs, grid, coefw, moved_ref, first_row, device, net)


def last_kernel(split, groups, prows, where_ref, *refs):
    codes, out_ref = refs[:-1], refs[-1]
    local, cols = codes[0].shape[1:]
    rows = groups * prows
    space, device = where_ref[0], where_ref[1]
    share = 8 // prows
    some = 16 if local % 16 == 0 else 8

    for tile_at in range(0, groups, share):
        t = position_of(tile_at ^ device, space, groups) // share
        slots = [(device_of(t * share + i, space, groups) ^ device) - tile_at for i in range(share)]

        @pl.loop(0, local // some)
        def _(n):
            at = pl.multiple_of(n * some, some)
            for h in range(cols // 128):
                lanes = pl.ds(h * 128, 128)
                tile = []
                for i in range(share):
                    for j in range(prows):
                        for m, members in enumerate(split):
                            if j in members:
                                source = codes[m * groups + tile_at : m * groups + tile_at + share]
                                found = [code[members.index(j), pl.ds(at, some), lanes] for code in source]
                        value = found[0]
                        for slot in range(1, share):
                            value = jnp.where(slots[i] == slot, found[slot], value)
                        tile.append(decode(value))
                tile = jnp.swapaxes(jnp.stack(tile), 0, 1)
                for k in range(some):
                    start = pl.multiple_of((at + k) * rows + t * 8, 8)
                    out_ref[pl.ds(start, 8), lanes] = tile[k]


def exchange(array, axis, bit):
    count = lax.axis_size(axis)
    return lax.ppermute(array, axis, [(i, i ^ bit) for i in range(count)])


def gather(piece, freq_bits, space_bits):
    have, places = piece[None], [(0, 0)]
    for bit in freq_bits[:-1]:
        have = jnp.concatenate([have, exchange(have, "freq", bit)], axis=0)
        places = places + [(f ^ bit, s) for f, s in places]
    arrays = [(have, places)]
    for bit in freq_bits[-1:]:
        arrays.append((exchange(have, "freq", bit), [(f ^ bit, s) for f, s in places]))
    for n, bit in enumerate(space_bits):
        got = []
        for have, places in arrays:
            flip = [(f, s ^ bit) for f, s in places]
            got.append((exchange(have, "space", bit), flip))
        if n == 0 or n == len(space_bits) - 1:
            arrays = arrays + got
        else:
            arrays = [
                (jnp.concatenate([a, b], axis=0), p + q) for (a, p), (b, q) in zip(arrays, got)
            ]
    return arrays


def bits_of(count):
    return [1 << n for n in reversed(range(count.bit_length() - 1))]


def split3(value):
    high = lax.reduce_precision(value, 8, 7)
    rest = value - high
    middle = lax.reduce_precision(rest, 8, 7)
    return [part.astype(bf16) for part in (high, middle, rest - middle)]


def body(spectrum, land_sea, courant, refract, depth_dx, depth_dy, w_in, w_out):
    groups, spaces = lax.axis_size("freq"), lax.axis_size("space")
    space, freq = lax.axis_index("space"), lax.axis_index("freq")
    freqs, dirs, rows, cols = spectrum.shape
    local = freqs * dirs
    channels = local * groups
    prows = rows // groups
    hidden_local = w_in.shape[1]
    hidden = hidden_local * groups

    last = spectrum[:, :, rows - 1, :].reshape(local, cols)
    first = spectrum[:, :, 0, :].reshape(local, cols)
    up = [(i, i + 1) for i in range(spaces - 1)]
    low = lax.ppermute(last, "space", up)
    high = lax.ppermute(first, "space", [(b, a) for a, b in up])

    hpart, cpart = hidden_local // spaces, channels // spaces
    win_piece = lax.dynamic_slice_in_dim(w_in, space * hpart, hpart, 1).T
    numbers = jnp.stack(split3(courant) + split3(refract))
    numbers = jnp.pad(numbers, ((0, 2), (0, channels - freqs)))
    win_piece = jnp.concatenate([win_piece, numbers], axis=0)
    wout_piece = lax.dynamic_slice_in_dim(w_out, space * cpart, cpart, 1).T
    win_arrays = gather(win_piece, bits_of(groups), bits_of(spaces))
    wout_arrays = gather(wout_piece, bits_of(groups), bits_of(spaces))
    plan, parts = [], []
    for kind, arrays in ((0, win_arrays), (1, wout_arrays)):
        for have, places in arrays:
            plan.append((kind, places))
            parts.append(have)
    found = {}
    for have, places in win_arrays[:2]:
        raw = have[:, hpart : hpart + 6, 0:freqs].astype(f32)
        raw = raw.reshape(len(places), 2, 3, freqs).sum(axis=2)
        found.update({f: raw[n] for n, (f, s) in enumerate(places)})
    numbers = jnp.concatenate([found[f] for f in range(groups)], axis=1)

    angles = (jnp.arange(DIRS, dtype=f32) + 0.5) * (2.0 * math.pi / DIRS)
    angles = jnp.stack([jnp.cos(angles), jnp.sin(angles)])
    angles = jnp.broadcast_to(jnp.tile(angles, (1, 2))[:, :, None], (2, BLOCK, 128))
    place = jnp.stack([space, freq]).astype(i32)

    any_spec = pl.BlockSpec(memory_space=pl.ANY)
    vmem = pl.BlockSpec(memory_space=pltpu.VMEM)
    smem = pl.BlockSpec(memory_space=pltpu.SMEM)
    params = pltpu.CompilerParams(vmem_limit_bytes=60 * 1024 * 1024)
    net_scratch = [
        pltpu.VMEM((channels, cols), bf16),
        pltpu.VMEM((hidden, cols), bf16),
        pltpu.VMEM((hidden, channels), bf16),
        pltpu.VMEM((channels, hidden), bf16),
        pltpu.SemaphoreType.DMA((2, groups * spaces)),
    ]

    outer = sorted({0, prows - 1})
    inner = [j for j in range(prows) if j not in outer]
    split = [outer] + ([inner] if inner else [])

    def code_shapes(own):
        return [jax.ShapeDtypeStruct((len(own), local, cols), i16)] * groups

    order = sorted(range(1, groups), key=lambda k: -k)

    def transpose(parts):
        arrived = list(parts)
        for k in order:
            arrived[k] = exchange(parts[k], "freq", k)
        return arrived

    flat = spectrum.reshape(local * rows, cols)
    sent = pl.pallas_call(
        lambda *refs: first_kernel(split, groups, prows, *refs),
        in_specs=[smem, smem, any_spec] + [vmem] * 5,
        out_specs=[vmem] * (len(split) * groups),
        out_shape=[shape for own in split for shape in code_shapes(own)],
        scratch_shapes=[pltpu.VMEM((local * rows, cols), f32)]
        + [pltpu.VMEM((local, rows, cols), f32)]
        + [pltpu.SemaphoreType.DMA((freqs,))],
        compiler_params=params,
        name="kfirst",
    )(place, jnp.stack([courant, refract]), flat, low, high, depth_dx, depth_dy, land_sea)
    arrived = [transpose(sent[n * groups : (n + 1) * groups]) for n in range(len(split))]

    sizes = (groups, spaces, prows)
    step_scratch = [pltpu.VMEM((channels, cols), f32), pltpu.VMEM((NCOEF, channels, 128), f32)]

    def field_shape(own):
        return jax.ShapeDtypeStruct((len(own), channels, cols), f32)

    edge_shape = jax.ShapeDtypeStruct((channels, cols), i16)
    field, *edge = pl.pallas_call(
        lambda *refs: outer_one_kernel(split, sizes, plan, *refs),
        in_specs=[smem, smem, any_spec] + [vmem] * groups + [any_spec] * len(plan),
        out_specs=[vmem] * 3,
        out_shape=[field_shape(outer), edge_shape, edge_shape],
        scratch_shapes=net_scratch,
        compiler_params=params,
        name="kone0",
    )(place, numbers, angles, *arrived[0], *parts)
    fields = [field]

    chain = []
    for n in range(spaces * groups):
        s, p = divmod(n, groups)
        chain.append(s * groups + device_of(p, s, groups))
    chain = list(zip(chain[:-1], chain[1:]))
    low = lax.ppermute(edge[1], ("space", "freq"), chain)
    high = lax.ppermute(edge[0], ("space", "freq"), [(b, a) for a, b in chain])

    grid = (numbers, angles, depth_dx, depth_dy, land_sea)
    back = []
    if inner:
        field, *sent = pl.pallas_call(
            lambda *refs: inner_kernel(split, sizes, plan, *refs),
            in_specs=[smem, smem] + [vmem] * (5 + groups) + [any_spec] * len(plan),
            out_specs=[vmem] * (1 + groups),
            out_shape=[field_shape(inner)] + code_shapes(inner),
            scratch_shapes=step_scratch + net_scratch,
            compiler_params=params,
            name="kmid",
        )(place, *grid, fields[0], *arrived[1], *parts)
        fields.append(field)
        back = transpose(sent)
    sent = pl.pallas_call(
        lambda *refs: outer_two_kernel(split, sizes, plan, *refs),
        in_specs=[smem, smem] + [vmem] * (4 + len(split) + 2) + [any_spec] * len(plan),
        out_specs=[vmem] * groups,
        out_shape=code_shapes(outer),
        scratch_shapes=[pltpu.VMEM((2, channels, cols), f32)] + step_scratch + net_scratch,
        compiler_params=params,
        name="ktwo0",
    )(place, *grid, *fields, low, high, *parts)
    back = transpose(sent) + back

    out = pl.pallas_call(
        lambda *refs: last_kernel(split, groups, prows, *refs),
        in_specs=[smem] + [vmem] * (len(split) * groups),
        out_specs=vmem,
        out_shape=jax.ShapeDtypeStruct((local * rows, cols), f32),
        compiler_params=params,
        name="klast",
    )(place, *back)
    return out.reshape(freqs, dirs, rows, cols)


def solution(mesh):
    placed = (
        P("freq", None, "space", None),
        P("space", None),
        P("freq"),
        P("freq"),
        P("space", None),
        P("space", None),
        P(None, "freq"),
        P("freq", None),
    )

    return jax.shard_map(
        body, mesh=mesh, in_specs=placed, out_specs=P("freq", None, "space", None), check_vma=False
    )
```

```python
import math

import jax
import jax.numpy as jnp
import numpy as np
from jax import lax
from jax.experimental import pallas as pl
from jax.experimental.pallas import tpu as pltpu
from jax.sharding import PartitionSpec as P


DIRS = 36
STEP_SCALE = 0.5
EPSILON = 1e-06
ROOT_MAX = 2.9
ENCODE = 32767.0 / ROOT_MAX
DECODE = ROOT_MAX / 32767.0
NCOEF = 5
BLOCK = 2 * DIRS
f32, bf16, i16, i32 = jnp.float32, jnp.bfloat16, jnp.int16, jnp.int32


def encode(value):
    return (jnp.sqrt(value) * ENCODE + 0.5).astype(i32).astype(i16)


def decode(code):
    root = code.astype(i32).astype(f32) * DECODE
    return root * root


def device_of(position, space, groups):
    flipped = position + (space & 1) * (groups - 1 - 2 * position)
    return flipped ^ ((flipped >> 1) & 1) if groups % 4 == 0 else flipped


def position_of(device, space, groups):
    flipped = device ^ ((device >> 1) & 1) if groups % 4 == 0 else device
    return flipped + (space & 1) * (groups - 1 - 2 * flipped)


def spread(numbers_ref, row, angle_ref, wide_ref, at):
    cosine, sine = angle_ref[0], angle_ref[1]
    second = lax.broadcasted_iota(i32, (BLOCK, 128), 0) >= DIRS
    courant = jnp.where(second, numbers_ref[0, row + 1], numbers_ref[0, row])
    refract = jnp.where(second, numbers_ref[1, row + 1], numbers_ref[1, row])
    sx, sy = courant * cosine, courant * sine
    sx, sy = jnp.abs(sx), jnp.abs(sy)
    values = [1.0 - sx - sy, sx, sy, refract * sine, refract * cosine]
    for k, value in enumerate(values):
        wide_ref[k, pl.ds(at, BLOCK), :] = value


def one_sided(positive, row, yes, no):
    if all(positive):
        return yes()
    if not any(positive):
        return no()
    change = next(n for n in range(8) if positive[n] != positive[0])
    first, second = (yes(), no()) if positive[0] else (no(), yes())
    return jnp.where(row < change, first, second)


def transport(at, here, above, below, coefw, dx, dy, sea, write):
    cols = dx.shape[1]
    row = lax.broadcasted_iota(i32, (8, cols), 0)
    lane = lax.broadcasted_iota(i32, (8, cols), 1)
    count = BLOCK // 8
    cosine = [math.cos((d + 0.5) * (2.0 * math.pi / DIRS)) > 0 for d in range(DIRS)] * 2
    sine = [math.sin((d + 0.5) * (2.0 * math.pi / DIRS)) > 0 for d in range(DIRS)] * 2
    part = [pl.ds(pl.multiple_of(at + g * 8, 8), 8) for g in range(count)]
    shifted, forward, backward = [], [], []
    for g in range(count):
        center = here(part[g])
        rows = slice(g * 8, g * 8 + 8)
        beside = one_sided(cosine[rows], row, lambda: above(part[g]), lambda: below(part[g]))
        behind = one_sided(
            sine[rows],
            row,
            lambda: jnp.where(lane == 0, 0.0, pltpu.roll(center, 1, 1)),
            lambda: jnp.where(lane == cols - 1, 0.0, pltpu.roll(center, cols - 1, 1)),
        )
        keep, sx, sy, turn_x, turn_y = (
            jnp.concatenate([coefw[k, part[g], :]] * (cols // 128), axis=1) for k in range(NCOEF)
        )
        value = center * keep + beside * sx + behind * sy
        turning = (turn_x * dx - turn_y * dy) * value
        forward.append(jnp.maximum(turning, 0.0))
        backward.append(forward[g] - turning)
        shifted.append(value - jnp.abs(turning))
    down = [pltpu.roll(value, 1, 0) for value in forward]
    up = [pltpu.roll(value, 7, 0) for value in backward]
    half = DIRS // 8
    for g in range(count):
        before = pltpu.roll(forward[half], 5, 0) if g == 0 else down[g - 1]
        after = pltpu.roll(backward[half], 3, 0) if g == count - 1 else up[g + 1]
        moved = jnp.where(row == 0, before, down[g])
        other = jnp.where(row == 7, after, up[g])
        if g == half:
            moved = jnp.where(row == DIRS % 8, pltpu.roll(forward[count - 1], 5, 0), moved)
            other = jnp.where(row == DIRS % 8 - 1, pltpu.roll(backward[0], 3, 0), other)
        write(part[g], (shifted[g] + moved + other) * sea)


def first_kernel(split, groups, prows, where_ref, numbers_ref, source_ref, low_ref, high_ref, dx_ref, dy_ref, sea_ref, *refs):
    outs, (spec_ref, turned_ref, sem) = refs[: len(split) * groups], refs[len(split) * groups :]
    channels, cols = low_ref.shape
    rows = groups * prows
    space, device = where_ref[0], where_ref[1]
    line = lax.broadcasted_iota(i32, (rows, cols), 0)
    lane = lax.broadcasted_iota(i32, (rows, cols), 1)
    angles = [(d + 0.5) * (2.0 * math.pi / DIRS) for d in range(DIRS)]

    def copy(f):
        part = pl.ds(pl.multiple_of(f * (DIRS * rows), 8), DIRS * rows)
        return pltpu.make_async_copy(source_ref.at[part, :], spec_ref.at[part, :], sem.at[f])

    for f in range(channels // DIRS):
        copy(f).start()

    @pl.loop(0, channels // DIRS)
    def _(f):
        copy(f).wait()
        courant, refract = numbers_ref[0, f], numbers_ref[1, f]
        dx, dy = dx_ref[...] * refract, dy_ref[...] * refract
        sea = sea_ref[...].astype(f32)

        def flow(d):
            c = f * DIRS + d
            cosine, sine = math.cos(angles[d]), math.sin(angles[d])
            center = spec_ref[pl.ds(pl.multiple_of(c * rows, 8), rows), :]
            if cosine > 0:
                beside = jnp.where(line == 0, low_ref[pl.ds(c, 1), :], pltpu.roll(center, 1, 0))
            else:
                beside = jnp.where(line == rows - 1, high_ref[pl.ds(c, 1), :], pltpu.roll(center, rows - 1, 0))
            if sine > 0:
                behind = jnp.where(lane == 0, 0.0, pltpu.roll(center, 1, 1))
            else:
                behind = jnp.where(lane == cols - 1, 0.0, pltpu.roll(center, cols - 1, 1))
            sx, sy = courant * abs(cosine), courant * abs(sine)
            shifted = center * (1.0 - sx - sy) + beside * sx + behind * sy
            return shifted, (sine * dx - cosine * dy) * shifted

        final = flow(DIRS - 1)
        here = flow(0)
        before, opening = final[1], here[1]
        for d in range(DIRS):
            if d + 1 < DIRS - 1:
                following = flow(d + 1)
            else:
                following = final if d + 1 == DIRS - 1 else (None, opening)
            value = here[0] - jnp.abs(here[1]) + jnp.maximum(before, 0.0) - jnp.minimum(following[1], 0.0)
            turned_ref[f * DIRS + d] = value * sea
            before, here = here[1], following

    some = 16 if channels % 16 == 0 else 8

    share = 8 // prows

    for tile_at in range(0, groups, share):
        t = position_of(tile_at ^ device, space, groups) // share
        tall = pl.ds(pl.multiple_of(t * 8, 8), 8)
        slots = [(device_of(t * share + i, space, groups) ^ device) - tile_at for i in range(share)]

        @pl.loop(0, channels // some)
        def _(n):
            at = pl.multiple_of(n * some, some)
            for h in range(cols // 128):
                lanes = pl.ds(h * 128, 128)
                tile = [turned_ref[at + i, tall, lanes] for i in range(some)]
                tile = encode(jnp.swapaxes(jnp.stack(tile), 0, 1))
                for slot in range(share):
                    for j in range(prows):
                        value = tile[j]
                        for i in range(1, share):
                            value = jnp.where(slots[i] == slot, tile[i * prows + j], value)
                        for m, members in enumerate(split):
                            if j in members:
                                out = outs[m * groups + tile_at + slot]
                                out[members.index(j), pl.ds(at, some), lanes] = value


class Net:
    def __init__(self, plan, groups, spaces, space, parts, scratch):
        self.x, self.hid, self.win, self.wout, self.sem = scratch
        self.groups, self.spaces = groups, spaces
        self.hidden, self.channels = self.win.shape
        self.hpart = self.hidden // (groups * spaces)
        self.cpart = self.channels // spaces
        self.pending = True
        pieces = [(kind, f, s, part.at[n]) for part, (kind, places) in zip(parts, plan) for n, (f, s) in enumerate(places)]
        for kind, f, s, piece in sorted(pieces, key=lambda item: item[:3]):
            self.copy(kind, f, space ^ s, piece).start()
        self.piece = [part.at[0] for part in (parts[0], parts[-1])]

    def copy(self, kind, f, s, piece):
        if kind == 0:
            size, unit = self.hpart, f * self.spaces + s
            target = self.win.at[pl.ds(pl.multiple_of(unit * size, 8), size), :]
        else:
            size, unit = self.cpart, s * self.groups + f
            width = self.hidden // self.groups
            target = self.wout.at[pl.ds(pl.multiple_of(s * size, 8), size), pl.ds(f * width, width)]
        return pltpu.make_async_copy(piece.at[pl.ds(0, size), :], target, self.sem.at[kind, unit])

    def run(self, inverse, emit):
        mblock, cblock = min(512, self.hidden), 4 * BLOCK
        for m in range(0, self.hidden, mblock):
            if self.pending and m == 0:
                for unit in range(self.groups * self.spaces):
                    self.copy(0, unit // self.spaces, unit % self.spaces, self.piece[0]).wait()
            pre = jnp.dot(self.win[m : m + mblock, :], self.x[...], preferred_element_type=f32) * inverse
            half = 0.5 * pre
            inside = pre * (0.7978845608028654 + (0.7978845608028654 * 0.044715) * (pre * pre))
            self.hid[m : m + mblock, :] = (half + half * jnp.tanh(inside)).astype(bf16)
        for c in range(0, self.channels, cblock):
            if self.pending and c == 0:
                for s in range(self.spaces):
                    for f in range(self.groups):
                        self.copy(1, f, s, self.piece[1]).wait()
            source = jnp.dot(self.wout[c : c + cblock, :], self.hid[...], preferred_element_type=f32)
            emit(pl.ds(c, cblock), jnp.exp(STEP_SCALE * jnp.tanh(source)))
        self.pending = False


def mean_inverse(total, channels):
    total = jnp.sum(total, axis=0, keepdims=True)
    return 1.0 / (total * (1.0 / channels) + EPSILON)


def step_one(own, codes, field_ref, device, net):
    local, cols = codes[0].shape[1:]
    for n in range(len(own)):
        total = jnp.zeros((8, cols), f32)
        for k in range(len(codes)):
            row = (k ^ device) * local
            for b in range(local // BLOCK):
                value = decode(codes[k][n, pl.ds(b * BLOCK, BLOCK), :])
                field_ref[n, pl.ds(pl.multiple_of(row + b * BLOCK, 8), BLOCK), :] = value
                total = total + jnp.sum(value.reshape(BLOCK // 8, 8, cols), axis=0)
        net.x[...] = field_ref[n].astype(bf16)

        def emit(part, factor):
            field_ref[n, part, :] = field_ref[n, part, :] * factor

        net.run(mean_inverse(total, net.channels), emit)


def step_two(own, held, outs, grid, coefw, moved_ref, first_row, device, net):
    numbers_ref, angle_ref, dx_ref, dy_ref, sea_ref = grid
    local, cols = outs[0].shape[1:]
    groups, channels = len(outs), net.channels

    @pl.loop(0, groups)
    def _(q):
        row = (q ^ device) * (local // DIRS)
        for b in range(local // BLOCK):
            at = pl.multiple_of(q * local + b * BLOCK, 8)
            spread(numbers_ref, row + 2 * b, angle_ref, coefw, at)

    for n, j in enumerate(own):
        r = first_row + j
        dx, dy = dx_ref[pl.ds(r, 1), :], dy_ref[pl.ds(r, 1), :]
        sea = sea_ref[pl.ds(r, 1), :].astype(f32)
        (here, hn), (above, an), (below, bn) = held(j), held(j - 1), held(j + 1)

        def block(b, total):
            sums = [total]

            def write(part, value):
                moved_ref[part, :] = value
                sums.append(sums[-1] + value)

            at = pl.multiple_of(b * BLOCK, 8)
            transport(
                at,
                lambda part: here[hn, part, :],
                lambda part: above[an, part, :],
                lambda part: below[bn, part, :],
                coefw,
                jnp.broadcast_to(dx, (8, cols)),
                jnp.broadcast_to(dy, (8, cols)),
                jnp.broadcast_to(sea, (8, cols)),
                write,
            )
            return sums[-1]

        total = lax.fori_loop(0, channels // BLOCK, block, jnp.zeros((8, cols), f32))
        net.x[...] = moved_ref[...].astype(bf16)

        def emit(part, factor):
            moved_ref[part, :] = moved_ref[part, :] * factor

        net.run(mean_inverse(total, channels), emit)
        for k in range(groups):
            outs[k][n] = encode(moved_ref[pl.ds(pl.multiple_of((k ^ device) * local, 8), local), :])


def take(refs, count):
    return list(refs[:count]), refs[count:]


def outer_one_kernel(split, sizes, plan, where_ref, numbers_ref, angle_ref, *refs):
    groups, spaces, _ = sizes
    codes, refs = take(refs, groups)
    parts, refs = take(refs, len(plan))
    (field_ref, *edges), refs = take(refs, 3)
    net = Net(plan, groups, spaces, where_ref[0], parts, refs)
    step_one(split[0], codes, field_ref, where_ref[1], net)
    for edge, n in zip(edges, (0, len(split[0]) - 1)):
        edge[...] = encode(field_ref[n])


def inner_kernel(split, sizes, plan, where_ref, *refs):
    groups, spaces, prows = sizes
    grid, refs = take(refs, 5)
    (outer_ref,), refs = take(refs, 1)
    codes, refs = take(refs, groups)
    parts, refs = take(refs, len(plan))
    (field_ref,), refs = take(refs, 1)
    outs, refs = take(refs, groups)
    (moved_ref, coefw), scratch = take(refs, 2)
    space, device = where_ref[0], where_ref[1]
    net = Net(plan, groups, spaces, space, parts, scratch)
    step_one(split[1], codes, field_ref, device, net)

    def held(j):
        return (outer_ref, split[0].index(j)) if j in split[0] else (field_ref, split[1].index(j))

    first_row = position_of(device, space, groups) * prows
    step_two(split[1], held, outs, grid, coefw, moved_ref, first_row, device, net)


def outer_two_kernel(split, sizes, plan, where_ref, *refs):
    groups, spaces, prows = sizes
    grid, refs = take(refs, 5)
    fields, refs = take(refs, len(split))
    halos, refs = take(refs, 2)
    parts, refs = take(refs, len(plan))
    outs, refs = take(refs, groups)
    (halo_ref, moved_ref, coefw), scratch = take(refs, 3)
    space, device = where_ref[0], where_ref[1]
    net = Net(plan, groups, spaces, space, parts, scratch)
    for n, halo in enumerate(halos):
        halo_ref[n] = decode(halo[...])

    def held(j):
        if j < 0 or j >= prows:
            return halo_ref, int(j >= prows)
        for field, members in zip(fields, split):
            if j in members:
                return field, members.index(j)

    first_row = position_of(device, space, groups) * prows
    step_two(split[0], held, outs, grid, coefw, moved_ref, first_row, device, net)


def last_kernel(split, groups, prows, where_ref, *refs):
    codes, out_ref = refs[:-1], refs[-1]
    local, cols = codes[0].shape[1:]
    rows = groups * prows
    space, device = where_ref[0], where_ref[1]
    share = 8 // prows
    some = 16 if local % 16 == 0 else 8

    for tile_at in range(0, groups, share):
        t = position_of(tile_at ^ device, space, groups) // share
        slots = [(device_of(t * share + i, space, groups) ^ device) - tile_at for i in range(share)]

        @pl.loop(0, local // some)
        def _(n):
            at = pl.multiple_of(n * some, some)
            for h in range(cols // 128):
                lanes = pl.ds(h * 128, 128)
                tile = []
                for i in range(share):
                    for j in range(prows):
                        for m, members in enumerate(split):
                            if j in members:
                                source = codes[m * groups + tile_at : m * groups + tile_at + share]
                                found = [code[members.index(j), pl.ds(at, some), lanes] for code in source]
                        value = found[0]
                        for slot in range(1, share):
                            value = jnp.where(slots[i] == slot, found[slot], value)
                        tile.append(decode(value))
                tile = jnp.swapaxes(jnp.stack(tile), 0, 1)
                for k in range(some):
                    start = pl.multiple_of((at + k) * rows + t * 8, 8)
                    out_ref[pl.ds(start, 8), lanes] = tile[k]


def exchange(array, axis, bit):
    count = lax.axis_size(axis)
    return lax.ppermute(array, axis, [(i, i ^ bit) for i in range(count)])


def gather(piece, freq_bits, space_bits):
    have, places = piece[None], [(0, 0)]
    for bit in freq_bits[:-1]:
        have = jnp.concatenate([have, exchange(have, "freq", bit)], axis=0)
        places = places + [(f ^ bit, s) for f, s in places]
    arrays = [(have, places)]
    for bit in freq_bits[-1:]:
        arrays.append((exchange(have, "freq", bit), [(f ^ bit, s) for f, s in places]))
    for n, bit in enumerate(space_bits):
        got = []
        for have, places in arrays:
            flip = [(f, s ^ bit) for f, s in places]
            got.append((exchange(have, "space", bit), flip))
        if n == 0 or n == len(space_bits) - 1:
            arrays = arrays + got
        else:
            arrays = [
                (jnp.concatenate([a, b], axis=0), p + q) for (a, p), (b, q) in zip(arrays, got)
            ]
    return arrays


def bits_of(count):
    return [1 << n for n in reversed(range(count.bit_length() - 1))]


def split3(value):
    high = lax.reduce_precision(value, 8, 7)
    rest = value - high
    middle = lax.reduce_precision(rest, 8, 7)
    return [part.astype(bf16) for part in (high, middle, rest - middle)]


def body(spectrum, land_sea, courant, refract, depth_dx, depth_dy, w_in, w_out):
    groups, spaces = lax.axis_size("freq"), lax.axis_size("space")
    space, freq = lax.axis_index("space"), lax.axis_index("freq")
    freqs, dirs, rows, cols = spectrum.shape
    local = freqs * dirs
    channels = local * groups
    prows = rows // groups
    hidden_local = w_in.shape[1]
    hidden = hidden_local * groups

    last = spectrum[:, :, rows - 1, :].reshape(local, cols)
    first = spectrum[:, :, 0, :].reshape(local, cols)
    up = [(i, i + 1) for i in range(spaces - 1)]
    low = lax.ppermute(last, "space", up)
    high = lax.ppermute(first, "space", [(b, a) for a, b in up])

    hpart, cpart = hidden_local // spaces, channels // spaces
    win_piece = lax.dynamic_slice_in_dim(w_in, space * hpart, hpart, 1).T
    numbers = jnp.stack(split3(courant) + split3(refract))
    numbers = jnp.pad(numbers, ((0, 2), (0, channels - freqs)))
    win_piece = jnp.concatenate([win_piece, numbers], axis=0)
    wout_piece = lax.dynamic_slice_in_dim(w_out, space * cpart, cpart, 1).T
    win_arrays = gather(win_piece, bits_of(groups), bits_of(spaces))
    wout_arrays = gather(wout_piece, bits_of(groups), bits_of(spaces))
    plan, parts = [], []
    for kind, arrays in ((0, win_arrays), (1, wout_arrays)):
        for have, places in arrays:
            plan.append((kind, places))
            parts.append(have)
    found = {}
    for have, places in win_arrays[:2]:
        raw = have[:, hpart : hpart + 6, 0:freqs].astype(f32)
        raw = raw.reshape(len(places), 2, 3, freqs).sum(axis=2)
        found.update({f: raw[n] for n, (f, s) in enumerate(places)})
    numbers = jnp.concatenate([found[f] for f in range(groups)], axis=1)

    angles = (np.arange(BLOCK) % DIRS + 0.5) * (2.0 * math.pi / DIRS)
    angles = np.stack([np.cos(angles), np.sin(angles)]).astype(np.float32)
    angles = jnp.asarray(np.ascontiguousarray(np.broadcast_to(angles[:, :, None], (2, BLOCK, 128))))
    place = jnp.stack([space, freq]).astype(i32)

    any_spec = pl.BlockSpec(memory_space=pl.ANY)
    vmem = pl.BlockSpec(memory_space=pltpu.VMEM)
    smem = pl.BlockSpec(memory_space=pltpu.SMEM)
    params = pltpu.CompilerParams(vmem_limit_bytes=60 * 1024 * 1024)
    net_scratch = [
        pltpu.VMEM((channels, cols), bf16),
        pltpu.VMEM((hidden, cols), bf16),
        pltpu.VMEM((hidden, channels), bf16),
        pltpu.VMEM((channels, hidden), bf16),
        pltpu.SemaphoreType.DMA((2, groups * spaces)),
    ]

    outer = sorted({0, prows - 1})
    inner = [j for j in range(prows) if j not in outer]
    split = [outer] + ([inner] if inner else [])

    def code_shapes(own):
        return [jax.ShapeDtypeStruct((len(own), local, cols), i16)] * groups

    order = sorted(range(1, groups), key=lambda k: -k)

    def transpose(parts):
        arrived = list(parts)
        for k in order:
            arrived[k] = exchange(parts[k], "freq", k)
        return arrived

    flat = spectrum.reshape(local * rows, cols)
    sent = pl.pallas_call(
        lambda *refs: first_kernel(split, groups, prows, *refs),
        in_specs=[smem, smem, any_spec] + [vmem] * 5,
        out_specs=[vmem] * (len(split) * groups),
        out_shape=[shape for own in split for shape in code_shapes(own)],
        scratch_shapes=[pltpu.VMEM((local * rows, cols), f32)]
        + [pltpu.VMEM((local, rows, cols), f32)]
        + [pltpu.SemaphoreType.DMA((freqs,))],
        compiler_params=params,
        name="kfirst",
    )(place, jnp.stack([courant, refract]), flat, low, high, depth_dx, depth_dy, land_sea)
    arrived = [transpose(sent[n * groups : (n + 1) * groups]) for n in range(len(split))]

    sizes = (groups, spaces, prows)
    step_scratch = [pltpu.VMEM((channels, cols), f32), pltpu.VMEM((NCOEF, channels, 128), f32)]

    def field_shape(own):
        return jax.ShapeDtypeStruct((len(own), channels, cols), f32)

    edge_shape = jax.ShapeDtypeStruct((channels, cols), i16)
    field, *edge = pl.pallas_call(
        lambda *refs: outer_one_kernel(split, sizes, plan, *refs),
        in_specs=[smem, smem, any_spec] + [vmem] * groups + [any_spec] * len(plan),
        out_specs=[vmem] * 3,
        out_shape=[field_shape(outer), edge_shape, edge_shape],
        scratch_shapes=net_scratch,
        compiler_params=params,
        name="kone0",
    )(place, numbers, angles, *arrived[0], *parts)
    fields = [field]

    chain = []
    for n in range(spaces * groups):
        s, p = divmod(n, groups)
        chain.append(s * groups + device_of(p, s, groups))
    chain = list(zip(chain[:-1], chain[1:]))
    low = lax.ppermute(edge[1], ("space", "freq"), chain)
    high = lax.ppermute(edge[0], ("space", "freq"), [(b, a) for a, b in chain])

    grid = (numbers, angles, depth_dx, depth_dy, land_sea)
    back = []
    if inner:
        field, *sent = pl.pallas_call(
            lambda *refs: inner_kernel(split, sizes, plan, *refs),
            in_specs=[smem, smem] + [vmem] * (5 + groups) + [any_spec] * len(plan),
            out_specs=[vmem] * (1 + groups),
            out_shape=[field_shape(inner)] + code_shapes(inner),
            scratch_shapes=step_scratch + net_scratch,
            compiler_params=params,
            name="kmid",
        )(place, *grid, fields[0], *arrived[1], *parts)
        fields.append(field)
        back = transpose(sent)
    sent = pl.pallas_call(
        lambda *refs: outer_two_kernel(split, sizes, plan, *refs),
        in_specs=[smem, smem] + [vmem] * (4 + len(split) + 2) + [any_spec] * len(plan),
        out_specs=[vmem] * groups,
        out_shape=code_shapes(outer),
        scratch_shapes=[pltpu.VMEM((2, channels, cols), f32)] + step_scratch + net_scratch,
        compiler_params=params,
        name="ktwo0",
    )(place, *grid, *fields, low, high, *parts)
    back = transpose(sent) + back

    out = pl.pallas_call(
        lambda *refs: last_kernel(split, groups, prows, *refs),
        in_specs=[smem] + [vmem] * (len(split) * groups),
        out_specs=vmem,
        out_shape=jax.ShapeDtypeStruct((local * rows, cols), f32),
        compiler_params=params,
        name="klast",
    )(place, *back)
    return out.reshape(freqs, dirs, rows, cols)


def solution(mesh):
    placed = (
        P("freq", None, "space", None),
        P("space", None),
        P("freq"),
        P("freq"),
        P("space", None),
        P("space", None),
        P(None, "freq"),
        P("freq", None),
    )

    return jax.shard_map(
        body, mesh=mesh, in_specs=placed, out_specs=P("freq", None, "space", None), check_vma=False
    )
```

```python
import math

import jax
import jax.numpy as jnp
import numpy as np
from jax import lax
from jax.experimental import pallas as pl
from jax.experimental.pallas import tpu as pltpu
from jax.sharding import PartitionSpec as P


DIRS = 36
STEP_SCALE = 0.5
EPSILON = 1e-06
ROOT_MAX = 2.9
ENCODE = 32767.0 / ROOT_MAX
DECODE = ROOT_MAX / 32767.0
NCOEF = 5
BLOCK = 2 * DIRS
f32, bf16, i16, i32 = jnp.float32, jnp.bfloat16, jnp.int16, jnp.int32


def encode(value):
    return (jnp.sqrt(value) * ENCODE + 0.5).astype(i32).astype(i16)


def decode(code):
    root = code.astype(i32).astype(f32) * DECODE
    return root * root


def device_of(position, space, groups):
    flipped = position + (space & 1) * (groups - 1 - 2 * position)
    return flipped ^ ((flipped >> 1) & 1) if groups % 4 == 0 else flipped


def position_of(device, space, groups):
    flipped = device ^ ((device >> 1) & 1) if groups % 4 == 0 else device
    return flipped + (space & 1) * (groups - 1 - 2 * flipped)


def spread(numbers_ref, row, angle_ref, wide_ref, at):
    cosine, sine = angle_ref[0], angle_ref[1]
    second = lax.broadcasted_iota(i32, (BLOCK, 128), 0) >= DIRS
    courant = jnp.where(second, numbers_ref[0, row + 1], numbers_ref[0, row])
    refract = jnp.where(second, numbers_ref[1, row + 1], numbers_ref[1, row])
    sx, sy = courant * cosine, courant * sine
    sx, sy = jnp.abs(sx), jnp.abs(sy)
    values = [1.0 - sx - sy, sx, sy, refract * sine, refract * cosine]
    for k, value in enumerate(values):
        wide_ref[k, pl.ds(at, BLOCK), :] = value


def one_sided(positive, row, yes, no):
    if all(positive):
        return yes()
    if not any(positive):
        return no()
    change = next(n for n in range(8) if positive[n] != positive[0])
    first, second = (yes(), no()) if positive[0] else (no(), yes())
    return jnp.where(row < change, first, second)


def transport(at, here, above, below, coefw, dx, dy, sea, write):
    cols = dx.shape[1]
    row = lax.broadcasted_iota(i32, (8, cols), 0)
    lane = lax.broadcasted_iota(i32, (8, cols), 1)
    count = BLOCK // 8
    cosine = [math.cos((d + 0.5) * (2.0 * math.pi / DIRS)) > 0 for d in range(DIRS)] * 2
    sine = [math.sin((d + 0.5) * (2.0 * math.pi / DIRS)) > 0 for d in range(DIRS)] * 2
    part = [pl.ds(pl.multiple_of(at + g * 8, 8), 8) for g in range(count)]
    shifted, forward, backward = [], [], []
    for g in range(count):
        center = here(part[g])
        rows = slice(g * 8, g * 8 + 8)
        beside = one_sided(cosine[rows], row, lambda: above(part[g]), lambda: below(part[g]))
        behind = one_sided(
            sine[rows],
            row,
            lambda: jnp.where(lane == 0, 0.0, pltpu.roll(center, 1, 1)),
            lambda: jnp.where(lane == cols - 1, 0.0, pltpu.roll(center, cols - 1, 1)),
        )
        keep, sx, sy, turn_x, turn_y = (
            jnp.concatenate([coefw[k, part[g], :]] * (cols // 128), axis=1) for k in range(NCOEF)
        )
        value = center * keep + beside * sx + behind * sy
        turning = (turn_x * dx - turn_y * dy) * value
        forward.append(jnp.maximum(turning, 0.0))
        backward.append(forward[g] - turning)
        shifted.append(value - jnp.abs(turning))
    down = [pltpu.roll(value, 1, 0) for value in forward]
    up = [pltpu.roll(value, 7, 0) for value in backward]
    half = DIRS // 8
    for g in range(count):
        before = pltpu.roll(forward[half], 5, 0) if g == 0 else down[g - 1]
        after = pltpu.roll(backward[half], 3, 0) if g == count - 1 else up[g + 1]
        moved = jnp.where(row == 0, before, down[g])
        other = jnp.where(row == 7, after, up[g])
        if g == half:
            moved = jnp.where(row == DIRS % 8, pltpu.roll(forward[count - 1], 5, 0), moved)
            other = jnp.where(row == DIRS % 8 - 1, pltpu.roll(backward[0], 3, 0), other)
        write(part[g], (shifted[g] + moved + other) * sea)


def first_kernel(split, groups, prows, where_ref, numbers_ref, source_ref, low_ref, high_ref, dx_ref, dy_ref, sea_ref, *refs):
    outs, (spec_ref, turned_ref, sem) = refs[: len(split) * groups], refs[len(split) * groups :]
    channels, cols = low_ref.shape
    rows = groups * prows
    space, device = where_ref[0], where_ref[1]
    line = lax.broadcasted_iota(i32, (rows, cols), 0)
    lane = lax.broadcasted_iota(i32, (rows, cols), 1)
    angles = [(d + 0.5) * (2.0 * math.pi / DIRS) for d in range(DIRS)]

    def copy(f):
        part = pl.ds(pl.multiple_of(f * (DIRS * rows), 8), DIRS * rows)
        return pltpu.make_async_copy(source_ref.at[part, :], spec_ref.at[part, :], sem.at[f])

    for f in range(channels // DIRS):
        copy(f).start()

    @pl.loop(0, channels // DIRS)
    def _(f):
        copy(f).wait()
        courant, refract = numbers_ref[0, f], numbers_ref[1, f]
        dx, dy = dx_ref[...] * refract, dy_ref[...] * refract
        sea = sea_ref[...].astype(f32)

        def flow(d):
            c = f * DIRS + d
            cosine, sine = math.cos(angles[d]), math.sin(angles[d])
            center = spec_ref[pl.ds(pl.multiple_of(c * rows, 8), rows), :]
            if cosine > 0:
                beside = jnp.where(line == 0, low_ref[pl.ds(c, 1), :], pltpu.roll(center, 1, 0))
            else:
                beside = jnp.where(line == rows - 1, high_ref[pl.ds(c, 1), :], pltpu.roll(center, rows - 1, 0))
            if sine > 0:
                behind = jnp.where(lane == 0, 0.0, pltpu.roll(center, 1, 1))
            else:
                behind = jnp.where(lane == cols - 1, 0.0, pltpu.roll(center, cols - 1, 1))
            sx, sy = courant * abs(cosine), courant * abs(sine)
            shifted = center * (1.0 - sx - sy) + beside * sx + behind * sy
            return shifted, (sine * dx - cosine * dy) * shifted

        final = flow(DIRS - 1)
        here = flow(0)
        before, opening = final[1], here[1]
        for d in range(DIRS):
            if d + 1 < DIRS - 1:
                following = flow(d + 1)
            else:
                following = final if d + 1 == DIRS - 1 else (None, opening)
            value = here[0] - jnp.abs(here[1]) + jnp.maximum(before, 0.0) - jnp.minimum(following[1], 0.0)
            turned_ref[f * DIRS + d] = value * sea
            before, here = here[1], following

    some = 16 if channels % 16 == 0 else 8

    share = 8 // prows

    for tile_at in range(0, groups, share):
        t = position_of(tile_at ^ device, space, groups) // share
        tall = pl.ds(pl.multiple_of(t * 8, 8), 8)
        slots = [(device_of(t * share + i, space, groups) ^ device) - tile_at for i in range(share)]

        @pl.loop(0, channels // some)
        def _(n):
            at = pl.multiple_of(n * some, some)
            for h in range(cols // 128):
                lanes = pl.ds(h * 128, 128)
                tile = [turned_ref[at + i, tall, lanes] for i in range(some)]
                tile = encode(jnp.swapaxes(jnp.stack(tile), 0, 1))
                for slot in range(share):
                    for j in range(prows):
                        value = tile[j]
                        for i in range(1, share):
                            value = jnp.where(slots[i] == slot, tile[i * prows + j], value)
                        for m, members in enumerate(split):
                            if j in members:
                                out = outs[m * groups + tile_at + slot]
                                out[members.index(j), pl.ds(at, some), lanes] = value


class Net:
    def __init__(self, plan, groups, spaces, space, parts, scratch):
        self.x, self.hid, self.win, self.wout, self.sem = scratch
        self.groups, self.spaces = groups, spaces
        self.hidden, self.channels = self.win.shape
        self.hpart = self.hidden // (groups * spaces)
        self.cpart = self.channels // spaces
        self.pending = True
        pieces = [(kind, f, s, part.at[n]) for part, (kind, places) in zip(parts, plan) for n, (f, s) in enumerate(places)]
        for kind, f, s, piece in sorted(pieces, key=lambda item: item[:3]):
            self.copy(kind, f, space ^ s, piece).start()
        self.piece = [part.at[0] for part in (parts[0], parts[-1])]

    def copy(self, kind, f, s, piece):
        if kind == 0:
            size, unit = self.hpart, f * self.spaces + s
            target = self.win.at[pl.ds(pl.multiple_of(unit * size, 8), size), :]
        else:
            size, unit = self.cpart, s * self.groups + f
            width = self.hidden // self.groups
            target = self.wout.at[pl.ds(pl.multiple_of(s * size, 8), size), pl.ds(f * width, width)]
        return pltpu.make_async_copy(piece.at[pl.ds(0, size), :], target, self.sem.at[kind, unit])

    def run(self, inverse, emit):
        mblock, cblock = min(512, self.hidden), 4 * BLOCK
        for m in range(0, self.hidden, mblock):
            if self.pending and m == 0:
                for unit in range(self.groups * self.spaces):
                    self.copy(0, unit // self.spaces, unit % self.spaces, self.piece[0]).wait()
            pre = jnp.dot(self.win[m : m + mblock, :], self.x[...], preferred_element_type=f32) * inverse
            half = 0.5 * pre
            inside = pre * (0.7978845608028654 + (0.7978845608028654 * 0.044715) * (pre * pre))
            self.hid[m : m + mblock, :] = (half + half * jnp.tanh(inside)).astype(bf16)
        for c in range(0, self.channels, cblock):
            if self.pending and c == 0:
                for s in range(self.spaces):
                    for f in range(self.groups):
                        self.copy(1, f, s, self.piece[1]).wait()
            source = jnp.dot(self.wout[c : c + cblock, :], self.hid[...], preferred_element_type=f32)
            emit(pl.ds(c, cblock), jnp.exp(STEP_SCALE * jnp.tanh(source)))
        self.pending = False


def mean_inverse(total, channels):
    total = jnp.sum(total, axis=0, keepdims=True)
    return 1.0 / (total * (1.0 / channels) + EPSILON)


def step_one(own, codes, field_ref, device, net):
    local, cols = codes[0].shape[1:]
    for n in range(len(own)):
        total = jnp.zeros((8, cols), f32)
        for k in range(len(codes)):
            row = (k ^ device) * local
            for b in range(local // BLOCK):
                value = decode(codes[k][n, pl.ds(b * BLOCK, BLOCK), :])
                field_ref[n, pl.ds(pl.multiple_of(row + b * BLOCK, 8), BLOCK), :] = value
                total = total + jnp.sum(value.reshape(BLOCK // 8, 8, cols), axis=0)
        net.x[...] = field_ref[n].astype(bf16)

        def emit(part, factor):
            field_ref[n, part, :] = field_ref[n, part, :] * factor

        net.run(mean_inverse(total, net.channels), emit)


def step_two(own, held, outs, grid, coefw, moved_ref, first_row, device, net):
    numbers_ref, angle_ref, dx_ref, dy_ref, sea_ref = grid
    local, cols = outs[0].shape[1:]
    groups, channels = len(outs), net.channels

    @pl.loop(0, groups)
    def _(q):
        row = (q ^ device) * (local // DIRS)
        for b in range(local // BLOCK):
            at = pl.multiple_of(q * local + b * BLOCK, 8)
            spread(numbers_ref, row + 2 * b, angle_ref, coefw, at)

    for n, j in enumerate(own):
        r = first_row + j
        dx, dy = dx_ref[pl.ds(r, 1), :], dy_ref[pl.ds(r, 1), :]
        sea = sea_ref[pl.ds(r, 1), :].astype(f32)
        (here, hn), (above, an), (below, bn) = held(j), held(j - 1), held(j + 1)

        def block(b, total):
            sums = [total]

            def write(part, value):
                moved_ref[part, :] = value
                sums.append(sums[-1] + value)

            at = pl.multiple_of(b * BLOCK, 8)
            transport(
                at,
                lambda part: here[hn, part, :],
                lambda part: above[an, part, :],
                lambda part: below[bn, part, :],
                coefw,
                jnp.broadcast_to(dx, (8, cols)),
                jnp.broadcast_to(dy, (8, cols)),
                jnp.broadcast_to(sea, (8, cols)),
                write,
            )
            return sums[-1]

        total = lax.fori_loop(0, channels // BLOCK, block, jnp.zeros((8, cols), f32))
        net.x[...] = moved_ref[...].astype(bf16)

        def emit(part, factor):
            moved_ref[part, :] = moved_ref[part, :] * factor

        net.run(mean_inverse(total, channels), emit)
        for k in range(groups):
            outs[k][n] = encode(moved_ref[pl.ds(pl.multiple_of((k ^ device) * local, 8), local), :])


def take(refs, count):
    return list(refs[:count]), refs[count:]


def outer_one_kernel(split, sizes, plan, where_ref, numbers_ref, angle_ref, *refs):
    groups, spaces, _ = sizes
    codes, refs = take(refs, groups)
    parts, refs = take(refs, len(plan))
    (field_ref, *edges), refs = take(refs, 3)
    net = Net(plan, groups, spaces, where_ref[0], parts, refs)
    step_one(split[0], codes, field_ref, where_ref[1], net)
    for edge, n in zip(edges, (0, len(split[0]) - 1)):
        edge[...] = encode(field_ref[n])


def inner_kernel(split, sizes, plan, where_ref, *refs):
    groups, spaces, prows = sizes
    grid, refs = take(refs, 5)
    (outer_ref,), refs = take(refs, 1)
    codes, refs = take(refs, groups)
    parts, refs = take(refs, len(plan))
    (field_ref,), refs = take(refs, 1)
    outs, refs = take(refs, groups)
    (moved_ref, coefw), scratch = take(refs, 2)
    space, device = where_ref[0], where_ref[1]
    net = Net(plan, groups, spaces, space, parts, scratch)
    step_one(split[1], codes, field_ref, device, net)

    def held(j):
        return (outer_ref, split[0].index(j)) if j in split[0] else (field_ref, split[1].index(j))

    first_row = position_of(device, space, groups) * prows
    step_two(split[1], held, outs, grid, coefw, moved_ref, first_row, device, net)


def outer_two_kernel(split, sizes, plan, where_ref, *refs):
    groups, spaces, prows = sizes
    grid, refs = take(refs, 5)
    fields, refs = take(refs, len(split))
    halos, refs = take(refs, 2)
    parts, refs = take(refs, len(plan))
    outs, refs = take(refs, groups)
    (halo_ref, moved_ref, coefw), scratch = take(refs, 3)
    space, device = where_ref[0], where_ref[1]
    net = Net(plan, groups, spaces, space, parts, scratch)
    for n, halo in enumerate(halos):
        halo_ref[n] = decode(halo[...])

    def held(j):
        if j < 0 or j >= prows:
            return halo_ref, int(j >= prows)
        for field, members in zip(fields, split):
            if j in members:
                return field, members.index(j)

    first_row = position_of(device, space, groups) * prows
    step_two(split[0], held, outs, grid, coefw, moved_ref, first_row, device, net)


def last_kernel(split, groups, prows, where_ref, *refs):
    codes, (out_ref, stage, sem) = refs[:-3], refs[-3:]
    local, cols = codes[0].shape[1:]
    space, device = where_ref[0], where_ref[1]
    share = 8 // prows
    some = 16 if local % 16 == 0 else 8
    copies = []

    for tile_at in range(0, groups, share):
        t = position_of(tile_at ^ device, space, groups) // share
        slots = [(device_of(t * share + i, space, groups) ^ device) - tile_at for i in range(share)]

        @pl.loop(0, local // some)
        def _(n):
            at = pl.multiple_of(n * some, some)
            for h in range(cols // 128):
                lanes = pl.ds(h * 128, 128)
                tile = []
                for i in range(share):
                    for j in range(prows):
                        for m, members in enumerate(split):
                            if j in members:
                                source = codes[m * groups + tile_at : m * groups + tile_at + share]
                                found = [code[members.index(j), pl.ds(at, some), lanes] for code in source]
                        value = found[0]
                        for slot in range(1, share):
                            value = jnp.where(slots[i] == slot, found[slot], value)
                        tile.append(decode(value))
                tile = jnp.swapaxes(jnp.stack(tile), 0, 1)
                for k in range(some):
                    stage[at + k, pl.ds(pl.multiple_of(t * 8, 8), 8), lanes] = tile[k]

        rows_of = pl.ds(pl.multiple_of(t * 8, 8), 8)
        copies.append(pltpu.make_async_copy(stage.at[:, rows_of, :], out_ref.at[:, rows_of, :], sem.at[len(copies)]))
        copies[-1].start()

    for copy in copies:
        copy.wait()


def exchange(array, axis, bit):
    count = lax.axis_size(axis)
    return lax.ppermute(array, axis, [(i, i ^ bit) for i in range(count)])


def gather(piece, freq_bits, space_bits):
    have, places = piece[None], [(0, 0)]
    for bit in freq_bits[:-1]:
        have = jnp.concatenate([have, exchange(have, "freq", bit)], axis=0)
        places = places + [(f ^ bit, s) for f, s in places]
    arrays = [(have, places)]
    for bit in freq_bits[-1:]:
        arrays.append((exchange(have, "freq", bit), [(f ^ bit, s) for f, s in places]))
    for n, bit in enumerate(space_bits):
        got = []
        for have, places in arrays:
            flip = [(f, s ^ bit) for f, s in places]
            got.append((exchange(have, "space", bit), flip))
        if n == 0 or n == len(space_bits) - 1:
            arrays = arrays + got
        else:
            arrays = [
                (jnp.concatenate([a, b], axis=0), p + q) for (a, p), (b, q) in zip(arrays, got)
            ]
    return arrays


def bits_of(count):
    return [1 << n for n in reversed(range(count.bit_length() - 1))]


def split3(value):
    high = lax.reduce_precision(value, 8, 7)
    rest = value - high
    middle = lax.reduce_precision(rest, 8, 7)
    return [part.astype(bf16) for part in (high, middle, rest - middle)]


def body(spectrum, land_sea, courant, refract, depth_dx, depth_dy, w_in, w_out):
    groups, spaces = lax.axis_size("freq"), lax.axis_size("space")
    space, freq = lax.axis_index("space"), lax.axis_index("freq")
    freqs, dirs, rows, cols = spectrum.shape
    local = freqs * dirs
    channels = local * groups
    prows = rows // groups
    hidden_local = w_in.shape[1]
    hidden = hidden_local * groups

    last = spectrum[:, :, rows - 1, :].reshape(local, cols)
    first = spectrum[:, :, 0, :].reshape(local, cols)
    up = [(i, i + 1) for i in range(spaces - 1)]
    low = lax.ppermute(last, "space", up)
    high = lax.ppermute(first, "space", [(b, a) for a, b in up])

    hpart, cpart = hidden_local // spaces, channels // spaces
    win_piece = lax.dynamic_slice_in_dim(w_in, space * hpart, hpart, 1).T
    numbers = jnp.stack(split3(courant) + split3(refract))
    numbers = jnp.pad(numbers, ((0, 2), (0, channels - freqs)))
    win_piece = jnp.concatenate([win_piece, numbers], axis=0)
    wout_piece = lax.dynamic_slice_in_dim(w_out, space * cpart, cpart, 1).T
    win_arrays = gather(win_piece, bits_of(groups), bits_of(spaces))
    wout_arrays = gather(wout_piece, bits_of(groups), bits_of(spaces))
    plan, parts = [], []
    for kind, arrays in ((0, win_arrays), (1, wout_arrays)):
        for have, places in arrays:
            plan.append((kind, places))
            parts.append(have)
    found = {}
    for have, places in win_arrays[:2]:
        raw = have[:, hpart : hpart + 6, 0:freqs].astype(f32)
        raw = raw.reshape(len(places), 2, 3, freqs).sum(axis=2)
        found.update({f: raw[n] for n, (f, s) in enumerate(places)})
    numbers = jnp.concatenate([found[f] for f in range(groups)], axis=1)

    angles = (np.arange(BLOCK) % DIRS + 0.5) * (2.0 * math.pi / DIRS)
    angles = np.stack([np.cos(angles), np.sin(angles)]).astype(np.float32)
    angles = jnp.asarray(np.ascontiguousarray(np.broadcast_to(angles[:, :, None], (2, BLOCK, 128))))
    place = jnp.stack([space, freq]).astype(i32)

    any_spec = pl.BlockSpec(memory_space=pl.ANY)
    vmem = pl.BlockSpec(memory_space=pltpu.VMEM)
    smem = pl.BlockSpec(memory_space=pltpu.SMEM)
    params = pltpu.CompilerParams(vmem_limit_bytes=60 * 1024 * 1024)
    net_scratch = [
        pltpu.VMEM((channels, cols), bf16),
        pltpu.VMEM((hidden, cols), bf16),
        pltpu.VMEM((hidden, channels), bf16),
        pltpu.VMEM((channels, hidden), bf16),
        pltpu.SemaphoreType.DMA((2, groups * spaces)),
    ]

    outer = sorted({0, prows - 1})
    inner = [j for j in range(prows) if j not in outer]
    split = [outer] + ([inner] if inner else [])

    def code_shapes(own):
        return [jax.ShapeDtypeStruct((len(own), local, cols), i16)] * groups

    order = sorted(range(1, groups), key=lambda k: -k)

    def transpose(parts):
        arrived = list(parts)
        for k in order:
            arrived[k] = exchange(parts[k], "freq", k)
        return arrived

    flat = spectrum.reshape(local * rows, cols)
    sent = pl.pallas_call(
        lambda *refs: first_kernel(split, groups, prows, *refs),
        in_specs=[smem, smem, any_spec] + [vmem] * 5,
        out_specs=[vmem] * (len(split) * groups),
        out_shape=[shape for own in split for shape in code_shapes(own)],
        scratch_shapes=[pltpu.VMEM((local * rows, cols), f32)]
        + [pltpu.VMEM((local, rows, cols), f32)]
        + [pltpu.SemaphoreType.DMA((freqs,))],
        compiler_params=params,
        name="kfirst",
    )(place, jnp.stack([courant, refract]), flat, low, high, depth_dx, depth_dy, land_sea)
    arrived = [transpose(sent[n * groups : (n + 1) * groups]) for n in range(len(split))]

    sizes = (groups, spaces, prows)
    step_scratch = [pltpu.VMEM((channels, cols), f32), pltpu.VMEM((NCOEF, channels, 128), f32)]

    def field_shape(own):
        return jax.ShapeDtypeStruct((len(own), channels, cols), f32)

    edge_shape = jax.ShapeDtypeStruct((channels, cols), i16)
    field, *edge = pl.pallas_call(
        lambda *refs: outer_one_kernel(split, sizes, plan, *refs),
        in_specs=[smem, smem, any_spec] + [vmem] * groups + [any_spec] * len(plan),
        out_specs=[vmem] * 3,
        out_shape=[field_shape(outer), edge_shape, edge_shape],
        scratch_shapes=net_scratch,
        compiler_params=params,
        name="kone0",
    )(place, numbers, angles, *arrived[0], *parts)
    fields = [field]

    chain = []
    for n in range(spaces * groups):
        s, p = divmod(n, groups)
        chain.append(s * groups + device_of(p, s, groups))
    chain = list(zip(chain[:-1], chain[1:]))
    low = lax.ppermute(edge[1], ("space", "freq"), chain)
    high = lax.ppermute(edge[0], ("space", "freq"), [(b, a) for a, b in chain])

    grid = (numbers, angles, depth_dx, depth_dy, land_sea)
    back = []
    if inner:
        field, *sent = pl.pallas_call(
            lambda *refs: inner_kernel(split, sizes, plan, *refs),
            in_specs=[smem, smem] + [vmem] * (5 + groups) + [any_spec] * len(plan),
            out_specs=[vmem] * (1 + groups),
            out_shape=[field_shape(inner)] + code_shapes(inner),
            scratch_shapes=step_scratch + net_scratch,
            compiler_params=params,
            name="kmid",
        )(place, *grid, fields[0], *arrived[1], *parts)
        fields.append(field)
        back = transpose(sent)
    sent = pl.pallas_call(
        lambda *refs: outer_two_kernel(split, sizes, plan, *refs),
        in_specs=[smem, smem] + [vmem] * (4 + len(split) + 2) + [any_spec] * len(plan),
        out_specs=[vmem] * groups,
        out_shape=code_shapes(outer),
        scratch_shapes=[pltpu.VMEM((2, channels, cols), f32)] + step_scratch + net_scratch,
        compiler_params=params,
        name="ktwo0",
    )(place, *grid, *fields, low, high, *parts)
    back = transpose(sent) + back

    out = pl.pallas_call(
        lambda *refs: last_kernel(split, groups, prows, *refs),
        in_specs=[smem] + [vmem] * (len(split) * groups),
        out_specs=any_spec,
        out_shape=jax.ShapeDtypeStruct((local, rows, cols), f32),
        scratch_shapes=[pltpu.VMEM((local, rows, cols), f32), pltpu.SemaphoreType.DMA((groups,))],
        compiler_params=params,
        name="klast",
    )(place, *back)
    return out.reshape(freqs, dirs, rows, cols)


def solution(mesh):
    placed = (
        P("freq", None, "space", None),
        P("space", None),
        P("freq"),
        P("freq"),
        P("space", None),
        P("space", None),
        P(None, "freq"),
        P("freq", None),
    )

    return jax.shard_map(
        body, mesh=mesh, in_specs=placed, out_specs=P("freq", None, "space", None), check_vma=False
    )
```
